32 devices in a mesh: rep: 8 (over z, x), shard: 4 (over y, core).
Axes of the slice: x: 2, y: 2, z: 4, core: 2. Of those that a mesh axis runs over, the one named last changes fastest.
Arguments:
- tokens: bfloat16 [16384, 1024], P(('rep', 'shard')), may hold values from -6 to 6
- positions: int32 [16384], P(('rep', 'shard')), may hold values from 0 to 511, as said below
- lengths: int32 [64], replicated, may hold values from 0 to 512, as said below
- owner: int32 [64], replicated, may hold values from 0 to 31, as said below
- qkv_weight: bfloat16 [1024, 3072], P('shard'), may hold values from -0.1875 to 0.1875
- out_weight: bfloat16 [1024, 1024], P('shard'), may hold values from -1.5 to 1.5
- in_weight: bfloat16 [1024, 4096], P('shard'), may hold values from -0.1875 to 0.1875
- in_bias: bfloat16 [4096], P('shard'), may hold values from -3 to 3
- fc_weight: bfloat16 [4096, 1024], P('shard'), may hold values from -0.09375 to 0.09375
- fc_bias: bfloat16 [1024], P('shard'), may hold values from -3 to 3
- norm_gain: bfloat16 [1024], P('shard'), may hold values from 0.25 to 1.75
- norm_bias: bfloat16 [1024], P('shard'), may hold values from -2 to 2
- cotangent: bfloat16 [16384, 1024], P(('rep', 'shard')), may hold values from -6 to 6
Outputs:
- layer_out: bfloat16 [16384, 1024], P(('rep', 'shard'))
- input_grad: bfloat16 [16384, 1024], P(('rep', 'shard'))
- grad_qkv: float32 [1024, 3072], P('shard')
- grad_out: float32 [1024, 1024], P('shard')
- grad_in: float32 [1024, 4096], P('shard')
- grad_in_bias: float32 [4096], P('shard')
- grad_fc: float32 [4096, 1024], P('shard')
- grad_fc_bias: float32 [1024], P('shard')
- grad_gain: float32 [1024], P('shard')
- grad_norm_bias: float32 [1024], P('shard')
The draws below stay inside these ranges and needn't reach their ends.
Inputs may be any that keep to these rules, and one draw needn't show every extreme that they name: Sequences 2 i and 2 i + 1 go to one device; their lengths sum to at most 512; some sequence has exactly 512 tokens; a length may be 0. Sequences 2 i and 2 i + 1 have the same owner, and every device owns exactly one such pair. `positions`: a token's position within its sequence, with the sequences packed as the steps say; unused slots hold 0.
All inputs are finite; a program needn't handle non-finite values.
Results may differ from the reference program's by a relative error of at most 0.011.
Values may be sent and summed in bfloat16 or wider, within the bound.
A program may use at most 256 MiB of HBM per device.

```python
import math
import jax
import jax.numpy as jnp
from jax import lax

D = 1024
HEADS = 16
HEAD_DIM = 64
ROT_DIM = 32
FF = 4096
TOK_DEV = 512
TOKENS = 16384
N_REP = 8
N_SHARD = 4


def arrangement(key):
    base_key = jax.random.fold_in(key, 41)
    key_shift, key_trim, key_second, key_full, key_order = jax.random.split(base_key, 5)
    device_count = N_REP * N_SHARD
    shifts = jax.random.randint(key_shift, (device_count,), 0, 3).astype(jnp.int32)
    ceiling = jnp.right_shift(jnp.full((device_count,), TOK_DEV, jnp.int32), shifts)
    first_len = ceiling - jax.random.randint(key_trim, (device_count,), 0, ceiling // 4 + 1).astype(jnp.int32)
    chosen = jax.random.randint(key_full, (), 0, device_count)
    number = jnp.arange(device_count, dtype=jnp.int32)
    first_len = jnp.where(number == chosen, TOK_DEV, first_len).astype(jnp.int32)
    second = jax.random.randint(key_second, (device_count,), 0, (TOK_DEV - first_len) // 2 + 1).astype(jnp.int32)
    device_order = jax.random.permutation(key_order, device_count).astype(jnp.int32)
    return (first_len, second, device_order)


def draw_lengths(key, part):
    first_len, second, device_order = arrangement(key)
    return jnp.stack([first_len, second], 1).reshape(-1).astype(jnp.int32)


def draw_owner(key, part):
    first_len, second, device_order = arrangement(key)
    return jnp.repeat(device_order, 2).astype(jnp.int32)


def draw_positions(key, part):
    first_len, second, device_order = arrangement(key)
    device_count = N_REP * N_SHARD
    number = jnp.arange(device_count, dtype=jnp.int32)
    holder = jnp.zeros((device_count,), jnp.int32).at[device_order].set(number)
    first_dev = first_len[holder][:, None]
    second_dev = second[holder][:, None]
    slot_index = jnp.arange(TOK_DEV, dtype=jnp.int32)[None, :]
    placed = jnp.where(slot_index < first_dev, slot_index, jnp.where(slot_index < first_dev + second_dev, slot_index - first_dev, 0))
    return placed.reshape(-1).astype(jnp.int32)


def block_scale(stream_key, shape, cuts, least, high):
    level = 1.0
    for position, shards_of in cuts:
        draws = jax.random.uniform(jax.random.fold_in(jax.random.fold_in(stream_key, 6), position), (shards_of,), jnp.float32, least / len(cuts), high / len(cuts))
        level = level * jnp.repeat(jnp.exp(draws), shape[position] // shards_of).reshape((-1,) + (1,) * (len(shape) - 1 - position))
    return level


def bell_draw(stream_key, extent, scale, limit, shards=(), held_as=jnp.bfloat16):
    drawn = scale * jax.random.normal(stream_key, extent, jnp.float32)
    if shards:
        drawn = drawn * block_scale(stream_key, extent, shards, -0.22, 0.18)
    return jnp.clip(drawn, -limit, limit).astype(held_as)


def setup_inputs(seed: int = 0) -> dict:
    key_of = jax.random.split(jax.random.key(seed), 14)
    return {
        "tokens": bell_draw(key_of[0], (TOKENS, D), 1.0, 6.0, ((0, 32),)),
        "positions": draw_positions(jax.random.fold_in(key_of[13], 71), 0),
        "lengths": draw_lengths(jax.random.fold_in(key_of[13], 71), 0),
        "owner": draw_owner(jax.random.fold_in(key_of[13], 71), 0),
        "qkv_weight": bell_draw(key_of[4], (D, 3 * D), D ** -0.5, 0.1875, ((0, 4),)),
        "out_weight": bell_draw(key_of[5], (D, D), (D // 64) ** -0.5, 1.5, ((0, 4),)),
        "in_weight": bell_draw(key_of[6], (D, FF), D ** -0.5, 0.1875, ((0, 4),)),
        "in_bias": bell_draw(key_of[7], (FF,), 0.5, 3.0, ((0, 4),)),
        "fc_weight": bell_draw(key_of[8], (FF, D), FF ** -0.5, 0.09375, ((0, 4),)),
        "fc_bias": bell_draw(key_of[9], (D,), 0.5, 3.0, ((0, 4),)),
        "norm_gain": jnp.clip(1.0 + 0.15 * jax.random.normal(key_of[10], (D,), jnp.float32), 0.25, 1.75).astype(jnp.bfloat16),
        "norm_bias": bell_draw(key_of[11], (D,), 0.3, 2.0, ((0, 4),)),
        "cotangent": bell_draw(key_of[12], (TOKENS, D), 1.0, 6.0, ((0, 32),)),
    }


EPS = 1e-05
NEG = -1000000000.0
SCORE_SCALE = 0.125
PRECISION = lax.Precision.HIGHEST

@jax.custom_vjp
def low(v):
    return lax.optimization_barrier(v.astype(jnp.bfloat16)).astype(jnp.float32)

@jax.custom_vjp
def low_back(v):
    return v

def low_keep(v):
    return (low(v), None)

def low_pass(kept, grad):
    return (grad,)

def back_keep(v):
    return (v, None)

def back_low(kept, grad):
    return (low(grad),)
low.defvjp(low_keep, low_pass)
low_back.defvjp(back_keep, back_low)

def layout(lengths, owner, device):
    owned_mask = (owner == device).astype(jnp.int32)
    seq_ends = jnp.cumsum(lengths * owned_mask).astype(jnp.int32)
    seq_load = jnp.sum(lengths * owned_mask).astype(jnp.int32)
    slot_index = jnp.arange(TOK_DEV, dtype=jnp.int32)
    passed = (seq_ends[None, :] <= slot_index[:, None]) & (owned_mask[None, :] > 0)
    segment = lax.optimization_barrier(jnp.sum(passed.astype(jnp.int32), axis=1)).astype(jnp.int32)
    in_use = slot_index < seq_load
    return (jnp.where(in_use, segment, TOK_DEV + slot_index).astype(jnp.int32), in_use)

def layer_norm(inputs, scale_gain, norm_shift):
    center = inputs - lax.optimization_barrier(jnp.mean(inputs, axis=-1, keepdims=True))
    spread = lax.optimization_barrier(jnp.mean(center * center, axis=-1, keepdims=True))
    return center * lax.rsqrt(spread + EPS) * scale_gain + norm_shift

def rotary_tables(positions):
    freq_index = jnp.arange(ROT_DIM // 2, dtype=jnp.float32)
    inverse = jnp.exp(freq_index * (-2.0 * math.log(10000.0) / ROT_DIM))
    angles = positions.astype(jnp.float32)[:, None] * inverse[None, :]
    return (jnp.cos(angles), jnp.sin(angles))

def rotate(field, cosine, sine_table):
    row_count = field.shape[0]
    head_count = field.shape[1]
    turned = field[..., :ROT_DIM].reshape(row_count, head_count, ROT_DIM // 2, 2)
    first_half = turned[..., 0]
    second_half = turned[..., 1]
    cos_wide = cosine[:, None, :]
    sin_wide = sine_table[:, None, :]
    joined = jnp.stack([first_half * cos_wide - second_half * sin_wide, second_half * cos_wide + first_half * sin_wide], -1)
    return jnp.concatenate([joined.reshape(row_count, head_count, ROT_DIM), field[..., ROT_DIM:]], -1)

def device_block(inputs, segment, positions, weights):
    qkv_weight, out_weight, in_weight, in_bias, fc_weight, fc_bias, norm_gain, norm_bias = weights
    row_count = inputs.shape[0]
    normed = low(layer_norm(inputs, norm_gain, norm_bias))
    merged_rows = low_back(jnp.dot(normed, qkv_weight, precision=PRECISION))
    cosine, sine_table = rotary_tables(positions)
    queries = merged_rows[:, :D].reshape(row_count, HEADS, HEAD_DIM)
    key_rows = merged_rows[:, D:2 * D].reshape(row_count, HEADS, HEAD_DIM)
    value_rows = merged_rows[:, 2 * D:].reshape(row_count, HEADS, HEAD_DIM)
    queries = low_back(low(rotate(queries, cosine, sine_table)))
    key_rows = low_back(low(rotate(key_rows, cosine, sine_table)))
    value_rows = low_back(low(value_rows))
    slot_index = jnp.arange(row_count, dtype=jnp.int32)
    allowed = (segment[:, None] == segment[None, :]) & (slot_index[None, :] <= slot_index[:, None])
    scores = jnp.einsum('qhd,khd->hqk', queries, key_rows, precision=PRECISION) * SCORE_SCALE
    scores = low_back(jnp.where(allowed[None], scores, NEG))
    soft_weights = low(jax.nn.softmax(scores, axis=-1))
    attended = jnp.einsum('hqk,khd->qhd', soft_weights, value_rows, precision=PRECISION).reshape(row_count, D)
    attended = low_back(low(attended))
    hidden = low_back(jnp.dot(normed, in_weight, precision=PRECISION) + in_bias)
    active = low(jax.nn.gelu(hidden, approximate=True))
    branch_attn = jnp.dot(attended, out_weight, precision=PRECISION)
    branch_mlp = jnp.dot(active, fc_weight, precision=PRECISION) + fc_bias
    return inputs + branch_attn + branch_mlp

def reference(tokens, positions, lengths, owner, qkv_weight, out_weight, in_weight, in_bias, fc_weight, fc_bias, norm_gain, norm_bias, cotangent):
    device_count = N_REP * N_SHARD
    device_ids = jnp.arange(device_count, dtype=jnp.int32)

    def one_layout(device):
        return layout(lengths, owner, device)
    segments, in_use = jax.vmap(one_layout)(device_ids)
    weights = (qkv_weight.astype(jnp.float32), out_weight.astype(jnp.float32), in_weight.astype(jnp.float32), in_bias.astype(jnp.float32), fc_weight.astype(jnp.float32), fc_bias.astype(jnp.float32), norm_gain.astype(jnp.float32), norm_bias.astype(jnp.float32))
    inputs_all = tokens.astype(jnp.float32).reshape(device_count, TOK_DEV, D)
    positions_all = positions.reshape(device_count, TOK_DEV)
    upstream = cotangent.astype(jnp.float32).reshape(device_count, TOK_DEV, D) * in_use[..., None].astype(jnp.float32)

    def forward(inputs_given, weights_given):

        def one_device(packed):
            block_in, block_segment, block_positions = packed
            return device_block(block_in, block_segment, block_positions, weights_given)
        return lax.map(jax.checkpoint(one_device), (inputs_given, segments, positions_all))
    outputs, pullback = jax.vjp(forward, inputs_all, weights)
    input_grads, weight_grads = pullback(upstream)
    grad_scale = 1.0 / math.sqrt(TOKENS)
    grad_qkv, grad_out, grad_in, grad_in_bias, grad_fc, grad_fc_bias, grad_gain, grad_norm_bias = weight_grads
    layer_out = outputs.reshape(TOKENS, D).astype(jnp.bfloat16)
    input_grad = input_grads.reshape(TOKENS, D).astype(jnp.bfloat16)
    return (layer_out, input_grad, grad_qkv * grad_scale, grad_out * grad_scale, grad_in * grad_scale, grad_in_bias * grad_scale, grad_fc * grad_scale, grad_fc_bias * grad_scale, grad_gain * grad_scale, grad_norm_bias * grad_scale)
```

```python
from functools import partial
import math

import jax
import jax.numpy as jnp
from jax import lax
from jax.sharding import PartitionSpec as P

D = 1024
HEADS = 16
HEAD_DIM = 64
ROT_DIM = 32
TOK_DEV = 512


EPS = 1e-05
NEG = -1000000000.0
SCORE_SCALE = 0.125


def layout(lengths, owner, device):
    owned_mask = (owner == device).astype(jnp.int32)
    seq_ends = jnp.cumsum(lengths * owned_mask)
    seq_load = jnp.sum(lengths * owned_mask)
    slot_index = jnp.arange(TOK_DEV, dtype=jnp.int32)
    passed = (seq_ends[None, :] <= slot_index[:, None]) & (owned_mask[None, :] > 0)
    segment = jnp.sum(passed.astype(jnp.int32), axis=1)
    in_use = slot_index < seq_load
    return (jnp.where(in_use, segment, TOK_DEV + slot_index), in_use)


def layer_norm(inputs, scale_gain, norm_shift):
    center = inputs - jnp.mean(inputs, axis=-1, keepdims=True)
    spread = jnp.mean(center * center, axis=-1, keepdims=True)
    return center * lax.rsqrt(spread + EPS) * scale_gain + norm_shift


def rotary_tables(positions):
    freq_index = jnp.arange(ROT_DIM // 2, dtype=jnp.float32)
    inverse = jnp.exp(freq_index * (-2.0 * math.log(10000.0) / ROT_DIM))
    angles = positions.astype(jnp.float32)[:, None] * inverse[None, :]
    return (jnp.cos(angles), jnp.sin(angles))


def rotate(field, cosine, sine_table):
    row_count = field.shape[0]
    head_count = field.shape[1]
    turned = field[..., :ROT_DIM].reshape(row_count, head_count, ROT_DIM // 2, 2)
    first_half = turned[..., 0]
    second_half = turned[..., 1]
    cos_wide = cosine[:, None, :]
    sin_wide = sine_table[:, None, :]
    joined = jnp.stack(
        [
            first_half * cos_wide - second_half * sin_wide,
            second_half * cos_wide + first_half * sin_wide,
        ],
        -1,
    )
    return jnp.concatenate(
        [joined.reshape(row_count, head_count, ROT_DIM), field[..., ROT_DIM:]], -1
    )


def block_scores(query_block, key_block, allowed_block):
    raw_scores = (
        jnp.einsum("qhd,khd->hqk", query_block, key_block, preferred_element_type=jnp.float32)
        * SCORE_SCALE
    )
    return jnp.where(allowed_block[None], raw_scores, NEG)


def attend(queries, key_rows, value_rows, allowed):
    row_count = queries.shape[0]
    head_count = queries.shape[1]
    block_rows = min(512, row_count)
    group_size = min(8, head_count)
    head_parts = []
    norm_parts = []
    for head_start in range(0, head_count, group_size):
        head_end = head_start + group_size
        scores = block_scores(
            queries[0:block_rows, head_start:head_end], key_rows[:, head_start:head_end], allowed
        )
        row_peak = jnp.max(scores, axis=-1, keepdims=True)
        exponent = jnp.exp(scores - row_peak)
        row_total = jnp.sum(exponent, axis=-1, keepdims=True)
        soft_weights = (exponent / row_total).astype(jnp.bfloat16)
        row_parts = jnp.einsum(
            "hqk,khd->qhd",
            soft_weights,
            value_rows[:, head_start:head_end],
            preferred_element_type=jnp.float32,
        )
        row_norms = (row_peak + jnp.log(row_total))[..., 0]
        head_parts.append(row_parts)
        norm_parts.append(row_norms)
    return (jnp.concatenate(head_parts, 1), jnp.concatenate(norm_parts, 0))


def attend_back(queries, key_rows, value_rows, grad_attended, log_norm, allowed):
    row_count = queries.shape[0]
    head_count = queries.shape[1]
    block_rows = min(512, row_count)
    group_size = min(8, head_count)
    query_parts = []
    key_parts = []
    value_parts = []
    for head_start in range(0, head_count, group_size):
        head_end = head_start + group_size
        key_block = key_rows[:, head_start:head_end]
        value_block = value_rows[:, head_start:head_end]
        query_block = queries[0:block_rows, head_start:head_end]
        grad_block = grad_attended[0:block_rows, head_start:head_end]
        scores = block_scores(query_block, key_block, allowed)
        soft_full = jnp.exp(scores - log_norm[head_start:head_end, 0:block_rows][..., None])
        soft_low = soft_full.astype(jnp.bfloat16)
        grad_soft = jnp.einsum(
            "qhd,khd->hqk", grad_block, value_block, preferred_element_type=jnp.float32
        )
        row_delta = jnp.sum(soft_full * grad_soft, axis=-1, keepdims=True)
        grad_scores = (soft_full * (grad_soft - row_delta)).astype(jnp.bfloat16)
        row_parts = (
            jnp.einsum("hqk,khd->qhd", grad_scores, key_block, preferred_element_type=jnp.float32)
            * SCORE_SCALE
        )
        key_sum = (
            jnp.einsum("hqk,qhd->khd", grad_scores, query_block, preferred_element_type=jnp.float32)
            * SCORE_SCALE
        )
        value_sum = jnp.einsum(
            "hqk,qhd->khd", soft_low, grad_block, preferred_element_type=jnp.float32
        )
        query_parts.append(row_parts)
        key_parts.append(key_sum)
        value_parts.append(value_sum)
    return (
        jnp.concatenate(query_parts, 1),
        jnp.concatenate(key_parts, 1),
        jnp.concatenate(value_parts, 1),
    )


def body(
    tokens,
    positions,
    lengths,
    owner,
    qkv_weight,
    out_weight,
    in_weight,
    in_bias,
    fc_weight,
    fc_bias,
    norm_gain,
    norm_bias,
    cotangent,
):
    device = lax.axis_index(("rep", "shard"))
    segment, in_use = layout(lengths, owner, device)
    row_count = tokens.shape[0]
    slot_index = jnp.arange(row_count, dtype=jnp.int32)
    allowed = (segment[:, None] == segment[None, :]) & (slot_index[None, :] <= slot_index[:, None])
    gathered = (
        lax.all_gather(qkv_weight, "shard", axis=0, tiled=True),
        lax.all_gather(out_weight, "shard", axis=0, tiled=True),
        lax.all_gather(in_weight, "shard", axis=0, tiled=True),
        lax.all_gather(in_bias, "shard", axis=0, tiled=True),
        lax.all_gather(fc_weight, "shard", axis=0, tiled=True),
        lax.all_gather(fc_bias, "shard", axis=0, tiled=True),
        lax.all_gather(norm_gain, "shard", axis=0, tiled=True),
        lax.all_gather(norm_bias, "shard", axis=0, tiled=True),
    )
    qkv_full, out_full, in_full, in_bias_full, fc_full, fc_bias_full, gain_full, shift_full = (
        gathered
    )
    inputs = tokens.astype(jnp.float32)
    normed = layer_norm(
        inputs, gain_full.astype(jnp.float32), shift_full.astype(jnp.float32)
    ).astype(jnp.bfloat16)
    merged_rows = jnp.dot(normed, qkv_full, preferred_element_type=jnp.float32)
    cosine, sine_table = rotary_tables(positions)
    queries = rotate(
        merged_rows[:, :D].reshape(row_count, HEADS, HEAD_DIM), cosine, sine_table
    ).astype(jnp.bfloat16)
    key_rows = rotate(
        merged_rows[:, D : 2 * D].reshape(row_count, HEADS, HEAD_DIM), cosine, sine_table
    ).astype(jnp.bfloat16)
    value_rows = merged_rows[:, 2 * D :].reshape(row_count, HEADS, HEAD_DIM).astype(jnp.bfloat16)
    attended, log_norm = attend(queries, key_rows, value_rows, allowed)
    attended_low = attended.reshape(row_count, D).astype(jnp.bfloat16)
    hidden = jnp.dot(normed, in_full, preferred_element_type=jnp.float32) + in_bias_full.astype(
        jnp.float32
    )
    active = jax.nn.gelu(hidden, approximate=True).astype(jnp.bfloat16)
    branch_attn = jnp.dot(attended_low, out_full, preferred_element_type=jnp.float32)
    branch_mlp = jnp.dot(active, fc_full, preferred_element_type=jnp.float32) + fc_bias_full.astype(
        jnp.float32
    )
    layer_out = (inputs + branch_attn + branch_mlp).astype(jnp.bfloat16)
    regathered = (
        lax.all_gather(qkv_weight, "shard", axis=0, tiled=True),
        lax.all_gather(out_weight, "shard", axis=0, tiled=True),
        lax.all_gather(in_weight, "shard", axis=0, tiled=True),
        lax.all_gather(fc_weight, "shard", axis=0, tiled=True),
        lax.all_gather(norm_gain, "shard", axis=0, tiled=True),
        lax.all_gather(norm_bias, "shard", axis=0, tiled=True),
    )
    qkv_back, out_back, in_back, fc_back, gain_back, shift_back = regathered
    upstream = cotangent * in_use[:, None].astype(jnp.bfloat16)
    grad_fc = jnp.einsum("tf,td->fd", active, upstream, preferred_element_type=jnp.float32)
    grad_fc_bias = jnp.sum(upstream.astype(jnp.float32), axis=0)
    grad_out = jnp.einsum("te,td->ed", attended_low, upstream, preferred_element_type=jnp.float32)
    grad_active = jnp.einsum("td,fd->tf", upstream, fc_back, preferred_element_type=jnp.float32)
    hidden_out, gelu_back = jax.vjp(partial(jax.nn.gelu, approximate=True), hidden)
    grad_hidden = gelu_back(grad_active)[0].astype(jnp.bfloat16)
    grad_in = jnp.einsum("td,tf->df", normed, grad_hidden, preferred_element_type=jnp.float32)
    grad_in_bias = jnp.sum(grad_hidden.astype(jnp.float32), axis=0)
    grad_attended = (
        jnp.einsum("td,ed->te", upstream, out_back, preferred_element_type=jnp.float32)
        .astype(jnp.bfloat16)
        .reshape(row_count, HEADS, HEAD_DIM)
    )
    grad_queries, grad_keys, grad_values = attend_back(
        queries, key_rows, value_rows, grad_attended, log_norm, allowed
    )
    query_back = rotate(
        grad_queries.astype(jnp.bfloat16).astype(jnp.float32), cosine, -sine_table
    ).reshape(row_count, D)
    key_back = rotate(
        grad_keys.astype(jnp.bfloat16).astype(jnp.float32), cosine, -sine_table
    ).reshape(row_count, D)
    grad_merged = jnp.concatenate(
        [query_back, key_back, grad_values.reshape(row_count, D)], -1
    ).astype(jnp.bfloat16)
    grad_qkv = jnp.einsum("td,te->de", normed, grad_merged, preferred_element_type=jnp.float32)
    grad_normed = jnp.einsum(
        "te,de->td", grad_merged, qkv_back, preferred_element_type=jnp.float32
    ) + jnp.einsum("tf,df->td", grad_hidden, in_back, preferred_element_type=jnp.float32)
    normed_again, norm_back = jax.vjp(
        layer_norm, inputs, gain_back.astype(jnp.float32), shift_back.astype(jnp.float32)
    )
    grad_inputs, grad_gain, grad_shift = norm_back(grad_normed)
    input_grad = (grad_inputs + upstream.astype(jnp.float32)).astype(jnp.bfloat16)
    rep_count = lax.axis_size("rep")
    shard_count = lax.axis_size("shard")
    grad_scale = 1.0 / math.sqrt(TOK_DEV * rep_count * shard_count)
    grad_qkv = (grad_qkv * grad_scale).astype(jnp.bfloat16)
    grad_out = (grad_out * grad_scale).astype(jnp.bfloat16)
    grad_in = (grad_in * grad_scale).astype(jnp.bfloat16)
    grad_in_bias = grad_in_bias * grad_scale
    grad_fc = (grad_fc * grad_scale).astype(jnp.bfloat16)
    grad_fc_bias = grad_fc_bias * grad_scale
    grad_gain = grad_gain * grad_scale
    grad_shift = grad_shift * grad_scale
    owner_sums = (
        lax.psum_scatter(grad_qkv, "shard", scatter_dimension=0, tiled=True),
        lax.psum_scatter(grad_out, "shard", scatter_dimension=0, tiled=True),
        lax.psum_scatter(grad_in, "shard", scatter_dimension=0, tiled=True),
        lax.psum_scatter(grad_in_bias, "shard", scatter_dimension=0, tiled=True),
        lax.psum_scatter(grad_fc, "shard", scatter_dimension=0, tiled=True),
        lax.psum_scatter(grad_fc_bias, "shard", scatter_dimension=0, tiled=True),
        lax.psum_scatter(grad_gain, "shard", scatter_dimension=0, tiled=True),
        lax.psum_scatter(grad_shift, "shard", scatter_dimension=0, tiled=True),
    )
    summed = lax.psum(
        (
            owner_sums[0],
            owner_sums[1],
            owner_sums[2],
            owner_sums[3],
            owner_sums[4],
            owner_sums[5],
            owner_sums[6],
            owner_sums[7],
        ),
        "rep",
    )
    return (
        layer_out,
        input_grad,
        summed[0].astype(jnp.float32),
        summed[1].astype(jnp.float32),
        summed[2].astype(jnp.float32),
        summed[3],
        summed[4].astype(jnp.float32),
        summed[5],
        summed[6],
        summed[7],
    )


def solution(mesh):
    in_specs = (
        P(("rep", "shard"), None),
        P(("rep", "shard")),
        P(),
        P(),
        P("shard", None),
        P("shard", None),
        P("shard", None),
        P("shard"),
        P("shard", None),
        P("shard"),
        P("shard"),
        P("shard"),
        P(("rep", "shard"), None),
    )
    out_specs = (
        P(("rep", "shard"), None),
        P(("rep", "shard"), None),
        P("shard", None),
        P("shard", None),
        P("shard", None),
        P("shard"),
        P("shard", None),
        P("shard"),
        P("shard"),
        P("shard"),
    )
    return jax.shard_map(body, mesh=mesh, in_specs=in_specs, out_specs=out_specs, check_vma=False)
```

```python
import functools
from functools import partial
import math

import jax
import jax.numpy as jnp
from jax import lax
from jax.experimental import pallas as pl
from jax.experimental.pallas import tpu as pltpu
from jax.sharding import PartitionSpec as P

D = 1024
HEADS = 16
HEAD_DIM = 64
ROT_DIM = 32
TOK_DEV = 512

MESH = pl.DeviceIdType.MESH
BLK = 128
COL = 512
SLOTS = 8
LAGS = (1, 2, 2, 2, 2, 2, 2, 2)

EPS = 1e-05
NEG = -1000000000.0
SCORE_SCALE = 0.125


def layout(lengths, owner, device):
    owned_mask = (owner == device).astype(jnp.int32)
    seq_ends = jnp.cumsum(lengths * owned_mask)
    seq_load = jnp.sum(lengths * owned_mask)
    slot_index = jnp.arange(TOK_DEV, dtype=jnp.int32)
    passed = (seq_ends[None, :] <= slot_index[:, None]) & (owned_mask[None, :] > 0)
    segment = jnp.sum(passed.astype(jnp.int32), axis=1)
    in_use = slot_index < seq_load
    return (jnp.where(in_use, segment, TOK_DEV + slot_index), in_use)


def layer_norm(inputs, scale_gain, norm_shift):
    center = inputs - jnp.mean(inputs, axis=-1, keepdims=True)
    spread = jnp.mean(center * center, axis=-1, keepdims=True)
    return center * lax.rsqrt(spread + EPS) * scale_gain + norm_shift


def rotary_tables(positions):
    freq_index = jnp.arange(ROT_DIM // 2, dtype=jnp.float32)
    inverse = jnp.exp(freq_index * (-2.0 * math.log(10000.0) / ROT_DIM))
    angles = positions.astype(jnp.float32)[:, None] * inverse[None, :]
    return (jnp.cos(angles), jnp.sin(angles))


def rotate(field, cosine, sine_table):
    row_count = field.shape[0]
    head_count = field.shape[1]
    turned = field[..., :ROT_DIM].reshape(row_count, head_count, ROT_DIM // 2, 2)
    first_half = turned[..., 0]
    second_half = turned[..., 1]
    cos_wide = cosine[:, None, :]
    sin_wide = sine_table[:, None, :]
    joined = jnp.stack(
        [
            first_half * cos_wide - second_half * sin_wide,
            second_half * cos_wide + first_half * sin_wide,
        ],
        -1,
    )
    return jnp.concatenate(
        [joined.reshape(row_count, head_count, ROT_DIM), field[..., ROT_DIM:]], -1
    )


def block_scores(query_block, key_block, allowed_block):
    raw_scores = (
        jnp.einsum("qhd,khd->hqk", query_block, key_block, preferred_element_type=jnp.float32)
        * SCORE_SCALE
    )
    return jnp.where(allowed_block[None], raw_scores, NEG)


def attend(queries, key_rows, value_rows, allowed):
    row_count = queries.shape[0]
    head_count = queries.shape[1]
    block_rows = min(512, row_count)
    group_size = min(8, head_count)
    head_parts = []
    norm_parts = []
    for head_start in range(0, head_count, group_size):
        head_end = head_start + group_size
        scores = block_scores(
            queries[0:block_rows, head_start:head_end], key_rows[:, head_start:head_end], allowed
        )
        row_peak = jnp.max(scores, axis=-1, keepdims=True)
        exponent = jnp.exp(scores - row_peak)
        row_total = jnp.sum(exponent, axis=-1, keepdims=True)
        soft_weights = (exponent / row_total).astype(jnp.bfloat16)
        row_parts = jnp.einsum(
            "hqk,khd->qhd",
            soft_weights,
            value_rows[:, head_start:head_end],
            preferred_element_type=jnp.float32,
        )
        row_norms = (row_peak + jnp.log(row_total))[..., 0]
        head_parts.append(row_parts)
        norm_parts.append(row_norms)
    return (jnp.concatenate(head_parts, 1), jnp.concatenate(norm_parts, 0))


def attend_back(queries, key_rows, value_rows, grad_attended, log_norm, allowed):
    row_count = queries.shape[0]
    head_count = queries.shape[1]
    block_rows = min(512, row_count)
    group_size = min(8, head_count)
    query_parts = []
    key_parts = []
    value_parts = []
    for head_start in range(0, head_count, group_size):
        head_end = head_start + group_size
        key_block = key_rows[:, head_start:head_end]
        value_block = value_rows[:, head_start:head_end]
        query_block = queries[0:block_rows, head_start:head_end]
        grad_block = grad_attended[0:block_rows, head_start:head_end]
        scores = block_scores(query_block, key_block, allowed)
        soft_full = jnp.exp(scores - log_norm[head_start:head_end, 0:block_rows][..., None])
        soft_low = soft_full.astype(jnp.bfloat16)
        grad_soft = jnp.einsum(
            "qhd,khd->hqk", grad_block, value_block, preferred_element_type=jnp.float32
        )
        row_delta = jnp.sum(soft_full * grad_soft, axis=-1, keepdims=True)
        grad_scores = (soft_full * (grad_soft - row_delta)).astype(jnp.bfloat16)
        row_parts = (
            jnp.einsum("hqk,khd->qhd", grad_scores, key_block, preferred_element_type=jnp.float32)
            * SCORE_SCALE
        )
        key_sum = (
            jnp.einsum("hqk,qhd->khd", grad_scores, query_block, preferred_element_type=jnp.float32)
            * SCORE_SCALE
        )
        value_sum = jnp.einsum(
            "hqk,qhd->khd", soft_low, grad_block, preferred_element_type=jnp.float32
        )
        query_parts.append(row_parts)
        key_parts.append(key_sum)
        value_parts.append(value_sum)
    return (
        jnp.concatenate(query_parts, 1),
        jnp.concatenate(key_parts, 1),
        jnp.concatenate(value_parts, 1),
    )


def reduce_kernel(n_rep, plan, lt_ref, r_ref, small_ref, out_ref, small_out,
                  c_send, c_keep, c_recv, y_send, y_keep, y_recv, work, recvs, s_buf, s_recv,
                  send_sem, recv_sem, s_send_sem, s_recv_sem):
    n_chunks = out_ref.shape[0]
    rep = lax.axis_index("rep")
    shard = lax.axis_index("shard")
    y, c = shard // 2, shard % 2
    nbits = int(math.log2(n_rep))
    bits = [(rep // (1 << b)) % 2 for b in range(nbits)]

    def rep_peer(b):
        return (rep + (1 << b) * (1 - 2 * bits[b]), shard)

    core_peer = (rep, shard + 1 - 2 * c)
    y_peer = (rep, shard + 2 - 4 * y)
    halving = list(range(min(3, nbits)))
    extra = list(range(min(3, nbits), nbits))
    sizes = [BLK >> (k + 1) for k in range(len(halving))]

    def base(k):
        off = 0
        for j in range(k):
            off = off + bits[halving[j]] * sizes[j]
        return off

    barrier = pltpu.get_barrier_semaphore()
    peers = [core_peer, y_peer] + [rep_peer(b) for b in range(nbits)]
    for p in peers:
        pl.semaphore_signal(barrier, inc=1, device_id=p, device_id_type=MESH)
    pl.semaphore_wait(barrier, len(peers))

    def copy(src, dst, stage, slot, peer):
        return pltpu.make_async_remote_copy(
            src_ref=src, dst_ref=dst, send_sem=send_sem.at[stage, slot],
            recv_sem=recv_sem.at[stage, slot], device_id=peer, device_id_type=MESH)

    def core_copy(t):
        s = t % SLOTS
        return copy(c_send.at[s], c_recv.at[s], 0, s, core_peer)

    def y_copy(t):
        s = t % SLOTS
        return copy(y_send.at[s], y_recv.at[s], 1, s, y_peer)

    def half_copy(k, t):
        s = t % SLOTS
        rows = sizes[k]
        start = pl.multiple_of(base(k) + (1 - bits[halving[k]]) * rows, 16)
        return copy(work.at[s, pl.ds(start, rows)], recvs[k].at[s], 2 + k, s, rep_peer(halving[k]))

    last = len(halving)

    def own():
        return pl.multiple_of(base(last), 16)

    tail = BLK >> last

    def extra_copy(j, t):
        s = t % SLOTS
        return copy(work.at[s, pl.ds(own(), tail)], recvs[last + j].at[s], 2 + last + j, s, rep_peer(extra[j]))

    def gather_copy(k, t):
        s = t % SLOTS
        rows = sizes[k]
        start = pl.multiple_of(base(k) + bits[halving[k]] * rows, 16)
        ref = out_ref.at[t, pl.ds(start, rows)]
        return copy(ref, ref, 2 + last + len(extra) + k, s, rep_peer(halving[k]))

    def compute(t):
        s = t % SLOTS
        lt_id, r_id = plan(t)
        for side, dst in ((1 - c, c_send), (c, c_keep)):
            lhs = lt_ref[lt_id, side].reshape(2 * BLK, lt_ref.shape[-1])
            part = jnp.dot(lhs, r_ref[r_id], preferred_element_type=jnp.float32)
            dst[s] = part.astype(jnp.bfloat16).reshape(2, BLK, COL)
        core_copy(t).start()

    def after_core(t):
        s = t % SLOTS
        core_copy(t).wait()
        y_send[s] = c_keep[s, 1 - y] + c_recv[s, 1 - y]
        y_copy(t).start()
        y_keep[s] = c_keep[s, y] + c_recv[s, y]

    def after_y(t):
        s = t % SLOTS
        y_copy(t).wait()
        work[s] = y_keep[s] + y_recv[s]
        half_copy(0, t).start()

    def after_half(k, t):
        s = t % SLOTS
        half_copy(k, t).wait()
        rows = sizes[k]
        start = pl.multiple_of(base(k + 1), 16)
        total = work[s, pl.ds(start, rows)] + recvs[k][s]
        if k + 1 < last:
            work[s, pl.ds(start, rows)] = total
            half_copy(k + 1, t).start()
        elif extra:
            work[s, pl.ds(start, rows)] = total
            extra_copy(0, t).start()
        else:
            out_ref[t, pl.ds(start, rows)] = total
            gather_copy(last - 1, t).start()

    def after_extra(j, t):
        s = t % SLOTS
        extra_copy(j, t).wait()
        total = work[s, pl.ds(own(), tail)] + recvs[last + j][s]
        if j + 1 < len(extra):
            work[s, pl.ds(own(), tail)] = total
            extra_copy(j + 1, t).start()
        else:
            out_ref[t, pl.ds(own(), tail)] = total
            gather_copy(last - 1, t).start()

    def after_gather(k, t):
        gather_copy(k, t).wait()
        if k > 0:
            gather_copy(k - 1, t).start()

    D = LAGS
    stages = [(0, compute), (D[0], after_core), (D[0]+D[1], after_y)]
    lag = D[0]+D[1]
    for k in range(last):
        lag += D[2+k]
        stages.append((lag, functools.partial(after_half, k)))
    for j in range(len(extra)):
        lag += 1
        stages.append((lag, functools.partial(after_extra, j)))
    for k in reversed(range(last)):
        lag += D[5+last-1-k]
        stages.append((lag, functools.partial(after_gather, k)))

    s_peers = peers

    def small_copy(j):
        return pltpu.make_async_remote_copy(
            src_ref=s_buf.at[j], dst_ref=s_recv.at[j], send_sem=s_send_sem.at[j],
            recv_sem=s_recv_sem.at[j], device_id=s_peers[j], device_id_type=MESH)

    def small_step(j):
        if j == 0:
            s_buf[0] = small_ref[...]
        else:
            small_copy(j - 1).wait()
            total = s_buf[j - 1] + s_recv[j - 1]
            if j < len(s_peers):
                s_buf[j] = total
            else:
                small_out[...] = total
        if j < len(s_peers):
            small_copy(j).start()

    def step(i, carry):
        for delay, stage in reversed(stages):
            @pl.when((i >= delay) & (i < n_chunks + delay))
            def _(stage=stage, delay=delay):
                stage(i - delay)
        for j in range(len(s_peers) + 1):
            @pl.when(i == 4 + j)
            def _(j=j):
                small_step(j)
        return carry

    lax.fori_loop(0, n_chunks + lag, step, 0)


def grad_reduce(lt, r, small, n_rep, n_chunks, plan):
    nbits = int(math.log2(n_rep))
    last = min(3, nbits)
    n_extra = nbits - last
    n_stage = 2 + last + n_extra + last
    bf = jnp.bfloat16
    recv_rows = [BLK >> (k + 1) for k in range(last)] + [BLK >> last] * n_extra
    chunk = (SLOTS, BLK, COL)
    pair = (SLOTS, 2, BLK, COL)
    n_small = 2 + nbits

    def kern(lt_ref, r_ref, small_ref, out_ref, small_out, c_send, c_keep, c_recv, y_send, y_keep, y_recv, work, *rest):
        recvs = rest[:len(recv_rows)]
        reduce_kernel(n_rep, plan, lt_ref, r_ref, small_ref, out_ref, small_out, c_send, c_keep, c_recv,
                      y_send, y_keep, y_recv, work, recvs, *rest[len(recv_rows):])

    vm = pl.BlockSpec(memory_space=pltpu.VMEM)
    return pl.pallas_call(
        kern,
        out_shape=(jax.ShapeDtypeStruct((n_chunks, BLK, COL), bf), jax.ShapeDtypeStruct(small.shape, jnp.float32)),
        in_specs=[vm, vm, vm],
        out_specs=(vm, vm),
        scratch_shapes=[
            pltpu.VMEM(pair, bf), pltpu.VMEM(pair, bf), pltpu.VMEM(pair, bf),
            pltpu.VMEM(chunk, bf), pltpu.VMEM(chunk, bf), pltpu.VMEM(chunk, bf), pltpu.VMEM(chunk, bf),
            *[pltpu.VMEM((SLOTS, rows, COL), bf) for rows in recv_rows],
            pltpu.VMEM((n_small,) + small.shape, jnp.float32), pltpu.VMEM((n_small,) + small.shape, jnp.float32),
            pltpu.SemaphoreType.DMA((n_stage, SLOTS)), pltpu.SemaphoreType.DMA((n_stage, SLOTS)),
            pltpu.SemaphoreType.DMA((n_small,)), pltpu.SemaphoreType.DMA((n_small,)),
        ],
        compiler_params=pltpu.CompilerParams(collective_id=1, has_side_effects=True, vmem_limit_bytes=60 * 2**20),
        name="grad_reduce",
    )(lt, r, small)


def chunk_plan(t):
    qkv = (t // 6, t % 6)
    o = (2 + (t - 12) // 2, 6 + (t - 12) % 2)
    a = ((t - 16) // 8, 8 + (t - 16) % 8)
    f = (4 + (t - 32) // 2, 6 + (t - 32) % 2)
    return tuple(jnp.where(t < 12, qkv[i], jnp.where(t < 16, o[i], jnp.where(t < 32, a[i], f[i]))) for i in range(2))


def body(
    tokens,
    positions,
    lengths,
    owner,
    qkv_weight,
    out_weight,
    in_weight,
    in_bias,
    fc_weight,
    fc_bias,
    norm_gain,
    norm_bias,
    cotangent,
):
    device = lax.axis_index(("rep", "shard"))
    segment, in_use = layout(lengths, owner, device)
    row_count = tokens.shape[0]
    slot_index = jnp.arange(row_count, dtype=jnp.int32)
    allowed = (segment[:, None] == segment[None, :]) & (slot_index[None, :] <= slot_index[:, None])
    gathered = (
        lax.all_gather(qkv_weight, "shard", axis=0, tiled=True),
        lax.all_gather(out_weight, "shard", axis=0, tiled=True),
        lax.all_gather(in_weight, "shard", axis=0, tiled=True),
        lax.all_gather(in_bias, "shard", axis=0, tiled=True),
        lax.all_gather(fc_weight, "shard", axis=0, tiled=True),
        lax.all_gather(fc_bias, "shard", axis=0, tiled=True),
        lax.all_gather(norm_gain, "shard", axis=0, tiled=True),
        lax.all_gather(norm_bias, "shard", axis=0, tiled=True),
    )
    qkv_full, out_full, in_full, in_bias_full, fc_full, fc_bias_full, gain_full, shift_full = (
        gathered
    )
    inputs = tokens.astype(jnp.float32)
    normed = layer_norm(
        inputs, gain_full.astype(jnp.float32), shift_full.astype(jnp.float32)
    ).astype(jnp.bfloat16)
    merged_rows = jnp.dot(normed, qkv_full, preferred_element_type=jnp.float32)
    cosine, sine_table = rotary_tables(positions)
    queries = rotate(
        merged_rows[:, :D].reshape(row_count, HEADS, HEAD_DIM), cosine, sine_table
    ).astype(jnp.bfloat16)
    key_rows = rotate(
        merged_rows[:, D : 2 * D].reshape(row_count, HEADS, HEAD_DIM), cosine, sine_table
    ).astype(jnp.bfloat16)
    value_rows = merged_rows[:, 2 * D :].reshape(row_count, HEADS, HEAD_DIM).astype(jnp.bfloat16)
    attended, log_norm = attend(queries, key_rows, value_rows, allowed)
    attended_low = attended.reshape(row_count, D).astype(jnp.bfloat16)
    hidden = jnp.dot(normed, in_full, preferred_element_type=jnp.float32) + in_bias_full.astype(
        jnp.float32
    )
    active = jax.nn.gelu(hidden, approximate=True).astype(jnp.bfloat16)
    branch_attn = jnp.dot(attended_low, out_full, preferred_element_type=jnp.float32)
    branch_mlp = jnp.dot(active, fc_full, preferred_element_type=jnp.float32) + fc_bias_full.astype(
        jnp.float32
    )
    layer_out = (inputs + branch_attn + branch_mlp).astype(jnp.bfloat16)
    regathered = (
        lax.all_gather(qkv_weight, "shard", axis=0, tiled=True),
        lax.all_gather(out_weight, "shard", axis=0, tiled=True),
        lax.all_gather(in_weight, "shard", axis=0, tiled=True),
        lax.all_gather(fc_weight, "shard", axis=0, tiled=True),
        lax.all_gather(norm_gain, "shard", axis=0, tiled=True),
        lax.all_gather(norm_bias, "shard", axis=0, tiled=True),
    )
    qkv_back, out_back, in_back, fc_back, gain_back, shift_back = regathered
    upstream = cotangent * in_use[:, None].astype(jnp.bfloat16)
    grad_fc_bias = jnp.sum(upstream.astype(jnp.float32), axis=0)
    grad_active = jnp.einsum("td,fd->tf", upstream, fc_back, preferred_element_type=jnp.float32)
    hidden_out, gelu_back = jax.vjp(partial(jax.nn.gelu, approximate=True), hidden)
    grad_hidden = gelu_back(grad_active)[0].astype(jnp.bfloat16)
    grad_in_bias = jnp.sum(grad_hidden.astype(jnp.float32), axis=0)
    grad_attended = (
        jnp.einsum("td,ed->te", upstream, out_back, preferred_element_type=jnp.float32)
        .astype(jnp.bfloat16)
        .reshape(row_count, HEADS, HEAD_DIM)
    )
    grad_queries, grad_keys, grad_values = attend_back(
        queries, key_rows, value_rows, grad_attended, log_norm, allowed
    )
    query_back = rotate(
        grad_queries.astype(jnp.bfloat16).astype(jnp.float32), cosine, -sine_table
    ).reshape(row_count, D)
    key_back = rotate(
        grad_keys.astype(jnp.bfloat16).astype(jnp.float32), cosine, -sine_table
    ).reshape(row_count, D)
    grad_merged = jnp.concatenate(
        [query_back, key_back, grad_values.reshape(row_count, D)], -1
    ).astype(jnp.bfloat16)
    grad_normed = jnp.einsum(
        "te,de->td", grad_merged, qkv_back, preferred_element_type=jnp.float32
    ) + jnp.einsum("tf,df->td", grad_hidden, in_back, preferred_element_type=jnp.float32)
    normed_again, norm_back = jax.vjp(
        layer_norm, inputs, gain_back.astype(jnp.float32), shift_back.astype(jnp.float32)
    )
    grad_inputs, grad_gain, grad_shift = norm_back(grad_normed)
    input_grad = (grad_inputs + upstream.astype(jnp.float32)).astype(jnp.bfloat16)
    rep_count = lax.axis_size("rep")
    shard_count = lax.axis_size("shard")
    shard = lax.axis_index("shard")
    grad_scale = 1.0 / math.sqrt(TOK_DEV * rep_count * shard_count)

    def left_blocks(rows):
        turned = rows.T.reshape(2, 2, -1, BLK, row_count)
        return turned.transpose(2, 1, 0, 3, 4)

    def right_blocks(rows):
        return rows.reshape(row_count, -1, COL).transpose(1, 0, 2)

    lt = jnp.concatenate([left_blocks(normed), left_blocks(attended_low), left_blocks(active)], 0)
    right = jnp.concatenate([right_blocks(grad_merged), right_blocks(upstream), right_blocks(grad_hidden)], 0)
    small = jnp.concatenate([grad_in_bias, grad_fc_bias, grad_gain, grad_shift]).reshape(-1, 128)
    blocks, small_sum = grad_reduce(lt, right, small, rep_count, 48, chunk_plan)

    def assemble(first, row_blocks, col_blocks):
        part = blocks[first : first + row_blocks * col_blocks].reshape(row_blocks, col_blocks, BLK, COL)
        part = part.transpose(0, 2, 1, 3).reshape(row_blocks * BLK, col_blocks * COL)
        return part.astype(jnp.float32) * grad_scale

    small_sum = small_sum.reshape(-1) * grad_scale

    def own_part(first, size):
        return lax.dynamic_slice_in_dim(small_sum, first + shard * (size // 4), size // 4)

    return (
        layer_out,
        input_grad,
        assemble(0, 2, 6),
        assemble(12, 2, 2),
        assemble(16, 2, 8),
        own_part(0, 4096),
        assemble(32, 8, 2),
        own_part(4096, D),
        own_part(4096 + D, D),
        own_part(4096 + 2 * D, D),
    )


def solution(mesh):
    in_specs = (
        P(("rep", "shard"), None),
        P(("rep", "shard")),
        P(),
        P(),
        P("shard", None),
        P("shard", None),
        P("shard", None),
        P("shard"),
        P("shard", None),
        P("shard"),
        P("shard"),
        P("shard"),
        P(("rep", "shard"), None),
    )
    out_specs = (
        P(("rep", "shard"), None),
        P(("rep", "shard"), None),
        P("shard", None),
        P("shard", None),
        P("shard", None),
        P("shard"),
        P("shard", None),
        P("shard"),
        P("shard"),
        P("shard"),
    )
    return jax.shard_map(body, mesh=mesh, in_specs=in_specs, out_specs=out_specs, check_vma=False)
```

```python
import functools
from functools import partial
import math

import jax
import jax.numpy as jnp
from jax import lax
from jax.experimental import pallas as pl
from jax.experimental.pallas import tpu as pltpu
from jax.sharding import PartitionSpec as P

D = 1024
HEADS = 16
HEAD_DIM = 64
ROT_DIM = 32
TOK_DEV = 512

MESH = pl.DeviceIdType.MESH
BLK = 128
COL = 512
SLOTS = 8
LAGS = (1, 2, 2, 2, 2, 2, 2, 2)

EPS = 1e-05
NEG = -1000000000.0
GELU_C = math.sqrt(2.0 / math.pi)
GELU_A = 0.044715
GATHER_LAGS = (0, 2, 4, 5)
SCORE_SCALE = 0.125


def layout(lengths, owner, device):
    owned_mask = (owner == device).astype(jnp.int32)
    seq_ends = jnp.cumsum(lengths * owned_mask)
    seq_load = jnp.sum(lengths * owned_mask)
    slot_index = jnp.arange(TOK_DEV, dtype=jnp.int32)
    passed = (seq_ends[None, :] <= slot_index[:, None]) & (owned_mask[None, :] > 0)
    segment = jnp.sum(passed.astype(jnp.int32), axis=1)
    in_use = slot_index < seq_load
    return (jnp.where(in_use, segment, TOK_DEV + slot_index), in_use)


def layer_norm(inputs, scale_gain, norm_shift):
    center = inputs - jnp.mean(inputs, axis=-1, keepdims=True)
    spread = jnp.mean(center * center, axis=-1, keepdims=True)
    return center * lax.rsqrt(spread + EPS) * scale_gain + norm_shift


def rotary_tables(positions):
    lane = jnp.arange(128, dtype=jnp.int32) % HEAD_DIM
    rotated = lane < ROT_DIM
    inverse = jnp.exp((lane // 2).astype(jnp.float32) * (-2.0 * math.log(10000.0) / ROT_DIM))
    angles = positions.astype(jnp.float32)[:, None] * jnp.where(rotated, inverse, 0.0)[None, :]
    sine = jnp.sin(angles)
    even = (lane % 2 == 0)[None, :]
    return (jnp.cos(angles), jnp.where(even, -sine, 0.0), jnp.where(even, 0.0, sine))


GATHER_CHUNKS = (4, 4, 4, 1)
FBLK = 256


def front_kernel(tok_ref, up_ref, cos_ref, sa_ref, sb_ref, small_ref, in_own, fc_own, qkv_own, out_own,
                 normed_ref, active_ref, gh_ref, rows_ref, base_ref, gn_ref, ga_ref, gib_ref, norm_ref,
                 qkv_full, out_full,
                 in_full, fc_full, small_full, bias_ref,
                 send_sem, recv_sem, core_send, core_recv, own_send, own_recv, local_sem, s_send, s_recv):
    rep = lax.axis_index("rep")
    shard = lax.axis_index("shard")
    y, c = shard // 2, shard % 2
    b0, b1 = rep % 2, (rep // 2) % 2
    core_shard = 2 * y + 1 - c
    other = 2 * (1 - y) + c
    diagonal = 2 * (1 - y) + 1 - c
    core_peer = (rep, core_shard)
    y_peer = (rep, other)
    diagonal_peer = (rep, diagonal)
    peer0 = (rep + 1 - 2 * b0, shard)
    peer1 = (rep + 2 - 4 * b1, shard)
    group = (core_peer, y_peer, diagonal_peer)

    barrier = pltpu.get_barrier_semaphore()
    for p in group + (peer0, peer1):
        pl.semaphore_signal(barrier, inc=1, device_id=p, device_id_type=MESH)
    pl.semaphore_wait(barrier, 5)

    owns = (in_own, fc_own, qkv_own, out_own)
    fulls = (in_full, fc_full, qkv_full, out_full)
    chunks = [(a, k) for a in range(4) for k in range(GATHER_CHUNKS[a])]
    n = len(chunks)
    ways = ((b0 + 2 * b1, b1, peer0, peer1), (b1 + 2 * b0, b0, peer1, peer0))

    def remote(src, dst, sems, index, peer):
        return pltpu.make_async_remote_copy(
            src_ref=src, dst_ref=dst, send_sem=sems[0].at[index], recv_sem=sems[1].at[index],
            device_id=peer, device_id_type=MESH)

    def place(i, h):
        a, k = chunks[i]
        own, full = owns[a], fulls[a]
        rows, cols = own.shape
        piece = rows // GATHER_CHUNKS[a] // 4
        return own, full, rows, k * 4 * piece, piece, pl.ds(h * (cols // 2), cols // 2)

    def y_copy(i, h):
        own, full, rows, start, piece, cols = place(i, h)
        at = pl.multiple_of(start + ways[h][0] * piece, 16)
        return remote(own.at[pl.ds(at, piece), cols],
                      full.at[pl.ds(pl.multiple_of(shard * rows + at, 16), piece), cols],
                      (send_sem, recv_sem), (0, i, h), y_peer)

    def first_copy(i, h):
        own, full, rows, start, piece, cols = place(i, h)
        at = pl.multiple_of(other * rows + start + ways[h][0] * piece, 16)
        ref = full.at[pl.ds(at, piece), cols]
        return remote(ref, ref, (send_sem, recv_sem), (1, i, h), ways[h][2])

    def second_copy(i, h):
        own, full, rows, start, piece, cols = place(i, h)
        at = pl.multiple_of(other * rows + start + ways[h][1] * 2 * piece, 16)
        ref = full.at[pl.ds(at, 2 * piece), cols]
        return remote(ref, ref, (send_sem, recv_sem), (2, i, h), ways[h][3])

    def core_copy(i):
        own, full, rows, start, piece, cols = place(i, 0)
        ref = full.at[pl.ds(pl.multiple_of(other * rows + start, 16), 4 * piece)]
        return remote(ref, ref, (core_send, core_recv), (i,), core_peer)

    def own_rows(a):
        rows = owns[a].shape[0]
        return fulls[a].at[pl.ds(pl.multiple_of(shard * rows, 16), rows)]

    def own_copy(a):
        return remote(owns[a], own_rows(a), (own_send, own_recv), (a,), core_peer)

    def local_copy(a):
        return pltpu.make_async_copy(owns[a], own_rows(a), local_sem.at[a])

    def small_copy(j):
        return remote(small_ref, small_full.at[shard], (s_send, s_recv), (j,), group[j])

    for j in range(3):
        small_copy(j).start()
    for i in range(n):
        for h in range(2):
            y_copy(i, h).start()
    for a in range(4):
        own_copy(a).start()
        local_copy(a).start()

    def norm_all():
        small_full[shard] = small_ref[...]
        for j in range(3):
            small_copy(j).wait()
        for o in range(4):
            for r in range(8):
                bias_ref[0:1, (o * 8 + r) * 128:(o * 8 + r + 1) * 128] = small_full[o, r:r + 1, :]
            for r in range(2):
                span = slice((o * 2 + r) * 128, (o * 2 + r + 1) * 128)
                norm_ref[2:3, span] = small_full[o, 8 + r:9 + r, :]
                norm_ref[0:1, span] = small_full[o, 10 + r:11 + r, :]
                norm_ref[1:2, span] = small_full[o, 12 + r:13 + r, :]

        def rows_step(r, carry):
            at = pl.ds(pl.multiple_of(r * 64, 64), 64)
            x = tok_ref[at, :].astype(jnp.float32)
            center = x - jnp.mean(x, axis=-1, keepdims=True)
            spread = jnp.mean(center * center, axis=-1, keepdims=True)
            normed = center * lax.rsqrt(spread + EPS) * norm_ref[0:1, :] + norm_ref[1:2, :]
            normed_ref[at, :] = normed.astype(jnp.bfloat16)
            base_ref[at, :] = x + norm_ref[2:3, :]
            return carry
        lax.fori_loop(0, TOK_DEV // 64, rows_step, 0)

    def span(j):
        return pl.ds(pl.multiple_of(j * FBLK, FBLK), FBLK)

    def hidden_block(j, carry):
        at = span(j)
        hidden = jnp.dot(normed_ref[...], in_full[:, at], preferred_element_type=jnp.float32) + bias_ref[0:1, at]
        cube = hidden * hidden
        turn = jnp.tanh(GELU_C * hidden * (1.0 + GELU_A * cube))
        half = 0.5 * (1.0 + turn)
        active_ref[:, at] = (hidden * half).astype(jnp.bfloat16)
        slope = half + 0.5 * hidden * (1.0 - turn * turn) * (GELU_C * (1.0 + 3.0 * GELU_A * cube))
        gh_ref[:, at] = slope.astype(jnp.bfloat16)
        return carry

    def back_block(j, carry):
        at = span(j)
        grad = lax.dot_general(up_ref[...], fc_full[at, :], (((1,), (1,)), ((), ())), preferred_element_type=jnp.float32)
        low = (grad * gh_ref[:, at].astype(jnp.float32)).astype(jnp.bfloat16)
        gh_ref[:, at] = low
        gib_ref[0:1, at] = jnp.sum(low.astype(jnp.float32), axis=0, keepdims=True)
        return carry

    def mlp_block(j, carry):
        at = span(j)
        base_ref[:, at] = base_ref[:, at] + jnp.dot(active_ref[...], fc_full[:, at], preferred_element_type=jnp.float32)
        gn_ref[:, at] = lax.dot_general(gh_ref[...], in_full[at, :], (((1,), (1,)), ((), ())), preferred_element_type=jnp.float32)
        return carry

    def turn_block(j, carry):
        at = span(j)
        rows = jnp.dot(normed_ref[...], qkv_full[:, at], preferred_element_type=jnp.float32)
        for g in range(FBLK // 128):
            part = rows[:, g * 128:(g + 1) * 128]
            turned = part * cos_ref[...] + pltpu.roll(part, 127, 1) * sa_ref[...] + pltpu.roll(part, 1, 1) * sb_ref[...]
            rows_ref[:, pl.ds(pl.multiple_of(j * FBLK + g * 128, 128), 128)] = turned.astype(jnp.bfloat16)
        return carry

    def value_block(j, carry):
        at = span(j)
        rows_ref[:, at] = jnp.dot(normed_ref[...], qkv_full[:, at], preferred_element_type=jnp.float32).astype(jnp.bfloat16)
        return carry

    def out_block(j, carry):
        at = span(j)
        ga_ref[:, at] = lax.dot_general(up_ref[...], out_full[at, :], (((1,), (1,)), ((), ())), preferred_element_type=jnp.float32).astype(jnp.bfloat16)
        return carry

    def loop(block, lo, hi):
        lax.fori_loop(lo, hi, block, 0)

    work = {0: [norm_all]}
    nf = 4096 // FBLK
    lag = GATHER_LAGS
    ends = [sum(GATHER_CHUNKS[:a + 1]) - 1 + lag[3] for a in range(4)]

    def ready(a):
        own_copy(a).wait_recv()
        local_copy(a).wait()

    def plan(step, *todo):
        work.setdefault(step, []).extend(todo)

    plan(ends[0], functools.partial(ready, 0))
    for j in range(4):
        plan(ends[0] + j, functools.partial(loop, hidden_block, j * nf // 4, (j + 1) * nf // 4))
    plan(ends[1], functools.partial(ready, 1))
    for j in range(4):
        plan(ends[1] + j, functools.partial(loop, back_block, j * nf // 4, (j + 1) * nf // 4))
    plan(ends[2], functools.partial(ready, 2), functools.partial(loop, mlp_block, 0, D // FBLK),
         functools.partial(loop, turn_block, 0, 2 * D // FBLK), functools.partial(loop, value_block, 2 * D // FBLK, 3 * D // FBLK))
    plan(ends[3], functools.partial(ready, 3), functools.partial(loop, out_block, 0, D // FBLK))

    for i in range(n + lag[3]):
        if i < n:
            for h in range(2):
                y_copy(i, h).wait_recv()
                first_copy(i, h).start()
        if 0 <= i - lag[1] < n:
            for h in range(2):
                first_copy(i - lag[1], h).wait_recv()
                second_copy(i - lag[1], h).start()
        if 0 <= i - lag[2] < n:
            for h in range(2):
                second_copy(i - lag[2], h).wait_recv()
            core_copy(i - lag[2]).start()
        if 0 <= i - lag[3] < n:
            core_copy(i - lag[3]).wait_recv()
        for todo in work.get(i, []):
            todo()
    for i in range(n):
        for h in range(2):
            y_copy(i, h).wait_send()
            first_copy(i, h).wait_send()
            second_copy(i, h).wait_send()
        core_copy(i).wait_send()
    for a in range(4):
        own_copy(a).wait_send()


def front(tokens, upstream, tables, small, in_own, fc_own, qkv_own, out_own, shards):
    bf, f32 = jnp.bfloat16, jnp.float32
    rows = tokens.shape[0]
    ff = in_own.shape[1]
    n = sum(GATHER_CHUNKS)
    vm = pl.BlockSpec(memory_space=pltpu.VMEM)
    hbm = pl.BlockSpec(memory_space=pl.ANY)

    def full(own):
        return (own.shape[0] * shards, own.shape[1])
    out_shape = [
        ((rows, D), bf), ((rows, ff), bf), ((rows, ff), bf), ((rows, 3 * D), bf), ((rows, D), f32), ((rows, D), f32),
        ((rows, D), bf), ((1, ff), f32), ((8, D), f32), (full(qkv_own), bf), (full(out_own), bf),
    ]
    dma = pltpu.SemaphoreType.DMA
    return pl.pallas_call(
        front_kernel,
        out_shape=[jax.ShapeDtypeStruct(s, d) for s, d in out_shape],
        in_specs=[vm] * 6 + [hbm] * 4,
        out_specs=[vm] * len(out_shape),
        scratch_shapes=[
            pltpu.VMEM(full(in_own), bf), pltpu.VMEM(full(fc_own), bf),
            pltpu.VMEM((shards,) + small.shape, f32), pltpu.VMEM((1, ff), f32),
            dma((3, n, 2)), dma((3, n, 2)), dma((n,)), dma((n,)), dma((4,)), dma((4,)), dma((4,)), dma((3,)), dma((3,)),
        ],
        compiler_params=pltpu.CompilerParams(collective_id=2, has_side_effects=True, vmem_limit_bytes=62 * 2**20),
        name="front",
    )(tokens, upstream, *tables, small, in_own, fc_own, qkv_own, out_own)


def attention_kernel(q_ref, k_ref, v_ref, ga_ref, seg_col, seg_row, cos_ref, sa_ref, sb_ref, att_ref, gm_ref, bias_ref):
    pair = pl.program_id(0)

    @pl.when(pair == 0)
    def _():
        row = lax.broadcasted_iota(jnp.int32, (TOK_DEV, TOK_DEV), 0)
        col = lax.broadcasted_iota(jnp.int32, (TOK_DEV, TOK_DEV), 1)
        allowed = (seg_col[...] == seg_row[...]) & (col <= row)
        bias_ref[...] = jnp.where(allowed, 0.0, NEG)

    attend_pair(pair, q_ref[...], k_ref[...], v_ref[...], ga_ref[...], bias_ref, cos_ref, sa_ref, sb_ref,
                lambda value: att_ref.__setitem__(Ellipsis, value),
                lambda part, value: gm_ref.__setitem__((slice(None), pl.ds(pl.multiple_of(part * D + pair * 128, 128), 128)), value))


QBLK = 256


def attend_pair(pair, q, k, v, ga, bias_ref, cos_ref, sa_ref, sb_ref, put_att, put_grad):
    f32, bf = jnp.float32, jnp.bfloat16
    nt = (((1,), (1,)), ((), ()))
    tn = (((0,), (0,)), ((), ()))
    lane = lax.broadcasted_iota(jnp.int32, (1, 128), 1)
    keep = [(lane < HEAD_DIM).astype(f32).astype(bf), (lane >= HEAD_DIM).astype(f32).astype(bf)]
    q = q * jnp.asarray(SCORE_SCALE, bf)
    attended, grad_q = [], []
    grad_k, grad_v = {}, {}
    n_blocks = TOK_DEV // QBLK

    def add(store, block, value):
        store[block] = value if block not in store else store[block] + value

    for r in range(n_blocks):
        rows = slice(r * QBLK, (r + 1) * QBLK)
        keys = (r + 1) * QBLK
        att = gq = None
        for h in range(2):
            qh = q[rows] * keep[h]
            gh = ga[rows] * keep[h]
            kh = k[:keys] * keep[h]
            vh = v[:keys] * keep[h]
            scores = lax.dot_general(qh, k[:keys], nt, preferred_element_type=f32) + bias_ref[rows, :keys]
            weight = jnp.exp(scores - jnp.max(scores, axis=-1, keepdims=True))
            soft = weight * (1.0 / jnp.sum(weight, axis=-1, keepdims=True))
            low = soft.astype(bf)
            grad_soft = lax.dot_general(gh, v[:keys], nt, preferred_element_type=f32)
            weighted = soft * grad_soft
            delta = jnp.sum(weighted, axis=-1, keepdims=True)
            grad_scores = (weighted - soft * delta).astype(bf)
            part = jnp.dot(low, vh, preferred_element_type=f32)
            att = part if att is None else att + part
            part = jnp.dot(grad_scores, kh, preferred_element_type=f32)
            gq = part if gq is None else gq + part
            gk = lax.dot_general(grad_scores, qh, tn, preferred_element_type=f32)
            gv = lax.dot_general(low, gh, tn, preferred_element_type=f32)
            for b in range(r + 1):
                span = slice(b * QBLK, (b + 1) * QBLK)
                add(grad_k, b, gk[span])
                add(grad_v, b, gv[span])
        attended.append(att)
        grad_q.append(gq)

    def unturn(x):
        x = x.astype(bf).astype(f32)
        return x * cos_ref[...] - pltpu.roll(x, 127, 1) * sa_ref[...] - pltpu.roll(x, 1, 1) * sb_ref[...]

    put_att(jnp.concatenate(attended, 0).astype(bf))
    put_grad(0, unturn(jnp.concatenate(grad_q, 0) * SCORE_SCALE).astype(bf))
    put_grad(1, unturn(jnp.concatenate([grad_k[b] for b in range(n_blocks)], 0)).astype(bf))
    put_grad(2, jnp.concatenate([grad_v[b] for b in range(n_blocks)], 0).astype(bf))


def attention(rows, ga, segment, tables):
    bf = jnp.bfloat16
    t = rows.shape[0]
    pairs = HEADS // 2
    whole = pl.BlockSpec(memory_space=pltpu.VMEM)
    return pl.pallas_call(
        attention_kernel,
        grid=(pairs,),
        out_shape=[jax.ShapeDtypeStruct((t, D), bf), jax.ShapeDtypeStruct((t, 3 * D), bf)],
        in_specs=[
            pl.BlockSpec((t, 128), lambda p: (0, p)), pl.BlockSpec((t, 128), lambda p: (0, pairs + p)),
            pl.BlockSpec((t, 128), lambda p: (0, 2 * pairs + p)), pl.BlockSpec((t, 128), lambda p: (0, p)),
            whole, whole, whole, whole, whole,
        ],
        out_specs=[pl.BlockSpec((t, 128), lambda p: (0, p)), pl.BlockSpec((t, 3 * D), lambda p: (0, 0))],
        scratch_shapes=[pltpu.VMEM((t, t), jnp.float32)],
        compiler_params=pltpu.CompilerParams(vmem_limit_bytes=48 * 2**20),
        name="attention",
    )(rows, rows, rows, ga, segment[:, None], segment[None, :], *tables)


def reduce_kernel(n_rep, normed_hbm, attended_hbm, active_hbm, gm_hbm, up_hbm, gh_hbm, small_ref, out_ref, small_out,
                  left, right, turned, load_sem, c_send, c_keep, c_recv, y_send, y_keep, y_recv, work, recvs, s_buf, s_recv,
                  send_sem, recv_sem, s_send_sem, s_recv_sem):
    n_chunks = out_ref.shape[0]
    rep = lax.axis_index("rep")
    shard = lax.axis_index("shard")
    y, c = shard // 2, shard % 2
    nbits = int(math.log2(n_rep))
    bits = [(rep // (1 << b)) % 2 for b in range(nbits)]

    def rep_peer(b):
        return (rep + (1 << b) * (1 - 2 * bits[b]), shard)

    core_peer = (rep, shard + 1 - 2 * c)
    y_peer = (rep, shard + 2 - 4 * y)
    halving = list(range(min(3, nbits)))
    extra = list(range(min(3, nbits), nbits))
    sizes = [BLK >> (k + 1) for k in range(len(halving))]

    def base(k):
        off = 0
        for j in range(k):
            off = off + bits[halving[j]] * sizes[j]
        return off

    loads = [
        pltpu.make_async_copy(src, dst.at[:, pl.ds(first, src.shape[1])], load_sem.at[j])
        for j, (src, dst, first) in enumerate([
            (normed_hbm, left, 0), (gh_hbm, right, 4 * D), (active_hbm, left, 2 * D), (up_hbm, right, 3 * D),
            (attended_hbm, left, D), (gm_hbm, right, 0)])]
    for load in loads:
        load.start()

    barrier = pltpu.get_barrier_semaphore()
    peers = [core_peer, y_peer] + [rep_peer(b) for b in range(nbits)]
    for p in peers:
        pl.semaphore_signal(barrier, inc=1, device_id=p, device_id_type=MESH)
    pl.semaphore_wait(barrier, len(peers))

    def copy(src, dst, stage, slot, peer):
        return pltpu.make_async_remote_copy(
            src_ref=src, dst_ref=dst, send_sem=send_sem.at[stage, slot],
            recv_sem=recv_sem.at[stage, slot], device_id=peer, device_id_type=MESH)

    def core_copy(t):
        s = t % SLOTS
        return copy(c_send.at[s], c_recv.at[s], 0, s, core_peer)

    def y_copy(t):
        s = t % SLOTS
        return copy(y_send.at[s], y_recv.at[s], 1, s, y_peer)

    def half_copy(k, t):
        s = t % SLOTS
        rows = sizes[k]
        start = pl.multiple_of(base(k) + (1 - bits[halving[k]]) * rows, 16)
        return copy(work.at[s, pl.ds(start, rows)], recvs[k].at[s], 2 + k, s, rep_peer(halving[k]))

    last = len(halving)

    def own():
        return pl.multiple_of(base(last), 16)

    tail = BLK >> last

    def extra_copy(j, t):
        s = t % SLOTS
        return copy(work.at[s, pl.ds(own(), tail)], recvs[last + j].at[s], 2 + last + j, s, rep_peer(extra[j]))

    def gather_copy(k, t):
        s = t % SLOTS
        rows = sizes[k]
        start = pl.multiple_of(base(k) + bits[halving[k]] * rows, 16)
        ref = out_ref.at[t, pl.ds(start, rows)]
        return copy(ref, ref, 2 + last + len(extra) + k, s, rep_peer(halving[k]))

    def compute(t):
        s = t % SLOTS
        for at, ready in ((0, loads[:2]), (16, loads[2:4]), (32, loads[4:])):
            @pl.when(t == at)
            def _(ready=ready):
                for load in ready:
                    load.wait()
        first, stride, column, new = chunk_plan(t)

        @pl.when(new)
        def _():
            for o in range(4):
                at = pl.multiple_of(first + o * stride, BLK)
                turned[o % 2, (o // 2) * BLK:(o // 2 + 1) * BLK, :] = left[:, pl.ds(at, BLK)].T
        operand = right[:, pl.ds(pl.multiple_of(column, COL), COL)]
        for side, dst in ((1 - c, c_send), (c, c_keep)):
            part = jnp.dot(turned[side], operand, preferred_element_type=jnp.float32)
            dst[s] = part.astype(jnp.bfloat16).reshape(2, BLK, COL)
        core_copy(t).start()

    def after_core(t):
        s = t % SLOTS
        core_copy(t).wait()
        y_send[s] = c_keep[s, 1 - y] + c_recv[s, 1 - y]
        y_copy(t).start()
        y_keep[s] = c_keep[s, y] + c_recv[s, y]

    def after_y(t):
        s = t % SLOTS
        y_copy(t).wait()
        work[s] = y_keep[s] + y_recv[s]
        half_copy(0, t).start()

    def after_half(k, t):
        s = t % SLOTS
        half_copy(k, t).wait()
        rows = sizes[k]
        start = pl.multiple_of(base(k + 1), 16)
        total = work[s, pl.ds(start, rows)] + recvs[k][s]
        if k + 1 < last:
            work[s, pl.ds(start, rows)] = total
            half_copy(k + 1, t).start()
        elif extra:
            work[s, pl.ds(start, rows)] = total
            extra_copy(0, t).start()
        else:
            out_ref[t, pl.ds(start, rows)] = total
            gather_copy(last - 1, t).start()

    def after_extra(j, t):
        s = t % SLOTS
        extra_copy(j, t).wait()
        total = work[s, pl.ds(own(), tail)] + recvs[last + j][s]
        if j + 1 < len(extra):
            work[s, pl.ds(own(), tail)] = total
            extra_copy(j + 1, t).start()
        else:
            out_ref[t, pl.ds(own(), tail)] = total
            gather_copy(last - 1, t).start()

    def after_gather(k, t):
        gather_copy(k, t).wait()
        if k > 0:
            gather_copy(k - 1, t).start()

    stages = [(0, compute), (LAGS[0], after_core), (LAGS[0]+LAGS[1], after_y)]
    lag = LAGS[0]+LAGS[1]
    for k in range(last):
        lag += LAGS[2+k]
        stages.append((lag, functools.partial(after_half, k)))
    for j in range(len(extra)):
        lag += 1
        stages.append((lag, functools.partial(after_extra, j)))
    for k in reversed(range(last)):
        lag += LAGS[5+last-1-k]
        stages.append((lag, functools.partial(after_gather, k)))

    s_peers = peers

    def small_copy(j):
        return pltpu.make_async_remote_copy(
            src_ref=s_buf.at[j], dst_ref=s_recv.at[j], send_sem=s_send_sem.at[j],
            recv_sem=s_recv_sem.at[j], device_id=s_peers[j], device_id_type=MESH)

    def small_step(j):
        if j == 0:
            s_buf[0] = small_ref[...]
        else:
            small_copy(j - 1).wait()
            total = s_buf[j - 1] + s_recv[j - 1]
            if j < len(s_peers):
                s_buf[j] = total
            else:
                small_out[...] = total
        if j < len(s_peers):
            small_copy(j).start()

    def step(i, carry):
        for delay, stage in reversed(stages):
            @pl.when((i >= delay) & (i < n_chunks + delay))
            def _(stage=stage, delay=delay):
                stage(i - delay)
        for j in range(len(s_peers) + 1):
            @pl.when(i == 4 + j)
            def _(j=j):
                small_step(j)
        return carry

    lax.fori_loop(0, n_chunks + lag, step, 0)


def grad_reduce(operands, small, n_rep, n_chunks):
    nbits = int(math.log2(n_rep))
    last = min(3, nbits)
    n_extra = nbits - last
    n_stage = 2 + last + n_extra + last
    bf = jnp.bfloat16
    recv_rows = [BLK >> (k + 1) for k in range(last)] + [BLK >> last] * n_extra
    chunk = (SLOTS, BLK, COL)
    pair = (SLOTS, 2, BLK, COL)
    n_small = 2 + nbits

    def kern(*refs):
        fixed, rest = refs[:20], refs[20:]
        recvs = rest[:len(recv_rows)]
        reduce_kernel(n_rep, *fixed, recvs, *rest[len(recv_rows):])

    tokens = operands[0].shape[0]
    hbm = pl.BlockSpec(memory_space=pl.ANY)
    vm = pl.BlockSpec(memory_space=pltpu.VMEM)
    return pl.pallas_call(
        kern,
        out_shape=(jax.ShapeDtypeStruct((n_chunks, BLK, COL), bf), jax.ShapeDtypeStruct(small.shape, jnp.float32)),
        in_specs=[hbm] * 6 + [vm],
        out_specs=(vm, vm),
        scratch_shapes=[
            pltpu.VMEM((tokens, 6 * D), bf), pltpu.VMEM((tokens, 8 * D), bf), pltpu.VMEM((2, 2 * BLK, tokens), bf),
            pltpu.SemaphoreType.DMA((6,)),
            pltpu.VMEM(pair, bf), pltpu.VMEM(pair, bf), pltpu.VMEM(pair, bf),
            pltpu.VMEM(chunk, bf), pltpu.VMEM(chunk, bf), pltpu.VMEM(chunk, bf), pltpu.VMEM(chunk, bf),
            *[pltpu.VMEM((SLOTS, rows, COL), bf) for rows in recv_rows],
            pltpu.VMEM((n_small,) + small.shape, jnp.float32), pltpu.VMEM((n_small,) + small.shape, jnp.float32),
            pltpu.SemaphoreType.DMA((n_stage, SLOTS)), pltpu.SemaphoreType.DMA((n_stage, SLOTS)),
            pltpu.SemaphoreType.DMA((n_small,)), pltpu.SemaphoreType.DMA((n_small,)),
        ],
        compiler_params=pltpu.CompilerParams(collective_id=1, has_side_effects=True, vmem_limit_bytes=60 * 2**20),
        name="grad_reduce",
    )(*operands, small)


def chunk_plan(t):
    cases = [
        ((t // 8) * BLK, D // 4, 4 * D + (t % 8) * COL, t % 8),
        (2 * D + ((t - 16) // 2) * BLK, D, 3 * D + (t % 2) * COL, t % 2),
        (((t - 32) // 6) * BLK, D // 4, ((t - 32) % 6) * COL, (t - 32) % 6),
        (D + ((t - 44) // 2) * BLK, D // 4, 3 * D + (t % 2) * COL, t % 2),
    ]
    first, stride, column, within = (
        jnp.where(t < 16, cases[0][i], jnp.where(t < 32, cases[1][i], jnp.where(t < 44, cases[2][i], cases[3][i])))
        for i in range(4))
    return first, stride, column, within == 0


def assemble(blocks, first, rows, cols, width, scale):
    def kern(in_ref, out_ref):
        for j in range(width):
            out_ref[:, j * COL:(j + 1) * COL] = in_ref[j].astype(jnp.float32) * scale

    across = cols // COL // width
    return pl.pallas_call(
        kern,
        grid=(rows // BLK, across),
        out_shape=jax.ShapeDtypeStruct((rows, cols), jnp.float32),
        in_specs=[pl.BlockSpec((width, BLK, COL), lambda i, j: (first // width + i * across + j, 0, 0))],
        out_specs=pl.BlockSpec((BLK, width * COL), lambda i, j: (i, j)),
        name="assemble",
    )(blocks)


def body(
    tokens,
    positions,
    lengths,
    owner,
    qkv_weight,
    out_weight,
    in_weight,
    in_bias,
    fc_weight,
    fc_bias,
    norm_gain,
    norm_bias,
    cotangent,
):
    rep_count = lax.axis_size("rep")
    shard_count = lax.axis_size("shard")
    device = lax.axis_index(("rep", "shard"))
    shard = lax.axis_index("shard")
    grad_scale = 1.0 / math.sqrt(TOK_DEV * rep_count * shard_count)
    segment, in_use = layout(lengths, owner, device)
    tables = rotary_tables(positions)
    upstream = cotangent * in_use[:, None].astype(jnp.bfloat16)
    small = jnp.concatenate([in_bias, fc_bias, norm_gain, norm_bias, jnp.zeros((256,), jnp.bfloat16)])
    small = small.astype(jnp.float32).reshape(16, 128)
    normed, active, grad_hidden, rows, base, grad_ff, grad_attended, grad_in_bias, norms, qkv_full, out_full = front(
        tokens, upstream, tables, small, in_weight, fc_weight, qkv_weight, out_weight, shard_count)
    attended, grad_merged = attention(rows, grad_attended, segment, tables)
    layer_out = (base + jnp.dot(attended, out_full, preferred_element_type=jnp.float32)).astype(jnp.bfloat16)
    grad_normed = grad_ff + jnp.einsum("te,de->td", grad_merged, qkv_full, preferred_element_type=jnp.float32)
    inputs = tokens.astype(jnp.float32)
    upstream_wide = upstream.astype(jnp.float32)
    _, norm_back = jax.vjp(layer_norm, inputs, norms[0], norms[1])
    grad_inputs, grad_gain, grad_shift = norm_back(grad_normed)
    input_grad = (grad_inputs + upstream_wide).astype(jnp.bfloat16)
    grad_fc_bias = jnp.sum(upstream_wide, axis=0)
    small_grads = jnp.concatenate([grad_in_bias[0], grad_fc_bias, grad_gain, grad_shift]).reshape(-1, 128)
    blocks, small_sum = grad_reduce(
        (normed, attended, active, grad_merged, upstream, grad_hidden), small_grads, rep_count, 48)
    small_sum = small_sum.reshape(-1) * grad_scale

    def own_part(first, size):
        return lax.dynamic_slice_in_dim(small_sum, first + shard * (size // 4), size // 4)

    return (
        layer_out,
        input_grad,
        assemble(blocks, 32, 256, 3 * D, 2, grad_scale),
        assemble(blocks, 44, 256, D, 2, grad_scale),
        assemble(blocks, 0, 256, 4 * D, 8, grad_scale),
        own_part(0, 4096),
        assemble(blocks, 16, 1024, D, 2, grad_scale),
        own_part(4096, D),
        own_part(4096 + D, D),
        own_part(4096 + 2 * D, D),
    )


def solution(mesh):
    in_specs = (
        P(("rep", "shard"), None),
        P(("rep", "shard")),
        P(),
        P(),
        P("shard", None),
        P("shard", None),
        P("shard", None),
        P("shard"),
        P("shard", None),
        P("shard"),
        P("shard"),
        P("shard"),
        P(("rep", "shard"), None),
    )
    out_specs = (
        P(("rep", "shard"), None),
        P(("rep", "shard"), None),
        P("shard", None),
        P("shard", None),
        P("shard", None),
        P("shard"),
        P("shard", None),
        P("shard"),
        P("shard"),
        P("shard"),
    )
    return jax.shard_map(body, mesh=mesh, in_specs=in_specs, out_specs=out_specs, check_vma=False)
```

```python
import functools
from functools import partial
import math

import jax
import jax.numpy as jnp
from jax import lax
from jax.experimental import pallas as pl
from jax.experimental.pallas import tpu as pltpu
from jax.sharding import PartitionSpec as P

D = 1024
HEADS = 16
HEAD_DIM = 64
ROT_DIM = 32
TOK_DEV = 512

MESH = pl.DeviceIdType.MESH
BLK = 128
COL = 512
SLOTS = 8
LAGS = (1, 2, 2, 2, 2, 2, 2, 2)

EPS = 1e-05
NEG = -1000000000.0
GELU_C = math.sqrt(2.0 / math.pi)
GELU_A = 0.044715
GATHER_LAGS = (0, 2, 4, 5)
SCORE_SCALE = 0.125


def layout(lengths, owner, device):
    owned_mask = (owner == device).astype(jnp.int32)
    seq_ends = jnp.cumsum(lengths * owned_mask)
    seq_load = jnp.sum(lengths * owned_mask)
    slot_index = jnp.arange(TOK_DEV, dtype=jnp.int32)
    passed = (seq_ends[None, :] <= slot_index[:, None]) & (owned_mask[None, :] > 0)
    segment = jnp.sum(passed.astype(jnp.int32), axis=1)
    in_use = slot_index < seq_load
    return (jnp.where(in_use, segment, TOK_DEV + slot_index), in_use)


def rotary_tables(positions):
    lane = jnp.arange(128, dtype=jnp.int32) % HEAD_DIM
    rotated = lane < ROT_DIM
    inverse = jnp.exp((lane // 2).astype(jnp.float32) * (-2.0 * math.log(10000.0) / ROT_DIM))
    angles = positions.astype(jnp.float32)[:, None] * jnp.where(rotated, inverse, 0.0)[None, :]
    sine = jnp.sin(angles)
    even = (lane % 2 == 0)[None, :]
    return (jnp.cos(angles), jnp.where(even, -sine, 0.0), jnp.where(even, 0.0, sine))


GATHER_CHUNKS = (4, 4, 4, 1)
FBLK = 256


def front_kernel(tok_ref, up_ref, small_ref, in_own, fc_own, qkv_own, out_own,
                 normed_out, active_out, gh_out, base_out, gn_out, gib_ref, norm_ref, qkv_full, out_full,
                 in_full, fc_full, qkv_stage, out_stage, normed_ref, active_ref, gh_ref, base_ref, gn_ref,
                 small_full, bias_ref,
                 send_sem, recv_sem, core_send, core_recv, own_send, own_recv, local_sem, store_sem, s_send, s_recv):
    rep = lax.axis_index("rep")
    shard = lax.axis_index("shard")
    y, c = shard // 2, shard % 2
    b0, b1 = rep % 2, (rep // 2) % 2
    core_shard = 2 * y + 1 - c
    other = 2 * (1 - y) + c
    diagonal = 2 * (1 - y) + 1 - c
    core_peer = (rep, core_shard)
    y_peer = (rep, other)
    diagonal_peer = (rep, diagonal)
    peer0 = (rep + 1 - 2 * b0, shard)
    peer1 = (rep + 2 - 4 * b1, shard)
    group = (core_peer, y_peer, diagonal_peer)

    barrier = pltpu.get_barrier_semaphore()
    for p in group + (peer0, peer1):
        pl.semaphore_signal(barrier, inc=1, device_id=p, device_id_type=MESH)
    pl.semaphore_wait(barrier, 5)

    owns = (in_own, fc_own, qkv_own, out_own)
    fulls = (in_full, fc_full, qkv_full, out_full)
    chunks = [(a, k) for a in range(4) for k in range(GATHER_CHUNKS[a])]
    n = len(chunks)
    ways = ((b0 + 2 * b1, b1, peer0, peer1), (b1 + 2 * b0, b0, peer1, peer0))

    def remote(src, dst, sems, index, peer):
        return pltpu.make_async_remote_copy(
            src_ref=src, dst_ref=dst, send_sem=sems[0].at[index], recv_sem=sems[1].at[index],
            device_id=peer, device_id_type=MESH)

    def place(i, h):
        a, k = chunks[i]
        own, full = owns[a], fulls[a]
        rows, cols = own.shape
        piece = rows // GATHER_CHUNKS[a] // 4
        return own, full, rows, k * 4 * piece, piece, pl.ds(h * (cols // 2), cols // 2)

    def y_copy(i, h):
        own, full, rows, start, piece, cols = place(i, h)
        at = pl.multiple_of(start + ways[h][0] * piece, 16)
        return remote(own.at[pl.ds(at, piece), cols],
                      full.at[pl.ds(pl.multiple_of(shard * rows + at, 16), piece), cols],
                      (send_sem, recv_sem), (0, i, h), y_peer)

    def first_copy(i, h):
        own, full, rows, start, piece, cols = place(i, h)
        at = pl.multiple_of(other * rows + start + ways[h][0] * piece, 16)
        ref = full.at[pl.ds(at, piece), cols]
        return remote(ref, ref, (send_sem, recv_sem), (1, i, h), ways[h][2])

    def second_copy(i, h):
        own, full, rows, start, piece, cols = place(i, h)
        at = pl.multiple_of(other * rows + start + ways[h][1] * 2 * piece, 16)
        ref = full.at[pl.ds(at, 2 * piece), cols]
        return remote(ref, ref, (send_sem, recv_sem), (2, i, h), ways[h][3])

    def core_copy(i):
        own, full, rows, start, piece, cols = place(i, 0)
        ref = full.at[pl.ds(pl.multiple_of(other * rows + start, 16), 4 * piece)]
        return remote(ref, ref, (core_send, core_recv), (i,), core_peer)

    def own_rows(a):
        rows = owns[a].shape[0]
        return fulls[a].at[pl.ds(pl.multiple_of(shard * rows, 16), rows)]

    def own_copy(a):
        return remote(owns[a], own_rows(a), (own_send, own_recv), (a,), core_peer)

    stages = (None, None, qkv_stage, out_stage)

    def local_copy(a):
        return pltpu.make_async_copy(owns[a], own_rows(a) if stages[a] is None else stages[a], local_sem.at[a])

    def stage_copy(a):
        return pltpu.make_async_copy(stages[a], own_rows(a), local_sem.at[a + 2])

    results = [(normed_ref, normed_out), (active_ref, active_out), (gh_ref, gh_out), (base_ref, base_out), (gn_ref, gn_out)]

    def store(j):
        return pltpu.make_async_copy(results[j][0], results[j][1], store_sem.at[j])

    def small_copy(j):
        return remote(small_ref, small_full.at[shard], (s_send, s_recv), (j,), group[j])

    for j in range(3):
        small_copy(j).start()
    for i in range(n):
        for h in range(2):
            y_copy(i, h).start()
    for a in range(4):
        own_copy(a).start()
        local_copy(a).start()

    def norm_all():
        small_full[shard] = small_ref[...]
        for j in range(3):
            small_copy(j).wait()
        for o in range(4):
            for r in range(8):
                bias_ref[0:1, (o * 8 + r) * 128:(o * 8 + r + 1) * 128] = small_full[o, r:r + 1, :]
            for r in range(2):
                span = slice((o * 2 + r) * 128, (o * 2 + r + 1) * 128)
                norm_ref[2:3, span] = small_full[o, 8 + r:9 + r, :]
                norm_ref[0:1, span] = small_full[o, 10 + r:11 + r, :]
                norm_ref[1:2, span] = small_full[o, 12 + r:13 + r, :]

        def rows_step(r, carry):
            at = pl.ds(pl.multiple_of(r * 64, 64), 64)
            x = tok_ref[at, :].astype(jnp.float32)
            center = x - jnp.mean(x, axis=-1, keepdims=True)
            spread = jnp.mean(center * center, axis=-1, keepdims=True)
            normed = center * lax.rsqrt(spread + EPS) * norm_ref[0:1, :] + norm_ref[1:2, :]
            normed_ref[at, :] = normed.astype(jnp.bfloat16)
            base_ref[at, :] = x + norm_ref[2:3, :]
            return carry
        lax.fori_loop(0, TOK_DEV // 64, rows_step, 0)

    def span(j):
        return pl.ds(pl.multiple_of(j * FBLK, FBLK), FBLK)

    def hidden_block(j, carry):
        at = span(j)
        hidden = jnp.dot(normed_ref[...], in_full[:, at], preferred_element_type=jnp.float32) + bias_ref[0:1, at]
        cube = hidden * hidden
        turn = jnp.tanh(GELU_C * hidden * (1.0 + GELU_A * cube))
        half = 0.5 * (1.0 + turn)
        active_ref[:, at] = (hidden * half).astype(jnp.bfloat16)
        slope = half + 0.5 * hidden * (1.0 - turn * turn) * (GELU_C * (1.0 + 3.0 * GELU_A * cube))
        gh_ref[:, at] = slope.astype(jnp.bfloat16)
        return carry

    def back_block(j, carry):
        at = span(j)
        grad = lax.dot_general(up_ref[...], fc_full[at, :], (((1,), (1,)), ((), ())), preferred_element_type=jnp.float32)
        low = (grad * gh_ref[:, at].astype(jnp.float32)).astype(jnp.bfloat16)
        gh_ref[:, at] = low
        gib_ref[0:1, at] = jnp.sum(low.astype(jnp.float32), axis=0, keepdims=True)
        return carry

    def mlp_block(j, carry):
        at = span(j)
        base_ref[:, at] = base_ref[:, at] + jnp.dot(active_ref[...], fc_full[:, at], preferred_element_type=jnp.float32)
        gn_ref[:, at] = lax.dot_general(gh_ref[...], in_full[at, :], (((1,), (1,)), ((), ())), preferred_element_type=jnp.float32)
        return carry

    def loop(block, lo, hi):
        lax.fori_loop(lo, hi, block, 0)

    work = {0: [norm_all]}
    nf = 4096 // FBLK
    lag = GATHER_LAGS
    ends = [sum(GATHER_CHUNKS[:a + 1]) - 1 + lag[3] for a in range(4)]

    def ready(a):
        own_copy(a).wait_recv()
        local_copy(a).wait()

    def plan(step, *todo):
        work.setdefault(step, []).extend(todo)

    def unstage():
        for a in (2, 3):
            local_copy(a).wait()
            stage_copy(a).start()

    bind = functools.partial
    plan(2, unstage, lambda: store(0).start())
    plan(ends[0], bind(ready, 0))
    for j in range(4):
        plan(ends[0] + j, bind(loop, hidden_block, j * nf // 4, (j + 1) * nf // 4))
    plan(ends[0] + 3, lambda: store(1).start())
    plan(ends[1], bind(ready, 1))
    for j in range(3):
        plan(ends[1] + j, bind(loop, back_block, j * nf // 4, (j + 1) * nf // 4))
    plan(ends[1] + 3, bind(loop, back_block, 3 * nf // 4, nf), lambda: store(2).start())
    nd = D // FBLK
    plan(ends[1] + 4, bind(loop, mlp_block, 0, nd // 2))
    plan(ends[1] + 5, bind(loop, mlp_block, nd // 2, nd), lambda: store(3).start(), lambda: store(4).start())

    for i in range(n + lag[3]):
        if i < n:
            for h in range(2):
                y_copy(i, h).wait_recv()
                first_copy(i, h).start()
        if 0 <= i - lag[1] < n:
            for h in range(2):
                first_copy(i - lag[1], h).wait_recv()
                second_copy(i - lag[1], h).start()
        if 0 <= i - lag[2] < n:
            for h in range(2):
                second_copy(i - lag[2], h).wait_recv()
            core_copy(i - lag[2]).start()
        if 0 <= i - lag[3] < n:
            core_copy(i - lag[3]).wait_recv()
        for todo in work.get(i, []):
            todo()
    for i in range(n):
        for h in range(2):
            y_copy(i, h).wait_send()
            first_copy(i, h).wait_send()
            second_copy(i, h).wait_send()
        core_copy(i).wait_send()
    for a in range(4):
        own_copy(a).wait_send()
    for a in (2, 3):
        own_copy(a).wait_recv()
        stage_copy(a).wait()
    for j in range(len(results)):
        store(j).wait()


def front(tokens, upstream, small, in_own, fc_own, qkv_own, out_own, shards):
    bf, f32 = jnp.bfloat16, jnp.float32
    rows = tokens.shape[0]
    ff = in_own.shape[1]
    n = sum(GATHER_CHUNKS)
    vm = pl.BlockSpec(memory_space=pltpu.VMEM)
    hbm = pl.BlockSpec(memory_space=pl.ANY)

    def full(own):
        return (own.shape[0] * shards, own.shape[1])
    held = [((rows, D), bf), ((rows, ff), bf), ((rows, ff), bf), ((rows, D), f32), ((rows, D), f32)]
    out_shape = held + [((1, ff), f32), ((8, D), f32), (full(qkv_own), bf), (full(out_own), bf)]
    dma = pltpu.SemaphoreType.DMA
    return pl.pallas_call(
        front_kernel,
        out_shape=[jax.ShapeDtypeStruct(s, d) for s, d in out_shape],
        in_specs=[vm] * 3 + [hbm] * 4,
        out_specs=[hbm] * 5 + [vm] * 2 + [hbm] * 2,
        scratch_shapes=[
            pltpu.VMEM(full(in_own), bf), pltpu.VMEM(full(fc_own), bf),
            pltpu.VMEM(qkv_own.shape, bf), pltpu.VMEM(out_own.shape, bf),
            *[pltpu.VMEM(s, d) for s, d in held],
            pltpu.VMEM((shards,) + small.shape, f32), pltpu.VMEM((1, ff), f32),
            dma((3, n, 2)), dma((3, n, 2)), dma((n,)), dma((n,)), dma((4,)), dma((4,)), dma((6,)), dma((5,)),
            dma((3,)), dma((3,)),
        ],
        compiler_params=pltpu.CompilerParams(collective_id=2, has_side_effects=True, vmem_limit_bytes=62 * 2**20),
        name="front",
    )(tokens, upstream, small, in_own, fc_own, qkv_own, out_own)


QBLK = 256


def attend_pair(q, k, v, ga, bias_ref, cos_ref, sa_ref, sb_ref, put_att, put_grad):
    f32, bf = jnp.float32, jnp.bfloat16
    nt = (((1,), (1,)), ((), ()))
    tn = (((0,), (0,)), ((), ()))
    lane = lax.broadcasted_iota(jnp.int32, (1, 128), 1)
    keep = [(lane < HEAD_DIM).astype(f32).astype(bf), (lane >= HEAD_DIM).astype(f32).astype(bf)]
    q = q * jnp.asarray(SCORE_SCALE, bf)
    attended, grad_q = [], []
    grad_k, grad_v = {}, {}
    n_blocks = TOK_DEV // QBLK

    def add(store, block, value):
        store[block] = value if block not in store else store[block] + value

    for r in range(n_blocks):
        rows = slice(r * QBLK, (r + 1) * QBLK)
        keys = (r + 1) * QBLK
        att = gq = None
        for h in range(2):
            qh = q[rows] * keep[h]
            gh = ga[rows] * keep[h]
            kh = k[:keys] * keep[h]
            vh = v[:keys] * keep[h]
            scores = lax.dot_general(qh, k[:keys], nt, preferred_element_type=f32) + bias_ref[rows, :keys]
            weight = jnp.exp(scores - jnp.max(scores, axis=-1, keepdims=True))
            soft = weight * (1.0 / jnp.sum(weight, axis=-1, keepdims=True))
            low = soft.astype(bf)
            grad_soft = lax.dot_general(gh, v[:keys], nt, preferred_element_type=f32)
            weighted = soft * grad_soft
            delta = jnp.sum(weighted, axis=-1, keepdims=True)
            grad_scores = (weighted - soft * delta).astype(bf)
            part = jnp.dot(low, vh, preferred_element_type=f32)
            att = part if att is None else att + part
            part = jnp.dot(grad_scores, kh, preferred_element_type=f32)
            gq = part if gq is None else gq + part
            gk = lax.dot_general(grad_scores, qh, tn, preferred_element_type=f32)
            gv = lax.dot_general(low, gh, tn, preferred_element_type=f32)
            for b in range(r + 1):
                span = slice(b * QBLK, (b + 1) * QBLK)
                add(grad_k, b, gk[span])
                add(grad_v, b, gv[span])
        attended.append(att)
        grad_q.append(gq)

    def unturn(x):
        x = x.astype(bf).astype(f32)
        return x * cos_ref[...] - pltpu.roll(x, 127, 1) * sa_ref[...] - pltpu.roll(x, 1, 1) * sb_ref[...]

    put_att(jnp.concatenate(attended, 0).astype(bf))
    put_grad(0, unturn(jnp.concatenate(grad_q, 0) * SCORE_SCALE).astype(bf))
    put_grad(1, unturn(jnp.concatenate([grad_k[b] for b in range(n_blocks)], 0)).astype(bf))
    put_grad(2, jnp.concatenate([grad_v[b] for b in range(n_blocks)], 0).astype(bf))


def reduce_kernel(n_rep, normed_hbm, gh_hbm, qkv_hbm, up_hbm, out_hbm, active_hbm, gn_hbm, base_hbm, tok_hbm,
                  bias_ref, cos_ref, sa_ref, sb_ref, gib_ref, norm_ref,
                  out_ref, small_out, layer_ref, grad_ref,
                  left, right, turned, qkv_full, out_full, gn_ref, base_ref, tok_ref, load_sem,
                  c_send, c_keep, c_recv, y_send, y_keep, y_recv, work, recvs, s_buf, s_recv,
                  send_sem, recv_sem, s_send_sem, s_recv_sem):
    n_chunks = out_ref.shape[0]
    rep = lax.axis_index("rep")
    shard = lax.axis_index("shard")
    y, c = shard // 2, shard % 2
    nbits = int(math.log2(n_rep))
    bits = [(rep // (1 << b)) % 2 for b in range(nbits)]

    def rep_peer(b):
        return (rep + (1 << b) * (1 - 2 * bits[b]), shard)

    core_peer = (rep, shard + 1 - 2 * c)
    y_peer = (rep, shard + 2 - 4 * y)
    halving = list(range(min(3, nbits)))
    extra = list(range(min(3, nbits), nbits))
    sizes = [BLK >> (k + 1) for k in range(len(halving))]

    def base(k):
        off = 0
        for j in range(k):
            off = off + bits[halving[j]] * sizes[j]
        return off

    loads = [
        pltpu.make_async_copy(src, dst, load_sem.at[j]) for j, (src, dst) in enumerate([
            (normed_hbm, left.at[:, 0:D]), (gh_hbm, right.at[:, 4 * D:8 * D]), (qkv_hbm, qkv_full),
            (up_hbm, right.at[:, 3 * D:4 * D]), (out_hbm, out_full), (active_hbm, left.at[:, 2 * D:6 * D]),
            (gn_hbm, gn_ref), (base_hbm, base_ref), (tok_hbm, tok_ref)])]
    for load in loads:
        load.start()

    barrier = pltpu.get_barrier_semaphore()
    peers = [core_peer, y_peer] + [rep_peer(b) for b in range(nbits)]
    for p in peers:
        pl.semaphore_signal(barrier, inc=1, device_id=p, device_id_type=MESH)
    pl.semaphore_wait(barrier, len(peers))

    def copy(src, dst, stage, slot, peer):
        return pltpu.make_async_remote_copy(
            src_ref=src, dst_ref=dst, send_sem=send_sem.at[stage, slot],
            recv_sem=recv_sem.at[stage, slot], device_id=peer, device_id_type=MESH)

    def core_copy(t):
        s = t % SLOTS
        return copy(c_send.at[s], c_recv.at[s], 0, s, core_peer)

    def y_copy(t):
        s = t % SLOTS
        return copy(y_send.at[s], y_recv.at[s], 1, s, y_peer)

    def half_copy(k, t):
        s = t % SLOTS
        rows = sizes[k]
        start = pl.multiple_of(base(k) + (1 - bits[halving[k]]) * rows, 16)
        return copy(work.at[s, pl.ds(start, rows)], recvs[k].at[s], 2 + k, s, rep_peer(halving[k]))

    last = len(halving)

    def own():
        return pl.multiple_of(base(last), 16)

    tail = BLK >> last

    def extra_copy(j, t):
        s = t % SLOTS
        return copy(work.at[s, pl.ds(own(), tail)], recvs[last + j].at[s], 2 + last + j, s, rep_peer(extra[j]))

    def gather_copy(k, t):
        s = t % SLOTS
        rows = sizes[k]
        start = pl.multiple_of(base(k) + bits[halving[k]] * rows, 16)
        ref = out_ref.at[t, pl.ds(start, rows)]
        return copy(ref, ref, 2 + last + len(extra) + k, s, rep_peer(halving[k]))

    def first_use(t, at, *which):
        @pl.when(t == at)
        def _():
            for j in which:
                loads[j].wait()

    f32, bf = jnp.float32, jnp.bfloat16
    nt = (((1,), (1,)), ((), ()))

    def block(start, j, size=256):
        return pl.ds(pl.multiple_of(start + j * size, size), size)

    def turn_rows(u):
        first_use(u, 0, 2)
        for b in range(2):
            rows = jnp.dot(left[:, 0:D], qkv_full[:, block(0, 2 * u + b)], preferred_element_type=f32)
            for g in range(2):
                part = rows[:, g * 128:(g + 1) * 128]
                part = part * cos_ref[...] + pltpu.roll(part, 127, 1) * sa_ref[...] + pltpu.roll(part, 1, 1) * sb_ref[...]
                right[:, block(0, 4 * u + 2 * b + g, 128)] = part.astype(bf)

    def value_rows(u):
        for b in range(2):
            at = block(2 * D, 2 * u + b)
            right[:, at] = jnp.dot(left[:, 0:D], qkv_full[:, at], preferred_element_type=f32).astype(bf)

    def grad_attended(u):
        first_use(u, 0, 3, 4)
        for b in range(2):
            part = lax.dot_general(right[:, 3 * D:4 * D], out_full[block(0, 2 * u + b), :], nt, preferred_element_type=f32)
            left[:, block(D, 2 * u + b)] = part.astype(bf)

    def attend(u):
        @pl.when(u % 2 == 0)
        def _():
            pair = u // 2
            spans = [block(k * D, pair, 128) for k in range(3)]
            span = block(D, pair, 128)

            def put_att(value):
                left[:, span] = value

            def put_grad(part, value):
                right[:, spans[part]] = value
            attend_pair(right[:, spans[0]], right[:, spans[1]], right[:, spans[2]], left[:, span],
                        bias_ref, cos_ref, sa_ref, sb_ref, put_att, put_grad)

    def grad_normed(u):
        first_use(u, 0, 6)
        at = block(0, u)
        gn_ref[:, at] = gn_ref[:, at] + lax.dot_general(right[:, 0:3 * D], qkv_full[at, :], nt, preferred_element_type=f32)

    def project(u):
        first_use(u, 0, 7)
        for b in range(2):
            at = block(0, 2 * u + b)
            layer_ref[:, at] = (base_ref[:, at] + jnp.dot(left[:, D:2 * D], out_full[:, at], preferred_element_type=f32)).astype(bf)

    def norm_back(u):
        first_use(u, 0, 8)

        @pl.when(u == 0)
        def _():
            s_buf[0] = jnp.zeros(s_buf.shape[1:], f32)
            s_buf[0, :, 0:4 * D] = gib_ref[...]
        at = block(0, u, 64)
        x = tok_ref[at, :].astype(f32)
        center = x - jnp.mean(x, axis=-1, keepdims=True)
        scale = lax.rsqrt(jnp.mean(center * center, axis=-1, keepdims=True) + EPS)
        unit = center * scale
        grad = gn_ref[at, :]
        upstream = right[at, 3 * D:4 * D].astype(f32)
        wide = grad * norm_ref[0:1, :]
        lean = wide - jnp.mean(wide, axis=-1, keepdims=True) - unit * jnp.mean(wide * unit, axis=-1, keepdims=True)
        grad_ref[at, :] = (lean * scale + upstream).astype(bf)
        for k, value in enumerate((upstream, grad * unit, grad)):
            span = slice((4 + k) * D, (5 + k) * D)
            s_buf[0, :, span] = s_buf[0, :, span] + jnp.sum(value, axis=0, keepdims=True)

    tasks = [(0, 4, turn_rows), (4, 2, value_rows), (6, 2, grad_attended), (8, 16, attend), (25, 4, grad_normed),
             (29, 2, project), (33, 8, norm_back)]

    def compute(t):
        s = t % SLOTS
        first_use(t, 0, 0, 1)
        first_use(t, 16, 5)
        first, stride, column, new = chunk_plan(t)

        @pl.when(new)
        def _():
            for o in range(4):
                at = pl.multiple_of(first + o * stride, BLK)
                turned[o % 2, (o // 2) * BLK:(o // 2 + 1) * BLK, :] = left[:, pl.ds(at, BLK)].T
        operand = right[:, pl.ds(pl.multiple_of(column, COL), COL)]
        for side, dst in ((1 - c, c_send), (c, c_keep)):
            part = jnp.dot(turned[side], operand, preferred_element_type=jnp.float32)
            dst[s] = part.astype(jnp.bfloat16).reshape(2, BLK, COL)
        core_copy(t).start()

    def after_core(t):
        s = t % SLOTS
        core_copy(t).wait()
        y_send[s] = c_keep[s, 1 - y] + c_recv[s, 1 - y]
        y_copy(t).start()
        y_keep[s] = c_keep[s, y] + c_recv[s, y]

    def after_y(t):
        s = t % SLOTS
        y_copy(t).wait()
        work[s] = y_keep[s] + y_recv[s]
        half_copy(0, t).start()

    def after_half(k, t):
        s = t % SLOTS
        half_copy(k, t).wait()
        rows = sizes[k]
        start = pl.multiple_of(base(k + 1), 16)
        total = work[s, pl.ds(start, rows)] + recvs[k][s]
        if k + 1 < last:
            work[s, pl.ds(start, rows)] = total
            half_copy(k + 1, t).start()
        elif extra:
            work[s, pl.ds(start, rows)] = total
            extra_copy(0, t).start()
        else:
            out_ref[t, pl.ds(start, rows)] = total
            gather_copy(last - 1, t).start()

    def after_extra(j, t):
        s = t % SLOTS
        extra_copy(j, t).wait()
        total = work[s, pl.ds(own(), tail)] + recvs[last + j][s]
        if j + 1 < len(extra):
            work[s, pl.ds(own(), tail)] = total
            extra_copy(j + 1, t).start()
        else:
            out_ref[t, pl.ds(own(), tail)] = total
            gather_copy(last - 1, t).start()

    def after_gather(k, t):
        gather_copy(k, t).wait()
        if k > 0:
            gather_copy(k - 1, t).start()

    stages = [(0, compute), (LAGS[0], after_core), (LAGS[0]+LAGS[1], after_y)]
    lag = LAGS[0]+LAGS[1]
    for k in range(last):
        lag += LAGS[2+k]
        stages.append((lag, functools.partial(after_half, k)))
    for j in range(len(extra)):
        lag += 1
        stages.append((lag, functools.partial(after_extra, j)))
    for k in reversed(range(last)):
        lag += LAGS[5+last-1-k]
        stages.append((lag, functools.partial(after_gather, k)))

    s_peers = peers

    def small_copy(j):
        return pltpu.make_async_remote_copy(
            src_ref=s_buf.at[j], dst_ref=s_recv.at[j], send_sem=s_send_sem.at[j],
            recv_sem=s_recv_sem.at[j], device_id=s_peers[j], device_id_type=MESH)

    def small_step(j):
        if j > 0:
            small_copy(j - 1).wait()
            total = s_buf[j - 1] + s_recv[j - 1]
            if j < len(s_peers):
                s_buf[j] = total
            else:
                small_out[...] = total
        if j < len(s_peers):
            small_copy(j).start()

    def step(i, carry):
        for delay, stage in reversed(stages):
            @pl.when((i >= delay) & (i < n_chunks + delay))
            def _(stage=stage, delay=delay):
                stage(i - delay)
        for start, count, task in tasks:
            @pl.when((i >= start) & (i < start + count))
            def _(start=start, task=task):
                task(i - start)
        for j in range(len(s_peers) + 1):
            @pl.when(i == 42 + j)
            def _(j=j):
                small_step(j)
        return carry

    lax.fori_loop(0, n_chunks + lag, step, 0)


def grad_reduce(stream, fixed, n_rep, n_chunks):
    nbits = int(math.log2(n_rep))
    last = min(3, nbits)
    n_extra = nbits - last
    n_stage = 2 + last + n_extra + last
    bf = jnp.bfloat16
    recv_rows = [BLK >> (k + 1) for k in range(last)] + [BLK >> last] * n_extra
    chunk = (SLOTS, BLK, COL)
    pair = (SLOTS, 2, BLK, COL)
    n_small = 2 + nbits

    def kern(*refs):
        first = refs[:n_fixed]
        reduce_kernel(n_rep, *first, refs[n_fixed:n_fixed + len(recv_rows)], *refs[n_fixed + len(recv_rows):])

    n_fixed = len(stream) + len(fixed) + 4 + 9 + 7
    tokens = stream[0].shape[0]
    small = (1, 7 * D)
    hbm = pl.BlockSpec(memory_space=pl.ANY)
    vm = pl.BlockSpec(memory_space=pltpu.VMEM)
    return pl.pallas_call(
        kern,
        out_shape=(jax.ShapeDtypeStruct((n_chunks, BLK, COL), bf), jax.ShapeDtypeStruct(small, jnp.float32),
                   jax.ShapeDtypeStruct((tokens, D), bf), jax.ShapeDtypeStruct((tokens, D), bf)),
        in_specs=[hbm] * len(stream) + [vm] * len(fixed),
        out_specs=(vm,) * 4,
        scratch_shapes=[
            pltpu.VMEM((tokens, 6 * D), bf), pltpu.VMEM((tokens, 8 * D), bf), pltpu.VMEM((2, 2 * BLK, tokens), bf),
            *[pltpu.VMEM(x.shape, x.dtype) for x in (stream[2], stream[4], stream[6], stream[7], stream[8])],
            pltpu.SemaphoreType.DMA((9,)),
            pltpu.VMEM(pair, bf), pltpu.VMEM(pair, bf), pltpu.VMEM(pair, bf),
            pltpu.VMEM(chunk, bf), pltpu.VMEM(chunk, bf), pltpu.VMEM(chunk, bf), pltpu.VMEM(chunk, bf),
            *[pltpu.VMEM((SLOTS, rows, COL), bf) for rows in recv_rows],
            pltpu.VMEM((n_small,) + small, jnp.float32), pltpu.VMEM((n_small,) + small, jnp.float32),
            pltpu.SemaphoreType.DMA((n_stage, SLOTS)), pltpu.SemaphoreType.DMA((n_stage, SLOTS)),
            pltpu.SemaphoreType.DMA((n_small,)), pltpu.SemaphoreType.DMA((n_small,)),
        ],
        compiler_params=pltpu.CompilerParams(collective_id=1, has_side_effects=True, vmem_limit_bytes=63 * 2**20),
        name="grad_reduce",
    )(*stream, *fixed)


def chunk_plan(t):
    cases = [
        ((t // 8) * BLK, D // 4, 4 * D + (t % 8) * COL, t % 8),
        (2 * D + ((t - 16) // 2) * BLK, D, 3 * D + (t % 2) * COL, t % 2),
        (((t - 32) // 6) * BLK, D // 4, ((t - 32) % 6) * COL, (t - 32) % 6),
        (D + ((t - 44) // 2) * BLK, D // 4, 3 * D + (t % 2) * COL, t % 2),
    ]
    first, stride, column, within = (
        jnp.where(t < 16, cases[0][i], jnp.where(t < 32, cases[1][i], jnp.where(t < 44, cases[2][i], cases[3][i])))
        for i in range(4))
    return first, stride, column, within == 0


def assemble(blocks, places, scale):
    def kern(in_ref, *rest):
        outs, (stage, sem) = rest[:-2], rest[-2:]
        copies = []
        for (first, rows, cols), out in zip(places, outs):
            across = cols // COL
            for i in range(rows // BLK):
                for j in range(across):
                    t = first + i * across + j
                    stage[t] = in_ref[t].astype(jnp.float32) * scale
                    copies.append(pltpu.make_async_copy(
                        stage.at[t], out.at[i * BLK:(i + 1) * BLK, j * COL:(j + 1) * COL], sem.at[t]))
                    copies[-1].start()
        for copy in copies:
            copy.wait()

    return pl.pallas_call(
        kern,
        out_shape=[jax.ShapeDtypeStruct((rows, cols), jnp.float32) for _, rows, cols in places],
        in_specs=[pl.BlockSpec(memory_space=pltpu.VMEM)],
        out_specs=[pl.BlockSpec(memory_space=pl.ANY)] * len(places),
        scratch_shapes=[pltpu.VMEM(blocks.shape, jnp.float32), pltpu.SemaphoreType.DMA((blocks.shape[0],))],
        compiler_params=pltpu.CompilerParams(vmem_limit_bytes=32 * 2**20),
        name="assemble",
    )(blocks)


def body(
    tokens,
    positions,
    lengths,
    owner,
    qkv_weight,
    out_weight,
    in_weight,
    in_bias,
    fc_weight,
    fc_bias,
    norm_gain,
    norm_bias,
    cotangent,
):
    rep_count = lax.axis_size("rep")
    shard_count = lax.axis_size("shard")
    device = lax.axis_index(("rep", "shard"))
    shard = lax.axis_index("shard")
    grad_scale = 1.0 / math.sqrt(TOK_DEV * rep_count * shard_count)
    segment, in_use = layout(lengths, owner, device)
    tables = rotary_tables(positions)
    slot_index = jnp.arange(tokens.shape[0], dtype=jnp.int32)
    allowed = (segment[:, None] == segment[None, :]) & (slot_index[None, :] <= slot_index[:, None])
    bias = jnp.where(allowed, 0.0, NEG)
    upstream = cotangent * in_use[:, None].astype(jnp.bfloat16)
    small = sum(jnp.pad(part.astype(jnp.float32), (first, 2048 - first - part.shape[0])) for first, part in (
        (0, in_bias), (1024, fc_bias), (1280, norm_gain), (1536, norm_bias))).reshape(16, 128)
    normed, active, grad_hidden, base, grad_ff, grad_in_bias, norms, qkv_full, out_full = front(
        tokens, upstream, small, in_weight, fc_weight, qkv_weight, out_weight, shard_count)
    blocks, small_sum, layer_out, input_grad = grad_reduce(
        (normed, grad_hidden, qkv_full, upstream, out_full, active, grad_ff, base, tokens),
        (bias, *tables, grad_in_bias, norms), rep_count, 48)
    small_sum = small_sum.reshape(-1) * grad_scale

    def own_part(first, size):
        return lax.dynamic_slice_in_dim(small_sum, first + shard * (size // 4), size // 4)

    grad_in, grad_fc, grad_qkv, grad_out = assemble(
        blocks, ((0, 256, 4 * D), (16, 1024, D), (32, 256, 3 * D), (44, 256, D)), grad_scale)
    return (
        layer_out,
        input_grad,
        grad_qkv,
        grad_out,
        grad_in,
        own_part(0, 4096),
        grad_fc,
        own_part(4096, D),
        own_part(4096 + D, D),
        own_part(4096 + 2 * D, D),
    )


def solution(mesh):
    in_specs = (
        P(("rep", "shard"), None),
        P(("rep", "shard")),
        P(),
        P(),
        P("shard", None),
        P("shard", None),
        P("shard", None),
        P("shard"),
        P("shard", None),
        P("shard"),
        P("shard"),
        P("shard"),
        P(("rep", "shard"), None),
    )
    out_specs = (
        P(("rep", "shard"), None),
        P(("rep", "shard"), None),
        P("shard", None),
        P("shard", None),
        P("shard", None),
        P("shard"),
        P("shard", None),
        P("shard"),
        P("shard"),
        P("shard"),
    )
    return jax.shard_map(body, mesh=mesh, in_specs=in_specs, out_specs=out_specs, check_vma=False)
```

```python
import functools
from functools import partial
import math

import jax
import jax.numpy as jnp
from jax import lax
from jax.experimental import pallas as pl
from jax.experimental.pallas import tpu as pltpu
from jax.sharding import PartitionSpec as P

D = 1024
HEADS = 16
HEAD_DIM = 64
ROT_DIM = 32
TOK_DEV = 512

MESH = pl.DeviceIdType.MESH
BLK = 128
COL = 512
SLOTS = 8
LAGS = (1, 2, 2, 2, 2, 2, 2, 2)
TURN = 0
EARLY = 6

EPS = 1e-05
NEG = -1000000000.0
GELU_C = math.sqrt(2.0 / math.pi)
GELU_A = 0.044715
GATHER_LAGS = (0, 2, 4, 5)
SCORE_SCALE = 0.125


def spans_of(lengths_ref, owner_ref, device):
    mine = jnp.where(owner_ref[...] == device, lengths_ref[...], 0).astype(jnp.float32)
    even = lax.broadcasted_iota(jnp.int32, mine.shape, 1) % 2 == 0
    first = jnp.sum(jnp.where(even, mine, 0.0), axis=1, keepdims=True)
    return first.astype(jnp.int32), jnp.sum(mine, axis=1, keepdims=True).astype(jnp.int32)


GATHER_CHUNKS = (4, 4, 4, 1)
GATHER_PAIRS = (0, 6, 11, 12)
FBLK = 256


def front_steps(shards, small_ref, lengths_ref, owner_ref, tok_hbm, cot_hbm, owns, fulls,
                normed_ref, active_ref, gh_ref, up_ref, base_ref, gn_ref, tok_ref, gib_ref, norm_ref, small_full, bias_ref,
                send_sem, recv_sem, core_send, core_recv, own_send, own_recv, local_sem, s_send, s_recv):
    in_full, fc_full = fulls[:2]
    rep = lax.axis_index("rep")
    shard = lax.axis_index("shard")
    y, c = shard // 2, shard % 2
    b0, b1 = rep % 2, (rep // 2) % 2
    core_shard = 2 * y + 1 - c
    other = 2 * (1 - y) + c
    diagonal = 2 * (1 - y) + 1 - c
    core_peer = (rep, core_shard)
    y_peer = (rep, other)
    diagonal_peer = (rep, diagonal)
    peer0 = (rep + 1 - 2 * b0, shard)
    peer1 = (rep + 2 - 4 * b1, shard)
    group = (core_peer, y_peer, diagonal_peer)

    loads = [pltpu.make_async_copy(src, dst, local_sem.at[4 + j]) for j, (src, dst) in enumerate(((tok_hbm, tok_ref), (cot_hbm, up_ref)))]
    chunks = [(a, k) for a in range(4) for k in range(GATHER_CHUNKS[a])]
    n = len(chunks)
    ways = ((b0 + 2 * b1, b1, peer0, peer1), (b1 + 2 * b0, b0, peer1, peer0))

    def remote(src, dst, sems, index, peer):
        return pltpu.make_async_remote_copy(
            src_ref=src, dst_ref=dst, send_sem=sems[0].at[index], recv_sem=sems[1].at[index],
            device_id=peer, device_id_type=MESH)

    def place(i, h):
        a, k = chunks[i]
        own, full = owns[a], fulls[a]
        rows, cols = own.shape
        piece = rows // GATHER_CHUNKS[a] // 4
        return own, full, rows, k * 4 * piece, piece, pl.ds(h * (cols // 2), cols // 2)

    def held(i, h, piece):
        if i in GATHER_PAIRS:
            return (b0, b1)[h] * 2 * piece, 2 * piece
        return ways[h][0] * piece, piece

    def y_copy(i, h):
        own, full, rows, start, piece, cols = place(i, h)
        off, piece = held(i, h, piece)
        at = pl.multiple_of(start + off, 16)
        return remote(own.at[pl.ds(at, piece), cols],
                      full.at[pl.ds(pl.multiple_of(shard * rows + at, 16), piece), cols],
                      (send_sem, recv_sem), (0, i, h), y_peer)

    def first_copy(i, h):
        own, full, rows, start, piece, cols = place(i, h)
        off, piece = held(i, h, piece)
        at = pl.multiple_of(other * rows + start + off, 16)
        ref = full.at[pl.ds(at, piece), cols]
        return remote(ref, ref, (send_sem, recv_sem), (1, i, h), ways[h][2])

    def second_copy(i, h):
        own, full, rows, start, piece, cols = place(i, h)
        at = pl.multiple_of(other * rows + start + ways[h][1] * 2 * piece, 16)
        ref = full.at[pl.ds(at, 2 * piece), cols]
        return remote(ref, ref, (send_sem, recv_sem), (2, i, h), ways[h][3])

    def core_copy(i):
        own, full, rows, start, piece, cols = place(i, 0)
        ref = full.at[pl.ds(pl.multiple_of(other * rows + start, 16), 4 * piece)]
        return remote(ref, ref, (core_send, core_recv), (i,), core_peer)

    def own_rows(a):
        rows = owns[a].shape[0]
        return fulls[a].at[pl.ds(pl.multiple_of(shard * rows, 16), rows)]

    def own_copy(a):
        return remote(owns[a], own_rows(a), (own_send, own_recv), (a,), core_peer)

    def local_copy(a):
        return pltpu.make_async_copy(owns[a], own_rows(a), local_sem.at[a])

    def small_copy(j):
        return remote(small_ref, small_full.at[shard], (s_send, s_recv), (j,), group[j])

    def begin():
        for load in loads:
            load.start()
        for j in range(3):
            small_copy(j).start()
        for i in range(n):
            for h in range(2):
                y_copy(i, h).start()
        for a in range(4):
            own_copy(a).start()
            local_copy(a).start()

    def norm_all():
        small_full[shard] = small_ref[...]
        for j in range(3):
            small_copy(j).wait()
        for o in range(4):
            for r in range(8):
                bias_ref[0:1, (o * 8 + r) * 128:(o * 8 + r + 1) * 128] = small_full[o, r:r + 1, :]
            for r in range(2):
                span = slice((o * 2 + r) * 128, (o * 2 + r + 1) * 128)
                norm_ref[2:3, span] = small_full[o, 8 + r:9 + r, :]
                norm_ref[0:1, span] = small_full[o, 10 + r:11 + r, :]
                norm_ref[1:2, span] = small_full[o, 12 + r:13 + r, :]
        for load in loads:
            load.wait()

    def norm_rows(r, carry):
        at = pl.ds(pl.multiple_of(r * 64, 64), 64)
        x = tok_ref[at, :].astype(jnp.float32)
        center = x - jnp.mean(x, axis=-1, keepdims=True)
        spread = jnp.mean(center * center, axis=-1, keepdims=True)
        normed = center * lax.rsqrt(spread + EPS) * norm_ref[0:1, :] + norm_ref[1:2, :]
        normed_ref[at, :] = normed.astype(jnp.bfloat16)
        base_ref[at, :] = x + norm_ref[2:3, :]
        slot = lax.broadcasted_iota(jnp.int32, (64, 1), 0) + r * 64
        _, used = spans_of(lengths_ref, owner_ref, rep * shards + shard)
        up_ref[at, :] = jnp.where(slot < used, up_ref[at, :].astype(jnp.float32), 0.0).astype(jnp.bfloat16)
        return carry

    def span(j):
        return pl.ds(pl.multiple_of(j * FBLK, FBLK), FBLK)

    def hidden_block(j, carry):
        at = span(j)
        hidden = jnp.dot(normed_ref[...], in_full[:, at], preferred_element_type=jnp.float32) + bias_ref[0:1, at]
        cube = hidden * hidden
        turn = jnp.tanh(GELU_C * hidden * (1.0 + GELU_A * cube))
        half = 0.5 * (1.0 + turn)
        active_ref[:, at] = (hidden * half).astype(jnp.bfloat16)
        slope = half + 0.5 * hidden * (1.0 - turn * turn) * (GELU_C * (1.0 + 3.0 * GELU_A * cube))
        gh_ref[:, at] = slope.astype(jnp.bfloat16)
        return carry

    def back_block(j, carry):
        at = span(j)
        grad = lax.dot_general(up_ref[...], fc_full[at, :], (((1,), (1,)), ((), ())), preferred_element_type=jnp.float32)
        low = (grad * gh_ref[:, at].astype(jnp.float32)).astype(jnp.bfloat16)
        gh_ref[:, at] = low
        gib_ref[0:1, at] = jnp.sum(low.astype(jnp.float32), axis=0, keepdims=True)
        return carry

    def mlp_block(j, carry):
        at = span(j)
        base_ref[:, at] = base_ref[:, at] + jnp.dot(active_ref[...], fc_full[:, at], preferred_element_type=jnp.float32)
        return carry

    def grad_block(j, carry):
        at = span(j)
        gn_ref[:, at] = lax.dot_general(gh_ref[...], in_full[at, :], (((1,), (1,)), ((), ())), preferred_element_type=jnp.float32)
        return carry

    def loop(block, lo, hi):
        lax.fori_loop(lo, hi, block, 0)

    work = {1: [norm_all]}
    nf = 4096 // FBLK
    lag = GATHER_LAGS
    ends = [sum(GATHER_CHUNKS[:a + 1]) - 1 + lag[3] for a in range(4)]

    def ready(a):
        own_copy(a).wait_recv()
        local_copy(a).wait()

    def plan(step, *todo):
        work.setdefault(step, []).extend(todo)

    bind = functools.partial
    nd = D // FBLK
    for j in range(4):
        plan(1 + j, bind(loop, norm_rows, 2 * j, 2 * j + 2))
    plan(ends[0], bind(ready, 0))
    for j in range(4):
        plan(ends[0] + j, bind(loop, hidden_block, j * nf // 4, (j + 1) * nf // 4))
    plan(ends[1], bind(ready, 1))
    for j in range(2):
        plan(ends[1] + j, bind(loop, back_block, j * nf // 2, (j + 1) * nf // 2))
    for j in range(2):
        plan(ends[1] + 2 + j, bind(loop, grad_block, j * nd // 2, (j + 1) * nd // 2))
    for j in range(2):
        plan(ends[1] + 4 + j, bind(loop, mlp_block, j * nd // 2, (j + 1) * nd // 2))

    def step(i):
        if i < n:
            for h in range(2):
                y_copy(i, h).wait_recv()
                first_copy(i, h).start()
        if 0 <= i - lag[1] < n:
            for h in range(2):
                first_copy(i - lag[1], h).wait_recv()
                if i - lag[1] not in GATHER_PAIRS:
                    second_copy(i - lag[1], h).start()
            if i - lag[1] in GATHER_PAIRS:
                core_copy(i - lag[1]).start()
        if 0 <= i - lag[2] < n and i - lag[2] not in GATHER_PAIRS:
            for h in range(2):
                second_copy(i - lag[2], h).wait_recv()
            core_copy(i - lag[2]).start()
        if 0 <= i - lag[3] < n:
            core_copy(i - lag[3]).wait_recv()
        for todo in work.get(i, []):
            todo()

    def finish():
        ready(2)
        ready(3)
        for i in range(n):
            for h in range(2):
                y_copy(i, h).wait_send()
                first_copy(i, h).wait_send()
                if i not in GATHER_PAIRS:
                    second_copy(i, h).wait_send()
            core_copy(i).wait_send()
        for a in range(4):
            own_copy(a).wait_send()

    return begin, n + lag[3], ends[0] + 4, step, finish


QBLK = 256


def attend_pair(q, k, v, ga, bias_ref, cos_ref, sa_ref, sb_ref, put_att, put_grad):
    f32, bf = jnp.float32, jnp.bfloat16
    nt = (((1,), (1,)), ((), ()))
    tn = (((0,), (0,)), ((), ()))
    lane = lax.broadcasted_iota(jnp.int32, (1, 128), 1)
    keep = [(lane < HEAD_DIM).astype(f32).astype(bf), (lane >= HEAD_DIM).astype(f32).astype(bf)]
    q = q * jnp.asarray(SCORE_SCALE, bf)
    attended, grad_q = [], []
    grad_k, grad_v = {}, {}
    n_blocks = TOK_DEV // QBLK

    def add(store, block, value):
        store[block] = value if block not in store else store[block] + value

    for r in range(n_blocks):
        rows = slice(r * QBLK, (r + 1) * QBLK)
        keys = (r + 1) * QBLK
        att = gq = None
        for h in range(2):
            qh = q[rows] * keep[h]
            gh = ga[rows] * keep[h]
            kh = k[:keys] * keep[h]
            vh = v[:keys] * keep[h]
            scores = lax.dot_general(qh, k[:keys], nt, preferred_element_type=f32) + bias_ref[rows, :keys]
            weight = jnp.exp(scores - jnp.max(scores, axis=-1, keepdims=True))
            soft = weight * (1.0 / jnp.sum(weight, axis=-1, keepdims=True))
            low = soft.astype(bf)
            grad_soft = lax.dot_general(gh, v[:keys], nt, preferred_element_type=f32)
            weighted = soft * grad_soft
            delta = jnp.sum(weighted, axis=-1, keepdims=True)
            grad_scores = (weighted - soft * delta).astype(bf)
            part = jnp.dot(low, vh, preferred_element_type=f32)
            att = part if att is None else att + part
            part = jnp.dot(grad_scores, kh, preferred_element_type=f32)
            gq = part if gq is None else gq + part
            gk = lax.dot_general(grad_scores, qh, tn, preferred_element_type=f32)
            gv = lax.dot_general(low, gh, tn, preferred_element_type=f32)
            for b in range(r + 1):
                span = slice(b * QBLK, (b + 1) * QBLK)
                add(grad_k, b, gk[span])
                add(grad_v, b, gv[span])
        attended.append(att)
        grad_q.append(gq)

    def unturn(x):
        x = x.astype(bf).astype(f32)
        return x * cos_ref[...] - pltpu.roll(x, 127, 1) * sa_ref[...] - pltpu.roll(x, 1, 1) * sb_ref[...]

    put_att(jnp.concatenate(attended, 0).astype(bf))
    put_grad(0, unturn(jnp.concatenate(grad_q, 0) * SCORE_SCALE).astype(bf))
    put_grad(1, unturn(jnp.concatenate([grad_k[b] for b in range(n_blocks)], 0)).astype(bf))
    put_grad(2, jnp.concatenate([grad_v[b] for b in range(n_blocks)], 0).astype(bf))


def reduce_steps(n_rep, n_chunks, lengths_ref, owner_ref, pos_ref, norm_ref, out_hbm_blocks, small_out, layer_ref, grad_ref,
                 left, right, turned, qkv_full, out_full, gn_ref, base_ref, tok_ref, held_ref,
                 bias_ref, cos_ref, sa_ref, sb_ref, store_sem, c_send, c_keep, c_recv, acc, y_recv, recvs, s_buf, s_recv,
                 send_sem, recv_sem, s_send_sem, s_recv_sem):
    rep = lax.axis_index("rep")
    shard = lax.axis_index("shard")
    y, c = shard // 2, shard % 2
    nbits = int(math.log2(n_rep))
    bits = [(rep // (1 << b)) % 2 for b in range(nbits)]

    def rep_peer(b):
        return (rep + (1 << b) * (1 - 2 * bits[b]), shard)

    core_peer = (rep, shard + 1 - 2 * c)
    y_peer = (rep, shard + 2 - 4 * y)
    last = 3
    extra = list(range(last, nbits))
    half = BLK // 2

    def way(t):
        return (t % TURN) // (TURN - 1) if TURN else 0

    def pick(d, zero, one):
        return zero + d * (one - zero)

    def bit_of(k, d):
        return bits[2] if k == 2 else pick(d, bits[k], bits[1 - k])

    def bit_peer(k, d):
        return rep_peer(2) if k == 2 else (pick(d, rep_peer(k)[0], rep_peer(1 - k)[0]), shard)

    def base(k, d):
        off = 0
        for j in range(k):
            off = off + bit_of(j, d) * (half >> j)
        return off

    peers = [core_peer, y_peer] + [rep_peer(b) for b in range(nbits)]

    def copy(src, dst, stage, slot, peer):
        return pltpu.make_async_remote_copy(
            src_ref=src, dst_ref=dst, send_sem=send_sem.at[stage, slot],
            recv_sem=recv_sem.at[stage, slot], device_id=peer, device_id_type=MESH)

    def core_copy(t):
        s = t % SLOTS
        return copy(c_send.at[s], c_recv.at[s], 0, s, core_peer)

    def first_copy(t, d):
        s = t % SLOTS
        if d:
            return copy(acc.at[s, :, 1 - bits[1]], y_recv.at[s], 1, s, rep_peer(1))
        return copy(acc.at[s, 1 - y], y_recv.at[s], 1, s, y_peer)

    def second_copy(t):
        s, d = t % SLOTS, way(t)
        src = acc.at[s, pick(d, y, 1 - y), pick(d, 1 - bits[0], bits[1])]
        peer = (pick(d, rep_peer(0)[0], rep), pick(d, shard, y_peer[1]))
        return copy(src, recvs[0].at[s], 2, s, peer)

    def rows_copy(k, t):
        s, d = t % SLOTS, way(t)
        rows = half >> k
        start = pl.multiple_of(base(k + 1, d) - bit_of(0, d) * half + (1 - 2 * bit_of(k, d)) * rows, 16)
        return copy(acc.at[s, y, bit_of(0, d), pl.ds(start, rows)], recvs[k].at[s], 2 + k, s, bit_peer(k, d))

    def own(t):
        return pl.multiple_of(base(last, way(t)), 16)

    def own_acc(t, k=last):
        d = way(t)
        return t % SLOTS, y, bit_of(0, d), pl.ds(pl.multiple_of(base(k, d) - bit_of(0, d) * half, 16), half >> (k - 1))

    tail = BLK >> last

    def extra_copy(j, t):
        s = t % SLOTS
        return copy(acc.at[own_acc(t)], recvs[last + j].at[s], 2 + last + j, s, rep_peer(extra[j]))

    across = held_ref.shape[1] // COL

    def held(t, start, rows):
        at = pl.multiple_of(t // across * BLK + start, 16)
        return held_ref.at[pl.ds(at, rows), pl.ds(pl.multiple_of(t % across * COL, COL), COL)]

    def gather_copy(k, t):
        s, d = t % SLOTS, way(t)
        ref = held(t, base(k + 1, d), half >> k)
        return copy(ref, ref, 2 + last + len(extra) + k, s, bit_peer(k, d))

    f32, bf = jnp.float32, jnp.bfloat16
    nt = (((1,), (1,)), ((), ()))

    def block(start, j, size=256):
        return pl.ds(pl.multiple_of(start + j * size, size), size)

    def tables(u):
        first, used = spans_of(lengths_ref, owner_ref, rep * lax.axis_size("shard") + shard)
        lane = lax.broadcasted_iota(jnp.int32, (128, 128), 1)
        even = lane % 2 == 0
        lane = lane % HEAD_DIM
        inverse = jnp.exp((lane // 2).astype(f32) * (-2.0 * math.log(10000.0) / ROT_DIM))
        inverse = jnp.where(lane < ROT_DIM, inverse, 0.0)
        key = lax.broadcasted_iota(jnp.int32, (128, TOK_DEV), 1)
        for g in range(TOK_DEV // 128):
            rows = slice(g * 128, (g + 1) * 128)
            query = lax.broadcasted_iota(jnp.int32, (128, TOK_DEV), 0) + g * 128
            same = (query < used) & ((query < first) == (key < first))
            bias_ref[rows, :] = jnp.where((key == query) | ((key < query) & same), 0.0, NEG)
            place = jnp.broadcast_to(pos_ref[g:g + 1, :].astype(f32), (128, 128)).T
            angles = place * inverse
            sine = jnp.sin(angles)
            cos_ref[rows, :] = jnp.cos(angles)
            sa_ref[rows, :] = jnp.where(even, -sine, 0.0)
            sb_ref[rows, :] = jnp.where(even, 0.0, sine)

    def turn_rows(u):
        for b in range(2):
            rows = jnp.dot(left[:, 0:D], qkv_full[:, block(0, 2 * u + b)], preferred_element_type=f32)
            for g in range(2):
                part = rows[:, g * 128:(g + 1) * 128]
                part = part * cos_ref[...] + pltpu.roll(part, 127, 1) * sa_ref[...] + pltpu.roll(part, 1, 1) * sb_ref[...]
                right[:, block(0, 4 * u + 2 * b + g, 128)] = part.astype(bf)

    def value_rows(u):
        for b in range(2):
            at = block(2 * D, 2 * u + b)
            right[:, at] = jnp.dot(left[:, 0:D], qkv_full[:, at], preferred_element_type=f32).astype(bf)

    def grad_attended(u):
        for b in range(2):
            part = lax.dot_general(right[:, 3 * D:4 * D], out_full[block(0, 2 * u + b), :], nt, preferred_element_type=f32)
            left[:, block(D, 2 * u + b)] = part.astype(bf)

    def attend(u):
        @pl.when(u % 2 == 0)
        def _():
            pair = u // 2
            spans = [block(k * D, pair, 128) for k in range(3)]
            span = block(D, pair, 128)

            def put_att(value):
                left[:, span] = value

            def put_grad(part, value):
                right[:, spans[part]] = value
            attend_pair(right[:, spans[0]], right[:, spans[1]], right[:, spans[2]], left[:, span],
                        bias_ref, cos_ref, sa_ref, sb_ref, put_att, put_grad)

    def grad_normed(u):
        at = block(0, u)
        gn_ref[:, at] = gn_ref[:, at] + lax.dot_general(right[:, 0:3 * D], qkv_full[at, :], nt, preferred_element_type=f32)

    def project(u):
        for b in range(2):
            at = block(0, 2 * u + b)
            layer_ref[:, at] = (base_ref[:, at] + jnp.dot(left[:, D:2 * D], out_full[:, at], preferred_element_type=f32)).astype(bf)

    def norm_back(u):
        @pl.when(u == 0)
        def _():
            s_buf[0, :, 4 * D:] = jnp.zeros((1, 3 * D), f32)
        at = block(0, u, 64)
        x = tok_ref[at, :].astype(f32)
        center = x - jnp.mean(x, axis=-1, keepdims=True)
        scale = lax.rsqrt(jnp.mean(center * center, axis=-1, keepdims=True) + EPS)
        unit = center * scale
        grad = gn_ref[at, :]
        upstream = right[at, 3 * D:4 * D].astype(f32)
        wide = grad * norm_ref[0:1, :]
        lean = wide - jnp.mean(wide, axis=-1, keepdims=True) - unit * jnp.mean(wide * unit, axis=-1, keepdims=True)
        grad_ref[at, :] = (lean * scale + upstream).astype(bf)
        for k, value in enumerate((upstream, grad * unit, grad)):
            span = slice((4 + k) * D, (5 + k) * D)
            s_buf[0, :, span] = s_buf[0, :, span] + jnp.sum(value, axis=0, keepdims=True)

    tasks = [(6, 1, tables), (7, 4, turn_rows), (11, 2, value_rows), (13, 2, grad_attended), (15, 16, attend),
             (32, 4, grad_normed), (36, 2, project), (38, 8, norm_back)]

    def store(t):
        return pltpu.make_async_copy(held(t, 0, BLK), out_hbm_blocks.at[t], store_sem.at[t % 4])

    def compute(t):
        s = t % SLOTS
        first, stride, column, new = chunk_plan(t)

        @pl.when(new)
        def _():
            for o in range(4):
                at = pl.multiple_of(first + o * stride, BLK)
                turned[o % 2, (o // 2) * BLK:(o // 2 + 1) * BLK, :] = left[:, pl.ds(at, BLK)].T
        operand = right[:, pl.ds(pl.multiple_of(column, COL), COL)]
        for side, dst in ((1 - c, c_send), (c, c_keep)):
            part = jnp.dot(turned[side], operand, preferred_element_type=jnp.float32)
            dst[s] = part.astype(jnp.bfloat16).reshape(2, 2, half, COL)
        core_copy(t).start()

    def each_way(t, body):
        for d in range(2 if TURN else 1):
            @pl.when(way(t) == d)
            def _(d=d):
                body(d)

    def after_core(t):
        s = t % SLOTS
        core_copy(t).wait()

        def total(d):
            for own_half in range(2):
                if d:
                    at = (s, slice(None), bits[1] if own_half else 1 - bits[1])
                else:
                    at = (s, y if own_half else 1 - y)
                acc[at] = c_keep[at] + c_recv[at]
                if not own_half:
                    first_copy(t, d).start()
        each_way(t, total)

    def after_first(t):
        s = t % SLOTS

        def total(d):
            first_copy(t, d).wait()
            at = (s, slice(None), bits[1]) if d else (s, y)
            acc[at] = acc[at] + y_recv[s]
        each_way(t, total)
        second_copy(t).start()

    def after_rows(k, t):
        s = t % SLOTS
        (second_copy(t) if k == 0 else rows_copy(k, t)).wait()
        at = own_acc(t, k + 1)
        total = acc[at] + recvs[k][s]
        if k + 1 < last:
            acc[at] = total
            rows_copy(k + 1, t).start()
        elif extra:
            acc[at] = total
            extra_copy(0, t).start()
        else:
            held(t, base(last, way(t)), tail)[...] = total
            gather_copy(last - 1, t).start()

    def after_extra(j, t):
        s = t % SLOTS
        extra_copy(j, t).wait()
        total = acc[own_acc(t)] + recvs[last + j][s]
        if j + 1 < len(extra):
            acc[own_acc(t)] = total
            extra_copy(j + 1, t).start()
        else:
            held(t, base(last, way(t)), tail)[...] = total
            gather_copy(last - 1, t).start()

    def after_gather(k, t):
        gather_copy(k, t).wait()
        if k > 0:
            gather_copy(k - 1, t).start()
        else:
            @pl.when(t >= 4)
            def _():
                store(t - 4).wait()
            store(t).start()

    stages = [(0, compute), (LAGS[0], after_core), (LAGS[0]+LAGS[1], after_first)]
    lag = LAGS[0]+LAGS[1]
    for k in range(last):
        lag += LAGS[2+k]
        stages.append((lag, functools.partial(after_rows, k)))
    for j in range(len(extra)):
        lag += 1
        stages.append((lag, functools.partial(after_extra, j)))
    for k in reversed(range(last)):
        lag += LAGS[5+last-1-k]
        stages.append((lag, functools.partial(after_gather, k)))

    s_peers = peers

    def small_copy(j):
        return pltpu.make_async_remote_copy(
            src_ref=s_buf.at[j], dst_ref=s_recv.at[j], send_sem=s_send_sem.at[j],
            recv_sem=s_recv_sem.at[j], device_id=s_peers[j], device_id_type=MESH)

    def small_step(j):
        if j > 0:
            small_copy(j - 1).wait()
            total = s_buf[j - 1] + s_recv[j - 1]
            if j < len(s_peers):
                s_buf[j] = total
            else:
                small_out[...] = total
        if j < len(s_peers):
            small_copy(j).start()

    def step(i, carry):
        for delay, stage in reversed(stages):
            @pl.when((i >= delay) & (i < n_chunks + delay))
            def _(stage=stage, delay=delay):
                stage(i - delay)
        for start, count, task in tasks:
            @pl.when((i >= start) & (i < start + count))
            def _(start=start, task=task):
                task(i - start)
        for j in range(len(s_peers) + 1):
            @pl.when(i == 47 + j)
            def _(j=j):
                small_step(j)
        return carry

    def finish():
        for t in range(n_chunks - 4, n_chunks):
            store(t).wait()
    return n_chunks + lag, step, finish


def block_kernel(shards, n_rep, n_chunks, n_recvs, small_ref, lengths_ref, owner_ref, pos_ref, tok_hbm, cot_hbm,
                 in_own, fc_own, qkv_own, out_own, blocks_hbm, small_out, layer_ref, grad_ref,
                 in_full, fc_full, qkv_full, out_full, left, right, turned, gn_ref, base_ref, tok_ref,
                 small_full, ff_bias, norm_ref, bias_ref, cos_ref, sa_ref, sb_ref, s_buf, s_recv,
                 c_send, c_keep, c_recv, acc, y_recv, *rest):
    recvs, sems = rest[:n_recvs], rest[n_recvs:]
    rep = lax.axis_index("rep")
    shard = lax.axis_index("shard")
    barrier = pltpu.get_barrier_semaphore()
    peers = [(rep, 4 * (shard // 4) + (shard + k) % 4) for k in range(1, 4)]
    b = 1
    while b < n_rep:
        peers.append((rep + b * (1 - 2 * ((rep // b) % 2)), shard))
        b *= 2
    for p in peers:
        pl.semaphore_signal(barrier, inc=1, device_id=p, device_id_type=MESH)
    pl.semaphore_wait(barrier, len(peers))

    begin, gather_steps, free_from, gather_step, gather_finish = front_steps(
        shards, small_ref, lengths_ref, owner_ref, tok_hbm, cot_hbm,
        (in_own, fc_own, qkv_own, out_own), (in_full, fc_full, qkv_full, out_full),
        left.at[:, 0:D], left.at[:, 2 * D:6 * D], right.at[:, 4 * D:8 * D], right.at[:, 3 * D:4 * D],
        base_ref, gn_ref, tok_ref, s_buf.at[0], norm_ref, small_full, ff_bias, *sems[:9])
    total, step, finish = reduce_steps(
        n_rep, n_chunks, lengths_ref, owner_ref, pos_ref, norm_ref, blocks_hbm, small_out, layer_ref, grad_ref,
        left, right, turned, qkv_full, out_full, gn_ref, base_ref, tok_ref, in_full,
        bias_ref, cos_ref, sa_ref, sb_ref, sems[9], c_send, c_keep, c_recv, acc, y_recv, recvs, s_buf, s_recv, *sems[10:])
    begin()
    early = 0
    for i in range(gather_steps):
        gather_step(i)
        while i >= free_from and early < min(EARLY, (i - free_from + 1) * EARLY // (gather_steps - free_from)):
            step(early, 0)
            early += 1
    gather_finish()
    lax.fori_loop(early, total, step, 0)
    finish()


def block(small, lengths, owner, positions, tokens, cotangent, in_own, fc_own, qkv_own, out_own, n_rep, shards, n_chunks):
    nbits = int(math.log2(n_rep))
    last = 3
    n_extra = nbits - last
    n_stage = 2 + last + n_extra + last
    bf, f32 = jnp.bfloat16, jnp.float32
    rows = tokens.shape[0]
    ff = in_own.shape[1]
    n = sum(GATHER_CHUNKS)
    recv_rows = [BLK >> (k + 1) for k in range(last)] + [BLK >> last] * n_extra
    chunk = (SLOTS, 2, BLK // 2, COL)
    pair = (SLOTS, 2, 2, BLK // 2, COL)
    n_small = 2 + nbits
    sums = (1, 3 * D + ff)
    hbm = pl.BlockSpec(memory_space=pl.ANY)
    vm = pl.BlockSpec(memory_space=pltpu.VMEM)
    dma = pltpu.SemaphoreType.DMA

    def full(own):
        return pltpu.VMEM((own.shape[0] * shards, own.shape[1]), bf)
    return pl.pallas_call(
        functools.partial(block_kernel, shards, n_rep, n_chunks, len(recv_rows)),
        out_shape=(jax.ShapeDtypeStruct((n_chunks, BLK, COL), bf), jax.ShapeDtypeStruct(sums, f32),
                   jax.ShapeDtypeStruct((rows, D), bf), jax.ShapeDtypeStruct((rows, D), bf)),
        in_specs=[vm] * 4 + [hbm] * 6,
        out_specs=(hbm,) + (vm,) * 3,
        scratch_shapes=[
            full(in_own), full(fc_own), full(qkv_own), full(out_own),
            pltpu.VMEM((rows, 2 * D + ff), bf), pltpu.VMEM((rows, 4 * D + ff), bf), pltpu.VMEM((2, 2 * BLK, rows), bf),
            pltpu.VMEM((rows, D), f32), pltpu.VMEM((rows, D), f32), pltpu.VMEM((rows, D), bf),
            pltpu.VMEM((shards,) + small.shape, f32), pltpu.VMEM((1, ff), f32), pltpu.VMEM((8, D), f32),
            pltpu.VMEM((rows, rows), f32), *[pltpu.VMEM((rows, 128), f32)] * 3,
            pltpu.VMEM((n_small,) + sums, f32), pltpu.VMEM((n_small,) + sums, f32),
            pltpu.VMEM(pair, bf), pltpu.VMEM(pair, bf), pltpu.VMEM(pair, bf), pltpu.VMEM(pair, bf), pltpu.VMEM(chunk, bf),
            *[pltpu.VMEM((SLOTS, r, COL), bf) for r in recv_rows],
            dma((3, n, 2)), dma((3, n, 2)), dma((n,)), dma((n,)), dma((4,)), dma((4,)), dma((6,)), dma((3,)), dma((3,)),
            dma((4,)), dma((n_stage, SLOTS)), dma((n_stage, SLOTS)), dma((n_small,)), dma((n_small,)),
        ],
        compiler_params=pltpu.CompilerParams(collective_id=1, has_side_effects=True, vmem_limit_bytes=67043328),
        name="block",
    )(small, lengths, owner, positions, tokens, cotangent, in_own, fc_own, qkv_own, out_own)


def chunk_plan(t):
    cases = [
        (2 * D + (t // 2) * BLK, D, 3 * D + (t % 2) * COL, t % 2),
        (((t - 16) // 8) * BLK, D // 4, 4 * D + (t % 8) * COL, t % 8),
        (((t - 32) // 6) * BLK, D // 4, ((t - 32) % 6) * COL, (t - 32) % 6),
        (D + ((t - 44) // 2) * BLK, D // 4, 3 * D + (t % 2) * COL, t % 2),
    ]
    first, stride, column, within = (
        jnp.where(t < 16, cases[0][i], jnp.where(t < 32, cases[1][i], jnp.where(t < 44, cases[2][i], cases[3][i])))
        for i in range(4))
    return first, stride, column, within == 0


def assemble(blocks, places, scale):
    def kern(in_hbm, *rest):
        outs, (in_ref, stage, load_sem, sem) = rest[:-4], rest[-4:]
        copies = []
        part = 4

        def load(g):
            at = pl.ds(g * part, part)
            return pltpu.make_async_copy(in_hbm.at[at], in_ref.at[at], load_sem.at[g])
        for g in range(blocks.shape[0] // part):
            load(g).start()
        for (first, rows, cols), out in zip(places, outs):
            across = cols // COL
            for i in range(rows // BLK):
                for j in range(across):
                    t = first + i * across + j
                    if t % part == 0:
                        load(t // part).wait()
                    stage[t] = in_ref[t].astype(jnp.float32) * scale
                    copies.append(pltpu.make_async_copy(
                        stage.at[t], out.at[i * BLK:(i + 1) * BLK, j * COL:(j + 1) * COL], sem.at[t]))
                    copies[-1].start()
        for copy in copies:
            copy.wait()

    return pl.pallas_call(
        kern,
        out_shape=[jax.ShapeDtypeStruct((rows, cols), jnp.float32) for _, rows, cols in places],
        in_specs=[pl.BlockSpec(memory_space=pl.ANY)],
        out_specs=[pl.BlockSpec(memory_space=pl.ANY)] * len(places),
        scratch_shapes=[pltpu.VMEM(blocks.shape, blocks.dtype), pltpu.VMEM(blocks.shape, jnp.float32),
                        pltpu.SemaphoreType.DMA((blocks.shape[0] // 4,)), pltpu.SemaphoreType.DMA((blocks.shape[0],))],
        compiler_params=pltpu.CompilerParams(vmem_limit_bytes=63 * 2**20),
        name="assemble",
    )(blocks)


def body(
    tokens,
    positions,
    lengths,
    owner,
    qkv_weight,
    out_weight,
    in_weight,
    in_bias,
    fc_weight,
    fc_bias,
    norm_gain,
    norm_bias,
    cotangent,
):
    rep_count = lax.axis_size("rep")
    shard_count = lax.axis_size("shard")
    shard = lax.axis_index("shard")
    grad_scale = 1.0 / math.sqrt(TOK_DEV * rep_count * shard_count)
    lengths, owner = lengths.reshape(1, -1), owner.reshape(1, -1)
    small = sum(jnp.pad(part.astype(jnp.float32), (first, 2048 - first - part.shape[0])) for first, part in (
        (0, in_bias), (1024, fc_bias), (1280, norm_gain), (1536, norm_bias))).reshape(16, 128)
    blocks, small_sum, layer_out, input_grad = block(
        small, lengths, owner, positions.reshape(-1, 128), tokens, cotangent, in_weight, fc_weight, qkv_weight, out_weight,
        rep_count, shard_count, 48)
    small_sum = small_sum.reshape(-1) * grad_scale

    def own_part(first, size):
        return lax.dynamic_slice_in_dim(small_sum, first + shard * (size // 4), size // 4)

    grad_in, grad_fc, grad_qkv, grad_out = assemble(
        blocks, ((16, 256, 4 * D), (0, 1024, D), (32, 256, 3 * D), (44, 256, D)), grad_scale)
    return (
        layer_out,
        input_grad,
        grad_qkv,
        grad_out,
        grad_in,
        own_part(0, 4096),
        grad_fc,
        own_part(4096, D),
        own_part(4096 + D, D),
        own_part(4096 + 2 * D, D),
    )


def solution(mesh):
    in_specs = (
        P(("rep", "shard"), None),
        P(("rep", "shard")),
        P(),
        P(),
        P("shard", None),
        P("shard", None),
        P("shard", None),
        P("shard"),
        P("shard", None),
        P("shard"),
        P("shard"),
        P("shard"),
        P(("rep", "shard"), None),
    )
    out_specs = (
        P(("rep", "shard"), None),
        P(("rep", "shard"), None),
        P("shard", None),
        P("shard", None),
        P("shard", None),
        P("shard"),
        P("shard", None),
        P("shard"),
        P("shard"),
        P("shard"),
    )
    return jax.shard_map(body, mesh=mesh, in_specs=in_specs, out_specs=out_specs, check_vma=False)
```

```python
import functools
from functools import partial
import math

import jax
import jax.numpy as jnp
from jax import lax
from jax.experimental import pallas as pl
from jax.experimental.pallas import tpu as pltpu
from jax.sharding import PartitionSpec as P

D = 1024
HEADS = 16
HEAD_DIM = 64
ROT_DIM = 32
TOK_DEV = 512

MESH = pl.DeviceIdType.MESH
BLK = 128
COL = 512
SLOTS = 8
LAGS = (1, 2, 2, 2, 2, 2, 2, 2)
TURN = 0
WRITES = 7
EARLY = 10

EPS = 1e-05
NEG = -1000000000.0
GELU_C = math.sqrt(2.0 / math.pi)
GELU_A = 0.044715
GATHER_LAGS = (0, 2, 4, 5)
SCORE_SCALE = 0.125


def spans_of(lengths_ref, owner_ref, device):
    mine = jnp.where(owner_ref[...] == device, lengths_ref[...], 0).astype(jnp.float32)
    even = lax.broadcasted_iota(jnp.int32, mine.shape, 1) % 2 == 0
    first = jnp.sum(jnp.where(even, mine, 0.0), axis=1, keepdims=True)
    return first.astype(jnp.int32), jnp.sum(mine, axis=1, keepdims=True).astype(jnp.int32)


GATHER_CHUNKS = (4, 4, 4, 1)
GATHER_PAIRS = (4, 6, 11, 12)
FBLK = 256


def front_steps(shards, small_ref, lengths_ref, owner_ref, tok_hbm, cot_hbm, owns, fulls,
                normed_ref, active_ref, gh_ref, up_ref, base_ref, gn_ref, tok_ref, gib_ref, norm_ref, small_full, bias_ref,
                send_sem, recv_sem, core_send, core_recv, own_send, own_recv, local_sem, s_send, s_recv):
    in_full, fc_full = fulls[:2]
    rep = lax.axis_index("rep")
    shard = lax.axis_index("shard")
    y, c = shard // 2, shard % 2
    b0, b1 = rep % 2, (rep // 2) % 2
    core_shard = 2 * y + 1 - c
    other = 2 * (1 - y) + c
    diagonal = 2 * (1 - y) + 1 - c
    core_peer = (rep, core_shard)
    y_peer = (rep, other)
    diagonal_peer = (rep, diagonal)
    peer0 = (rep + 1 - 2 * b0, shard)
    peer1 = (rep + 2 - 4 * b1, shard)
    group = (core_peer, y_peer, diagonal_peer)

    loads = [pltpu.make_async_copy(src, dst, local_sem.at[4 + j]) for j, (src, dst) in enumerate(((tok_hbm, tok_ref), (cot_hbm, up_ref)))]
    chunks = [(a, k) for a in range(4) for k in range(GATHER_CHUNKS[a])]
    n = len(chunks)
    ways = ((b0 + 2 * b1, b1, peer0, peer1), (b1 + 2 * b0, b0, peer1, peer0))

    def remote(src, dst, sems, index, peer):
        return pltpu.make_async_remote_copy(
            src_ref=src, dst_ref=dst, send_sem=sems[0].at[index], recv_sem=sems[1].at[index],
            device_id=peer, device_id_type=MESH)

    def place(i, h):
        a, k = chunks[i]
        own, full = owns[a], fulls[a]
        rows, cols = own.shape
        piece = rows // GATHER_CHUNKS[a] // 4
        return own, full, rows, k * 4 * piece, piece, pl.ds(h * (cols // 2), cols // 2)

    def held(i, h, piece):
        if i in GATHER_PAIRS:
            return (b0, b1)[h] * 2 * piece, 2 * piece
        return ways[h][0] * piece, piece

    def y_copy(i, h):
        own, full, rows, start, piece, cols = place(i, h)
        off, piece = held(i, h, piece)
        at = pl.multiple_of(start + off, 16)
        return remote(own.at[pl.ds(at, piece), cols],
                      full.at[pl.ds(pl.multiple_of(shard * rows + at, 16), piece), cols],
                      (send_sem, recv_sem), (0, i, h), y_peer)

    def first_copy(i, h):
        own, full, rows, start, piece, cols = place(i, h)
        off, piece = held(i, h, piece)
        at = pl.multiple_of(other * rows + start + off, 16)
        ref = full.at[pl.ds(at, piece), cols]
        return remote(ref, ref, (send_sem, recv_sem), (1, i, h), ways[h][2])

    def second_copy(i, h):
        own, full, rows, start, piece, cols = place(i, h)
        at = pl.multiple_of(other * rows + start + ways[h][1] * 2 * piece, 16)
        ref = full.at[pl.ds(at, 2 * piece), cols]
        return remote(ref, ref, (send_sem, recv_sem), (2, i, h), ways[h][3])

    def core_copy(i):
        own, full, rows, start, piece, cols = place(i, 0)
        ref = full.at[pl.ds(pl.multiple_of(other * rows + start, 16), 4 * piece)]
        return remote(ref, ref, (core_send, core_recv), (i,), core_peer)

    def own_rows(a):
        rows = owns[a].shape[0]
        return fulls[a].at[pl.ds(pl.multiple_of(shard * rows, 16), rows)]

    def own_copy(a):
        return remote(owns[a], own_rows(a), (own_send, own_recv), (a,), core_peer)

    def local_copy(a):
        return pltpu.make_async_copy(owns[a], own_rows(a), local_sem.at[a])

    def small_copy(j):
        return remote(small_ref, small_full.at[shard], (s_send, s_recv), (j,), group[j])

    def begin():
        for load in loads:
            load.start()
        for j in range(3):
            small_copy(j).start()
        for i in range(n):
            for h in range(2):
                y_copy(i, h).start()
        for a in range(4):
            own_copy(a).start()
            local_copy(a).start()

    def norm_all():
        small_full[shard] = small_ref[...]
        for j in range(3):
            small_copy(j).wait()
        for o in range(4):
            for r in range(8):
                bias_ref[0:1, (o * 8 + r) * 128:(o * 8 + r + 1) * 128] = small_full[o, r:r + 1, :]
            for r in range(2):
                span = slice((o * 2 + r) * 128, (o * 2 + r + 1) * 128)
                norm_ref[2:3, span] = small_full[o, 8 + r:9 + r, :]
                norm_ref[0:1, span] = small_full[o, 10 + r:11 + r, :]
                norm_ref[1:2, span] = small_full[o, 12 + r:13 + r, :]
        for load in loads:
            load.wait()

    def norm_rows(r, carry):
        at = pl.ds(pl.multiple_of(r * 64, 64), 64)
        x = tok_ref[at, :].astype(jnp.float32)
        center = x - jnp.mean(x, axis=-1, keepdims=True)
        spread = jnp.mean(center * center, axis=-1, keepdims=True)
        normed = center * lax.rsqrt(spread + EPS) * norm_ref[0:1, :] + norm_ref[1:2, :]
        normed_ref[at, :] = normed.astype(jnp.bfloat16)
        base_ref[at, :] = x + norm_ref[2:3, :]
        slot = lax.broadcasted_iota(jnp.int32, (64, 1), 0) + r * 64
        _, used = spans_of(lengths_ref, owner_ref, rep * shards + shard)
        up_ref[at, :] = jnp.where(slot < used, up_ref[at, :].astype(jnp.float32), 0.0).astype(jnp.bfloat16)
        return carry

    def span(j):
        return pl.ds(pl.multiple_of(j * FBLK, FBLK), FBLK)

    def hidden_block(j, carry):
        at = span(j % 4 * (4096 // FBLK // 4) + j // 4)
        hidden = jnp.dot(normed_ref[...], in_full[:, at], preferred_element_type=jnp.float32) + bias_ref[0:1, at]
        cube = hidden * hidden
        turn = jnp.tanh(GELU_C * hidden * (1.0 + GELU_A * cube))
        half = 0.5 * (1.0 + turn)
        active_ref[:, at] = (hidden * half).astype(jnp.bfloat16)
        slope = half + 0.5 * hidden * (1.0 - turn * turn) * (GELU_C * (1.0 + 3.0 * GELU_A * cube))
        gh_ref[:, at] = slope.astype(jnp.bfloat16)
        return carry

    def back_block(j, carry):
        at = span(j)
        grad = lax.dot_general(up_ref[...], fc_full[at, :], (((1,), (1,)), ((), ())), preferred_element_type=jnp.float32)
        low = (grad * gh_ref[:, at].astype(jnp.float32)).astype(jnp.bfloat16)
        gh_ref[:, at] = low
        gib_ref[0:1, at] = jnp.sum(low.astype(jnp.float32), axis=0, keepdims=True)
        return carry

    def mlp_block(j, carry):
        at = span(j)
        base_ref[:, at] = base_ref[:, at] + jnp.dot(active_ref[...], fc_full[:, at], preferred_element_type=jnp.float32)
        return carry

    def grad_block(j, carry):
        at = span(j)
        gn_ref[:, at] = lax.dot_general(gh_ref[...], in_full[at, :], (((1,), (1,)), ((), ())), preferred_element_type=jnp.float32)
        return carry

    def loop(block, lo, hi):
        lax.fori_loop(lo, hi, block, 0)

    work = {1: [norm_all]}
    nf = 4096 // FBLK
    lag = GATHER_LAGS
    ends = [sum(GATHER_CHUNKS[:a + 1]) - 1 + lag[3] for a in range(4)]

    def ready(a):
        own_copy(a).wait_recv()
        local_copy(a).wait()

    def plan(step, *todo):
        work.setdefault(step, []).extend(todo)

    bind = functools.partial
    nd = D // FBLK
    for j in range(4):
        plan(1 + j, bind(loop, norm_rows, 2 * j, 2 * j + 2))
    plan(ends[0], bind(ready, 0))
    for j in range(4):
        plan(ends[0] + j, bind(loop, hidden_block, j * nf // 4, (j + 1) * nf // 4))
    plan(ends[1], bind(ready, 1))
    for j in range(2):
        plan(ends[1] + j, bind(loop, back_block, j * nf // 2, (j + 1) * nf // 2))
    for j in range(2):
        plan(ends[1] + 2 + j, bind(loop, grad_block, j * nd // 2, (j + 1) * nd // 2))
    for j in range(2):
        plan(ends[1] + 4 + j, bind(loop, mlp_block, j * nd // 2, (j + 1) * nd // 2))

    def step(i):
        if i < n:
            for h in range(2):
                y_copy(i, h).wait_recv()
                first_copy(i, h).start()
        if 0 <= i - lag[1] < n:
            for h in range(2):
                first_copy(i - lag[1], h).wait_recv()
                if i - lag[1] not in GATHER_PAIRS:
                    second_copy(i - lag[1], h).start()
            if i - lag[1] in GATHER_PAIRS:
                core_copy(i - lag[1]).start()
        if 0 <= i - lag[2] < n and i - lag[2] not in GATHER_PAIRS:
            for h in range(2):
                second_copy(i - lag[2], h).wait_recv()
            core_copy(i - lag[2]).start()
        if 0 <= i - lag[3] < n:
            core_copy(i - lag[3]).wait_recv()
        for todo in work.get(i, []):
            todo()

    def sent(a):
        for i in range(n):
            if chunks[i][0] == a:
                for h in range(2):
                    y_copy(i, h).wait_send()
                    first_copy(i, h).wait_send()
                    if i not in GATHER_PAIRS:
                        second_copy(i, h).wait_send()
                core_copy(i).wait_send()
        own_copy(a).wait_send()

    plan(ends[1] + 3, bind(sent, 0))

    def finish():
        ready(2)
        ready(3)
        for a in range(1, 4):
            sent(a)

    return begin, n + lag[3], ends[0], ends[1] + 3, step, finish


QBLK = 256


def attend_pair(q, k, v, ga, bias_ref, cos_ref, sa_ref, sb_ref, put_att, put_grad):
    f32, bf = jnp.float32, jnp.bfloat16
    nt = (((1,), (1,)), ((), ()))
    tn = (((0,), (0,)), ((), ()))
    lane = lax.broadcasted_iota(jnp.int32, (1, 128), 1)
    keep = [(lane < HEAD_DIM).astype(f32).astype(bf), (lane >= HEAD_DIM).astype(f32).astype(bf)]
    q = q * jnp.asarray(SCORE_SCALE, bf)
    attended, grad_q = [], []
    grad_k, grad_v = {}, {}
    n_blocks = TOK_DEV // QBLK

    def add(store, block, value):
        store[block] = value if block not in store else store[block] + value

    for r in range(n_blocks):
        rows = slice(r * QBLK, (r + 1) * QBLK)
        keys = (r + 1) * QBLK
        att = gq = None
        for h in range(2):
            qh = q[rows] * keep[h]
            gh = ga[rows] * keep[h]
            kh = k[:keys] * keep[h]
            vh = v[:keys] * keep[h]
            scores = lax.dot_general(qh, k[:keys], nt, preferred_element_type=f32) + bias_ref[rows, :keys]
            weight = jnp.exp(scores - jnp.max(scores, axis=-1, keepdims=True))
            soft = weight * (1.0 / jnp.sum(weight, axis=-1, keepdims=True))
            low = soft.astype(bf)
            grad_soft = lax.dot_general(gh, v[:keys], nt, preferred_element_type=f32)
            weighted = soft * grad_soft
            delta = jnp.sum(weighted, axis=-1, keepdims=True)
            grad_scores = (weighted - soft * delta).astype(bf)
            part = jnp.dot(low, vh, preferred_element_type=f32)
            att = part if att is None else att + part
            part = jnp.dot(grad_scores, kh, preferred_element_type=f32)
            gq = part if gq is None else gq + part
            gk = lax.dot_general(grad_scores, qh, tn, preferred_element_type=f32)
            gv = lax.dot_general(low, gh, tn, preferred_element_type=f32)
            for b in range(r + 1):
                span = slice(b * QBLK, (b + 1) * QBLK)
                add(grad_k, b, gk[span])
                add(grad_v, b, gv[span])
        attended.append(att)
        grad_q.append(gq)

    def unturn(x):
        x = x.astype(bf).astype(f32)
        return x * cos_ref[...] - pltpu.roll(x, 127, 1) * sa_ref[...] - pltpu.roll(x, 1, 1) * sb_ref[...]

    put_att(jnp.concatenate(attended, 0).astype(bf))
    put_grad(0, unturn(jnp.concatenate(grad_q, 0) * SCORE_SCALE).astype(bf))
    put_grad(1, unturn(jnp.concatenate([grad_k[b] for b in range(n_blocks)], 0)).astype(bf))
    put_grad(2, jnp.concatenate([grad_v[b] for b in range(n_blocks)], 0).astype(bf))


def reduce_steps(n_rep, n_chunks, lengths_ref, owner_ref, pos_ref, norm_ref, out_hbm_blocks, small_out, layer_hbm, grad_hbm,
                 layer_ref, grad_ref, left, right, turned, qkv_full, out_full, gn_ref, base_ref, tok_ref, held_ref,
                 bias_ref, cos_ref, sa_ref, sb_ref, store_sem, c_send, c_keep, c_recv, acc, y_recv, recvs, s_buf, s_recv,
                 send_sem, recv_sem, s_send_sem, s_recv_sem):
    rep = lax.axis_index("rep")
    shard = lax.axis_index("shard")
    y, c = shard // 2, shard % 2
    nbits = int(math.log2(n_rep))
    bits = [(rep // (1 << b)) % 2 for b in range(nbits)]

    def rep_peer(b):
        return (rep + (1 << b) * (1 - 2 * bits[b]), shard)

    core_peer = (rep, shard + 1 - 2 * c)
    y_peer = (rep, shard + 2 - 4 * y)
    last = 3
    extra = list(range(last, nbits))
    half = BLK // 2

    def way(t):
        return (t % TURN) // (TURN - 1) if TURN else 0

    def pick(d, zero, one):
        return zero + d * (one - zero)

    def bit_of(k, d):
        return bits[2] if k == 2 else pick(d, bits[k], bits[1 - k])

    def bit_peer(k, d):
        return rep_peer(2) if k == 2 else (pick(d, rep_peer(k)[0], rep_peer(1 - k)[0]), shard)

    def base(k, d):
        off = 0
        for j in range(k):
            off = off + bit_of(j, d) * (half >> j)
        return off

    peers = [core_peer, y_peer] + [rep_peer(b) for b in range(nbits)]

    def copy(src, dst, stage, slot, peer):
        return pltpu.make_async_remote_copy(
            src_ref=src, dst_ref=dst, send_sem=send_sem.at[stage, slot],
            recv_sem=recv_sem.at[stage, slot], device_id=peer, device_id_type=MESH)

    def core_copy(t):
        s = t % SLOTS
        return copy(c_send.at[s], c_recv.at[s], 0, s, core_peer)

    def first_copy(t, d):
        s = t % SLOTS
        if d:
            return copy(acc.at[s, :, 1 - bits[1]], y_recv.at[s], 1, s, rep_peer(1))
        return copy(acc.at[s, 1 - y], y_recv.at[s], 1, s, y_peer)

    def second_copy(t):
        s, d = t % SLOTS, way(t)
        src = acc.at[s, pick(d, y, 1 - y), pick(d, 1 - bits[0], bits[1])]
        peer = (pick(d, rep_peer(0)[0], rep), pick(d, shard, y_peer[1]))
        return copy(src, recvs[0].at[s], 2, s, peer)

    def rows_copy(k, t):
        s, d = t % SLOTS, way(t)
        rows = half >> k
        start = pl.multiple_of(base(k + 1, d) - bit_of(0, d) * half + (1 - 2 * bit_of(k, d)) * rows, 16)
        return copy(acc.at[s, y, bit_of(0, d), pl.ds(start, rows)], recvs[k].at[s], 2 + k, s, bit_peer(k, d))

    def own(t):
        return pl.multiple_of(base(last, way(t)), 16)

    def own_acc(t, k=last):
        d = way(t)
        return t % SLOTS, y, bit_of(0, d), pl.ds(pl.multiple_of(base(k, d) - bit_of(0, d) * half, 16), half >> (k - 1))

    tail = BLK >> last

    def extra_copy(j, t):
        s = t % SLOTS
        return copy(acc.at[own_acc(t)], recvs[last + j].at[s], 2 + last + j, s, rep_peer(extra[j]))

    across = held_ref.shape[1] // COL

    def held(t, start, rows):
        at = pl.multiple_of(t // across * BLK + start, 16)
        return held_ref.at[pl.ds(at, rows), pl.ds(pl.multiple_of(t % across * COL, COL), COL)]

    def gather_copy(k, t):
        s, d = t % SLOTS, way(t)
        ref = held(t, base(k + 1, d), half >> k)
        return copy(ref, ref, 2 + last + len(extra) + k, s, bit_peer(k, d))

    f32, bf = jnp.float32, jnp.bfloat16
    nt = (((1,), (1,)), ((), ()))

    def block(start, j, size=256):
        return pl.ds(pl.multiple_of(start + j * size, size), size)

    def tables(u):
        first, used = spans_of(lengths_ref, owner_ref, rep * lax.axis_size("shard") + shard)
        lane = lax.broadcasted_iota(jnp.int32, (128, 128), 1)
        even = lane % 2 == 0
        lane = lane % HEAD_DIM
        inverse = jnp.exp((lane // 2).astype(f32) * (-2.0 * math.log(10000.0) / ROT_DIM))
        inverse = jnp.where(lane < ROT_DIM, inverse, 0.0)
        key = lax.broadcasted_iota(jnp.int32, (128, TOK_DEV), 1)
        for g in range(TOK_DEV // 128):
            rows = slice(g * 128, (g + 1) * 128)
            query = lax.broadcasted_iota(jnp.int32, (128, TOK_DEV), 0) + g * 128
            same = (query < used) & ((query < first) == (key < first))
            bias_ref[rows, :] = jnp.where((key == query) | ((key < query) & same), 0.0, NEG)
            place = jnp.broadcast_to(pos_ref[g:g + 1, :].astype(f32), (128, 128)).T
            angles = place * inverse
            sine = jnp.sin(angles)
            cos_ref[rows, :] = jnp.cos(angles)
            sa_ref[rows, :] = jnp.where(even, -sine, 0.0)
            sb_ref[rows, :] = jnp.where(even, 0.0, sine)

    def turn_rows(u):
        for b in range(2):
            rows = jnp.dot(left[:, 0:D], qkv_full[:, block(0, 2 * u + b)], preferred_element_type=f32)
            for g in range(2):
                part = rows[:, g * 128:(g + 1) * 128]
                part = part * cos_ref[...] + pltpu.roll(part, 127, 1) * sa_ref[...] + pltpu.roll(part, 1, 1) * sb_ref[...]
                right[:, block(0, 4 * u + 2 * b + g, 128)] = part.astype(bf)

    def value_rows(u):
        for b in range(2):
            at = block(2 * D, 2 * u + b)
            right[:, at] = jnp.dot(left[:, 0:D], qkv_full[:, at], preferred_element_type=f32).astype(bf)

    def grad_attended(u):
        for b in range(2):
            part = lax.dot_general(right[:, 3 * D:4 * D], out_full[block(0, 2 * u + b), :], nt, preferred_element_type=f32)
            left[:, block(D, 2 * u + b)] = part.astype(bf)

    def attend(u):
        @pl.when(u % 2 == 0)
        def _():
            pair = u // 2
            spans = [block(k * D, pair, 128) for k in range(3)]
            span = block(D, pair, 128)

            def put_att(value):
                left[:, span] = value

            def put_grad(part, value):
                right[:, spans[part]] = value
            attend_pair(right[:, spans[0]], right[:, spans[1]], right[:, spans[2]], left[:, span],
                        bias_ref, cos_ref, sa_ref, sb_ref, put_att, put_grad)

    def grad_normed(u):
        at = block(0, u)
        gn_ref[:, at] = gn_ref[:, at] + lax.dot_general(right[:, 0:3 * D], qkv_full[at, :], nt, preferred_element_type=f32)

    def project(u):
        for b in range(2):
            at = block(0, 2 * u + b)
            layer_ref[:, at] = (base_ref[:, at] + jnp.dot(left[:, D:2 * D], out_full[:, at], preferred_element_type=f32)).astype(bf)

    def norm_back(u):
        @pl.when(u == 0)
        def _():
            s_buf[0, :, 4 * D:] = jnp.zeros((1, 3 * D), f32)
        at = block(0, u, 64)
        x = tok_ref[at, :].astype(f32)
        center = x - jnp.mean(x, axis=-1, keepdims=True)
        scale = lax.rsqrt(jnp.mean(center * center, axis=-1, keepdims=True) + EPS)
        unit = center * scale
        grad = gn_ref[at, :]
        upstream = right[at, 3 * D:4 * D].astype(f32)
        wide = grad * norm_ref[0:1, :]
        lean = wide - jnp.mean(wide, axis=-1, keepdims=True) - unit * jnp.mean(wide * unit, axis=-1, keepdims=True)
        grad_ref[at, :] = (lean * scale + upstream).astype(bf)
        for k, value in enumerate((upstream, grad * unit, grad)):
            span = slice((4 + k) * D, (5 + k) * D)
            s_buf[0, :, span] = s_buf[0, :, span] + jnp.sum(value, axis=0, keepdims=True)

    row_copies = [pltpu.make_async_copy(src, dst, store_sem.at[4 + j])
                  for j, (src, dst) in enumerate(((layer_ref, layer_hbm), (grad_ref, grad_hbm)))]

    def send_rows(u):
        for row_copy in row_copies:
            row_copy.start()

    tasks = [(0, 1, tables), (EARLY, 4, turn_rows), (EARLY, 2, value_rows), (EARLY + 2, 2, grad_attended),
             (EARLY + 4, 16, attend), (EARLY + 20, 4, grad_normed), (EARLY + 24, 2, project), (EARLY + 26, 8, norm_back),
             (EARLY + 34, 1, send_rows)]

    def store(t):
        return pltpu.make_async_copy(held(t, 0, BLK), out_hbm_blocks.at[t], store_sem.at[t % 4])

    def compute(t):
        s = t % SLOTS
        first, stride, column, new = chunk_plan(t)

        @pl.when(new)
        def _():
            for o in range(4):
                at = pl.multiple_of(first + o * stride, BLK)
                turned[o % 2, (o // 2) * BLK:(o // 2 + 1) * BLK, :] = left[:, pl.ds(at, BLK)].T
        operand = right[:, pl.ds(pl.multiple_of(column, COL), COL)]
        for side, dst in ((1 - c, c_send), (c, c_keep)):
            part = jnp.dot(turned[side], operand, preferred_element_type=jnp.float32)
            dst[s] = part.astype(jnp.bfloat16).reshape(2, 2, half, COL)
        core_copy(t).start()

    def each_way(t, body):
        for d in range(2 if TURN else 1):
            @pl.when(way(t) == d)
            def _(d=d):
                body(d)

    def after_core(t):
        s = t % SLOTS
        core_copy(t).wait()

        def total(d):
            for own_half in range(2):
                if d:
                    at = (s, slice(None), bits[1] if own_half else 1 - bits[1])
                else:
                    at = (s, y if own_half else 1 - y)
                acc[at] = c_keep[at] + c_recv[at]
                if not own_half:
                    first_copy(t, d).start()
        each_way(t, total)

    def after_first(t):
        s = t % SLOTS

        def total(d):
            first_copy(t, d).wait()
            at = (s, slice(None), bits[1]) if d else (s, y)
            acc[at] = acc[at] + y_recv[s]
        each_way(t, total)
        second_copy(t).start()

    def after_rows(k, t):
        s = t % SLOTS
        (second_copy(t) if k == 0 else rows_copy(k, t)).wait()
        at = own_acc(t, k + 1)
        total = acc[at] + recvs[k][s]
        if k + 1 < last:
            acc[at] = total
            rows_copy(k + 1, t).start()
        elif extra:
            acc[at] = total
            extra_copy(0, t).start()
        else:
            held(t, base(last, way(t)), tail)[...] = total
            gather_copy(last - 1, t).start()

    def after_extra(j, t):
        s = t % SLOTS
        extra_copy(j, t).wait()
        total = acc[own_acc(t)] + recvs[last + j][s]
        if j + 1 < len(extra):
            acc[own_acc(t)] = total
            extra_copy(j + 1, t).start()
        else:
            held(t, base(last, way(t)), tail)[...] = total
            gather_copy(last - 1, t).start()

    def after_gather(k, t):
        gather_copy(k, t).wait()
        if k > 0:
            gather_copy(k - 1, t).start()
        else:
            @pl.when(t >= 4)
            def _():
                store(t - 4).wait()
            store(t).start()

    stages = [(0, compute), (LAGS[0], after_core), (LAGS[0]+LAGS[1], after_first)]
    lag = LAGS[0]+LAGS[1]
    for k in range(last):
        lag += LAGS[2+k]
        stages.append((lag, functools.partial(after_rows, k)))
    for j in range(len(extra)):
        lag += 1
        stages.append((lag, functools.partial(after_extra, j)))
    for k in reversed(range(last)):
        lag += LAGS[5+last-1-k]
        stages.append((lag, functools.partial(after_gather, k)))

    s_peers = peers

    def small_copy(j):
        return pltpu.make_async_remote_copy(
            src_ref=s_buf.at[j], dst_ref=s_recv.at[j], send_sem=s_send_sem.at[j],
            recv_sem=s_recv_sem.at[j], device_id=s_peers[j], device_id_type=MESH)

    def small_step(j):
        if j > 0:
            small_copy(j - 1).wait()
            total = s_buf[j - 1] + s_recv[j - 1]
            if j < len(s_peers):
                s_buf[j] = total
            else:
                small_out[...] = total
        if j < len(s_peers):
            small_copy(j).start()

    def step(i, carry):
        for delay, stage in reversed(stages):
            @pl.when((i >= delay) & (i < n_chunks + delay))
            def _(stage=stage, delay=delay):
                stage(i - delay)
        for start, count, task in tasks:
            @pl.when((i >= start) & (i < start + count))
            def _(start=start, task=task):
                task(i - start)
        for j in range(len(s_peers) + 1):
            @pl.when(i == 47 + j)
            def _(j=j):
                small_step(j)
        return carry

    def finish():
        for t in range(n_chunks - 4, n_chunks):
            store(t).wait()
        for row_copy in row_copies:
            row_copy.wait()
    return n_chunks + lag, step, finish


def block_kernel(shards, n_rep, n_chunks, n_recvs, small_ref, lengths_ref, owner_ref, pos_ref, tok_hbm, cot_hbm,
                 in_own, fc_own, qkv_own, out_own, blocks_hbm, small_out, layer_hbm, grad_hbm,
                 in_full, fc_full, qkv_full, out_full, left, right, turned, gn_ref, base_ref, tok_ref,
                 small_full, ff_bias, norm_ref, bias_ref, cos_ref, sa_ref, sb_ref, s_buf, s_recv,
                 layer_ref, grad_ref, c_send, c_keep, c_recv, acc, y_recv, *rest):
    recvs, sems = rest[:n_recvs], rest[n_recvs:]
    rep = lax.axis_index("rep")
    shard = lax.axis_index("shard")
    barrier = pltpu.get_barrier_semaphore()
    peers = [(rep, 4 * (shard // 4) + (shard + k) % 4) for k in range(1, 4)]
    b = 1
    while b < n_rep:
        peers.append((rep + b * (1 - 2 * ((rep // b) % 2)), shard))
        b *= 2
    for p in peers:
        pl.semaphore_signal(barrier, inc=1, device_id=p, device_id_type=MESH)
    pl.semaphore_wait(barrier, len(peers))

    begin, gather_steps, free_from, in_done, gather_step, gather_finish = front_steps(
        shards, small_ref, lengths_ref, owner_ref, tok_hbm, cot_hbm,
        (in_own, fc_own, qkv_own, out_own), (in_full, fc_full, qkv_full, out_full),
        left.at[:, 0:D], left.at[:, 2 * D:6 * D], right.at[:, 4 * D:8 * D], right.at[:, 3 * D:4 * D],
        base_ref, gn_ref, tok_ref, s_buf.at[0], norm_ref, small_full, ff_bias, *sems[:9])
    total, step, finish = reduce_steps(
        n_rep, n_chunks, lengths_ref, owner_ref, pos_ref, norm_ref, blocks_hbm, small_out, layer_hbm, grad_hbm,
        layer_ref, grad_ref, left, right, turned, qkv_full, out_full, gn_ref, base_ref, tok_ref, in_full,
        bias_ref, cos_ref, sa_ref, sb_ref, sems[9], c_send, c_keep, c_recv, acc, y_recv, recvs, s_buf, s_recv, *sems[10:])
    begin()
    early = 0
    for i in range(gather_steps):
        gather_step(i)
        due = (i - free_from + 1) * EARLY // (gather_steps - free_from)
        while early < (due if i >= in_done else min(due, WRITES)):
            step(early, 0)
            early += 1
    gather_finish()
    lax.fori_loop(early, total, step, 0)
    finish()


def block(small, lengths, owner, positions, tokens, cotangent, in_own, fc_own, qkv_own, out_own, n_rep, shards, n_chunks):
    nbits = int(math.log2(n_rep))
    last = 3
    n_extra = nbits - last
    n_stage = 2 + last + n_extra + last
    bf, f32 = jnp.bfloat16, jnp.float32
    rows = tokens.shape[0]
    ff = in_own.shape[1]
    n = sum(GATHER_CHUNKS)
    recv_rows = [BLK >> (k + 1) for k in range(last)] + [BLK >> last] * n_extra
    chunk = (SLOTS, 2, BLK // 2, COL)
    pair = (SLOTS, 2, 2, BLK // 2, COL)
    n_small = 2 + nbits
    sums = (1, 3 * D + ff)
    hbm = pl.BlockSpec(memory_space=pl.ANY)
    vm = pl.BlockSpec(memory_space=pltpu.VMEM)
    dma = pltpu.SemaphoreType.DMA

    def full(own):
        return pltpu.VMEM((own.shape[0] * shards, own.shape[1]), bf)
    return pl.pallas_call(
        functools.partial(block_kernel, shards, n_rep, n_chunks, len(recv_rows)),
        out_shape=(jax.ShapeDtypeStruct((n_chunks, BLK, COL), bf), jax.ShapeDtypeStruct(sums, f32),
                   jax.ShapeDtypeStruct((rows, D), bf), jax.ShapeDtypeStruct((rows, D), bf)),
        in_specs=[vm] * 4 + [hbm] * 6,
        out_specs=(hbm, vm, hbm, hbm),
        scratch_shapes=[
            full(in_own), full(fc_own), full(qkv_own), full(out_own),
            pltpu.VMEM((rows, 2 * D + ff), bf), pltpu.VMEM((rows, 4 * D + ff), bf), pltpu.VMEM((2, 2 * BLK, rows), bf),
            pltpu.VMEM((rows, D), f32), pltpu.VMEM((rows, D), f32), pltpu.VMEM((rows, D), bf),
            pltpu.VMEM((shards,) + small.shape, f32), pltpu.VMEM((1, ff), f32), pltpu.VMEM((8, D), f32),
            pltpu.VMEM((rows, rows), f32), *[pltpu.VMEM((rows, 128), f32)] * 3,
            pltpu.VMEM((n_small,) + sums, f32), pltpu.VMEM((n_small,) + sums, f32),
            pltpu.VMEM((rows, D), bf), pltpu.VMEM((rows, D), bf),
            pltpu.VMEM(pair, bf), pltpu.VMEM(pair, bf), pltpu.VMEM(pair, bf), pltpu.VMEM(pair, bf), pltpu.VMEM(chunk, bf),
            *[pltpu.VMEM((SLOTS, r, COL), bf) for r in recv_rows],
            dma((3, n, 2)), dma((3, n, 2)), dma((n,)), dma((n,)), dma((4,)), dma((4,)), dma((6,)), dma((3,)), dma((3,)),
            dma((6,)), dma((n_stage, SLOTS)), dma((n_stage, SLOTS)), dma((n_small,)), dma((n_small,)),
        ],
        compiler_params=pltpu.CompilerParams(collective_id=1, has_side_effects=True, vmem_limit_bytes=67043328),
        name="block",
    )(small, lengths, owner, positions, tokens, cotangent, in_own, fc_own, qkv_own, out_own)


def chunk_plan(t):
    cases = [
        (2 * D + (t // 2) * BLK, D, 3 * D + (t % 2) * COL, t % 2),
        (((t - 16) // 8) * BLK, D // 4, 4 * D + (t % 8) * COL, t % 8),
        (((t - 32) // 6) * BLK, D // 4, ((t - 32) % 6) * COL, (t - 32) % 6),
        (D + ((t - 44) // 2) * BLK, D // 4, 3 * D + (t % 2) * COL, t % 2),
    ]
    first, stride, column, within = (
        jnp.where(t < 16, cases[0][i], jnp.where(t < 32, cases[1][i], jnp.where(t < 44, cases[2][i], cases[3][i])))
        for i in range(4))
    return first, stride, column, within == 0


def assemble(blocks, rows, places, scale):
    def kern(in_hbm, *rest):
        n = len(rows)
        row_hbm, row_out, row_ref, outs = rest[:n], rest[n:2 * n], rest[-4 - n:-4], rest[2 * n:-4 - n]
        in_ref, stage, load_sem, sem = rest[-4:]
        first_row = blocks.shape[0]
        copies = []
        row_loads = [pltpu.make_async_copy(row_hbm[j], row_ref[j], sem.at[first_row + j]) for j in range(n)]
        row_stores = [pltpu.make_async_copy(row_ref[j], row_out[j], sem.at[first_row + n + j]) for j in range(n)]
        for load_row in row_loads:
            load_row.start()
        part = 4

        def load(g):
            at = pl.ds(g * part, part)
            return pltpu.make_async_copy(in_hbm.at[at], in_ref.at[at], load_sem.at[g])
        for g in range(blocks.shape[0] // part):
            load(g).start()
        for load_row, store_row in zip(row_loads, row_stores):
            load_row.wait()
            store_row.start()
            copies.append(store_row)
        for (first, height, cols), out in zip(places, outs):
            across = cols // COL
            for i in range(height // BLK):
                for j in range(across):
                    t = first + i * across + j
                    if t % part == 0:
                        load(t // part).wait()
                    stage[t] = in_ref[t].astype(jnp.float32) * scale
                    copies.append(pltpu.make_async_copy(
                        stage.at[t], out.at[i * BLK:(i + 1) * BLK, j * COL:(j + 1) * COL], sem.at[t]))
                    copies[-1].start()
        for copy in copies:
            copy.wait()

    return pl.pallas_call(
        kern,
        out_shape=[jax.ShapeDtypeStruct(x.shape, x.dtype) for x in rows]
        + [jax.ShapeDtypeStruct((height, cols), jnp.float32) for _, height, cols in places],
        in_specs=[pl.BlockSpec(memory_space=pl.ANY)] * (1 + len(rows)),
        out_specs=[pl.BlockSpec(memory_space=pl.ANY)] * (len(rows) + len(places)),
        scratch_shapes=[*[pltpu.VMEM(x.shape, x.dtype) for x in rows], pltpu.VMEM(blocks.shape, blocks.dtype), pltpu.VMEM(blocks.shape, jnp.float32),
                        pltpu.SemaphoreType.DMA((blocks.shape[0] // 4,)), pltpu.SemaphoreType.DMA((blocks.shape[0] + 2 * len(rows),))],
        compiler_params=pltpu.CompilerParams(vmem_limit_bytes=63 * 2**20),
        name="assemble",
    )(blocks, *rows)


def body(
    tokens,
    positions,
    lengths,
    owner,
    qkv_weight,
    out_weight,
    in_weight,
    in_bias,
    fc_weight,
    fc_bias,
    norm_gain,
    norm_bias,
    cotangent,
):
    rep_count = lax.axis_size("rep")
    shard_count = lax.axis_size("shard")
    shard = lax.axis_index("shard")
    grad_scale = 1.0 / math.sqrt(TOK_DEV * rep_count * shard_count)
    lengths, owner = lengths.reshape(1, -1), owner.reshape(1, -1)
    small = sum(jnp.pad(part.astype(jnp.float32), (first, 2048 - first - part.shape[0])) for first, part in (
        (0, in_bias), (1024, fc_bias), (1280, norm_gain), (1536, norm_bias))).reshape(16, 128)
    blocks, small_sum, layer_out, input_grad = block(
        small, lengths, owner, positions.reshape(-1, 128), tokens, cotangent, in_weight, fc_weight, qkv_weight, out_weight,
        rep_count, shard_count, 48)
    small_sum = small_sum.reshape(-1) * grad_scale

    def own_part(first, size):
        return lax.dynamic_slice_in_dim(small_sum, first + shard * (size // 4), size // 4)

    layer_out, input_grad, grad_in, grad_fc, grad_qkv, grad_out = assemble(
        blocks, (layer_out, input_grad), ((16, 256, 4 * D), (0, 1024, D), (32, 256, 3 * D), (44, 256, D)), grad_scale)
    return (
        layer_out,
        input_grad,
        grad_qkv,
        grad_out,
        grad_in,
        own_part(0, 4096),
        grad_fc,
        own_part(4096, D),
        own_part(4096 + D, D),
        own_part(4096 + 2 * D, D),
    )


def solution(mesh):
    in_specs = (
        P(("rep", "shard"), None),
        P(("rep", "shard")),
        P(),
        P(),
        P("shard", None),
        P("shard", None),
        P("shard", None),
        P("shard"),
        P("shard", None),
        P("shard"),
        P("shard"),
        P("shard"),
        P(("rep", "shard"), None),
    )
    out_specs = (
        P(("rep", "shard"), None),
        P(("rep", "shard"), None),
        P("shard", None),
        P("shard", None),
        P("shard", None),
        P("shard"),
        P("shard", None),
        P("shard"),
        P("shard"),
        P("shard"),
    )
    return jax.shard_map(body, mesh=mesh, in_specs=in_specs, out_specs=out_specs, check_vma=False)
```

```python
import functools
from functools import partial
import math

import jax
import jax.numpy as jnp
from jax import lax
from jax.experimental import pallas as pl
from jax.experimental.pallas import tpu as pltpu
from jax.sharding import PartitionSpec as P

D = 1024
HEADS = 16
HEAD_DIM = 64
ROT_DIM = 32
TOK_DEV = 512

MESH = pl.DeviceIdType.MESH
BLK = 128
COL = 512
SLOTS = 8
LAGS = (1, 2, 2, 2, 2, 2, 2, 2)
TURN = 0
WRITES = 7
EARLY = 10

EPS = 1e-05
NEG = -1000000000.0
GELU_C = math.sqrt(2.0 / math.pi)
GELU_A = 0.044715
GATHER_LAGS = (0, 2, 4, 5)
SCORE_SCALE = 0.125


def spans_of(lengths_ref, owner_ref, device):
    mine = jnp.where(owner_ref[...] == device, lengths_ref[...], 0).astype(jnp.float32)
    even = lax.broadcasted_iota(jnp.int32, mine.shape, 1) % 2 == 0
    first = jnp.sum(jnp.where(even, mine, 0.0), axis=1, keepdims=True)
    return first.astype(jnp.int32), jnp.sum(mine, axis=1, keepdims=True).astype(jnp.int32)


GATHER_CHUNKS = (4, 4, 4, 1)
GATHER_PAIRS = (4, 6, 11, 12)
FBLK = 256


def front_steps(shards, small_ref, lengths_ref, owner_ref, tok_hbm, cot_hbm, owns, fulls,
                normed_ref, active_ref, gh_ref, up_ref, base_ref, gn_ref, tok_ref, gib_ref, norm_ref, small_full, bias_ref,
                send_sem, recv_sem, core_send, core_recv, own_send, own_recv, local_sem, s_send, s_recv):
    in_full, fc_full = fulls[:2]
    rep = lax.axis_index("rep")
    shard = lax.axis_index("shard")
    y, c = shard // 2, shard % 2
    b0, b1 = rep % 2, (rep // 2) % 2
    core_shard = 2 * y + 1 - c
    other = 2 * (1 - y) + c
    diagonal = 2 * (1 - y) + 1 - c
    core_peer = (rep, core_shard)
    y_peer = (rep, other)
    diagonal_peer = (rep, diagonal)
    peer0 = (rep + 1 - 2 * b0, shard)
    peer1 = (rep + 2 - 4 * b1, shard)
    group = (core_peer, y_peer, diagonal_peer)

    loads = [pltpu.make_async_copy(src, dst, local_sem.at[4 + j]) for j, (src, dst) in enumerate(((tok_hbm, tok_ref), (cot_hbm, up_ref)))]
    chunks = [(a, k) for a in range(4) for k in range(GATHER_CHUNKS[a])]
    n = len(chunks)
    ways = ((b0 + 2 * b1, b1, peer0, peer1), (b1 + 2 * b0, b0, peer1, peer0))

    def remote(src, dst, sems, index, peer):
        return pltpu.make_async_remote_copy(
            src_ref=src, dst_ref=dst, send_sem=sems[0].at[index], recv_sem=sems[1].at[index],
            device_id=peer, device_id_type=MESH)

    def place(i, h):
        a, k = chunks[i]
        own, full = owns[a], fulls[a]
        rows, cols = own.shape
        piece = rows // GATHER_CHUNKS[a] // 4
        return own, full, rows, k * 4 * piece, piece, pl.ds(h * (cols // 2), cols // 2)

    def held(i, h, piece):
        if i in GATHER_PAIRS:
            return (b0, b1)[h] * 2 * piece, 2 * piece
        return ways[h][0] * piece, piece

    def y_copy(i, h):
        own, full, rows, start, piece, cols = place(i, h)
        off, piece = held(i, h, piece)
        at = pl.multiple_of(start + off, 16)
        return remote(own.at[pl.ds(at, piece), cols],
                      full.at[pl.ds(pl.multiple_of(shard * rows + at, 16), piece), cols],
                      (send_sem, recv_sem), (0, i, h), y_peer)

    def first_copy(i, h):
        own, full, rows, start, piece, cols = place(i, h)
        off, piece = held(i, h, piece)
        at = pl.multiple_of(other * rows + start + off, 16)
        ref = full.at[pl.ds(at, piece), cols]
        return remote(ref, ref, (send_sem, recv_sem), (1, i, h), ways[h][2])

    def second_copy(i, h):
        own, full, rows, start, piece, cols = place(i, h)
        at = pl.multiple_of(other * rows + start + ways[h][1] * 2 * piece, 16)
        ref = full.at[pl.ds(at, 2 * piece), cols]
        return remote(ref, ref, (send_sem, recv_sem), (2, i, h), ways[h][3])

    def core_copy(i):
        own, full, rows, start, piece, cols = place(i, 0)
        ref = full.at[pl.ds(pl.multiple_of(other * rows + start, 16), 4 * piece)]
        return remote(ref, ref, (core_send, core_recv), (i,), core_peer)

    def own_rows(a):
        rows = owns[a].shape[0]
        return fulls[a].at[pl.ds(pl.multiple_of(shard * rows, 16), rows)]

    def own_copy(a):
        return remote(owns[a], own_rows(a), (own_send, own_recv), (a,), core_peer)

    def local_copy(a):
        return pltpu.make_async_copy(owns[a], own_rows(a), local_sem.at[a])

    def small_copy(j):
        return remote(small_ref, small_full.at[shard], (s_send, s_recv), (j,), group[j])

    def begin():
        for load in loads:
            load.start()
        for j in range(3):
            small_copy(j).start()
        for i in range(n):
            for h in range(2):
                y_copy(i, h).start()
        for a in range(4):
            own_copy(a).start()
            local_copy(a).start()

    def norm_all():
        small_full[shard] = small_ref[...]
        for j in range(3):
            small_copy(j).wait()
        for o in range(4):
            for r in range(8):
                bias_ref[0:1, (o * 8 + r) * 128:(o * 8 + r + 1) * 128] = small_full[o, r:r + 1, :]
            for r in range(2):
                span = slice((o * 2 + r) * 128, (o * 2 + r + 1) * 128)
                norm_ref[2:3, span] = small_full[o, 8 + r:9 + r, :]
                norm_ref[0:1, span] = small_full[o, 10 + r:11 + r, :]
                norm_ref[1:2, span] = small_full[o, 12 + r:13 + r, :]
        for load in loads:
            load.wait()

    def norm_rows(r, carry):
        at = pl.ds(pl.multiple_of(r * 64, 64), 64)
        x = tok_ref[at, :].astype(jnp.float32)
        center = x - jnp.mean(x, axis=-1, keepdims=True)
        spread = jnp.mean(center * center, axis=-1, keepdims=True)
        normed = center * lax.rsqrt(spread + EPS) * norm_ref[0:1, :] + norm_ref[1:2, :]
        normed_ref[at, :] = normed.astype(jnp.bfloat16)
        base_ref[at, :] = x + norm_ref[2:3, :]
        slot = lax.broadcasted_iota(jnp.int32, (64, 1), 0) + r * 64
        _, used = spans_of(lengths_ref, owner_ref, rep * shards + shard)
        up_ref[at, :] = jnp.where(slot < used, up_ref[at, :].astype(jnp.float32), 0.0).astype(jnp.bfloat16)
        return carry

    def span(j):
        return pl.ds(pl.multiple_of(j * FBLK, FBLK), FBLK)

    def hidden_block(j, carry):
        at = span(j % 4 * (4096 // FBLK // 4) + j // 4)
        hidden = jnp.dot(normed_ref[...], in_full[:, at], preferred_element_type=jnp.float32) + bias_ref[0:1, at]
        cube = hidden * hidden
        turn = jnp.tanh(GELU_C * hidden * (1.0 + GELU_A * cube))
        half = 0.5 * (1.0 + turn)
        active_ref[:, at] = (hidden * half).astype(jnp.bfloat16)
        slope = half + 0.5 * hidden * (1.0 - turn * turn) * (GELU_C * (1.0 + 3.0 * GELU_A * cube))
        gh_ref[:, at] = slope.astype(jnp.bfloat16)
        return carry

    def back_block(j, carry):
        at = span(j)
        grad = lax.dot_general(up_ref[...], fc_full[at, :], (((1,), (1,)), ((), ())), preferred_element_type=jnp.float32)
        low = (grad * gh_ref[:, at].astype(jnp.float32)).astype(jnp.bfloat16)
        gh_ref[:, at] = low
        gib_ref[0:1, at] = jnp.sum(low.astype(jnp.float32), axis=0, keepdims=True)
        return carry

    def grad_block(j, carry):
        at = span(j)
        gn_ref[:, at] = lax.dot_general(gh_ref[...], in_full[at, :], (((1,), (1,)), ((), ())), preferred_element_type=jnp.float32)
        return carry

    def loop(block, lo, hi):
        lax.fori_loop(lo, hi, block, 0)

    work = {1: [norm_all]}
    nf = 4096 // FBLK
    lag = GATHER_LAGS
    ends = [sum(GATHER_CHUNKS[:a + 1]) - 1 + lag[3] for a in range(4)]

    def ready(a):
        own_copy(a).wait_recv()
        local_copy(a).wait()

    def plan(step, *todo):
        work.setdefault(step, []).extend(todo)

    bind = functools.partial
    nd = D // FBLK
    for j in range(4):
        plan(1 + j, bind(loop, norm_rows, 2 * j, 2 * j + 2))
    plan(ends[0], bind(ready, 0))
    for j in range(4):
        plan(ends[0] + j, bind(loop, hidden_block, j * nf // 4, (j + 1) * nf // 4))
    plan(ends[1], bind(ready, 1))
    for j in range(2):
        plan(ends[1] + j, bind(loop, back_block, j * nf // 2, (j + 1) * nf // 2))
    for j in range(2):
        plan(ends[1] + 2 + j, bind(loop, grad_block, j * nd // 2, (j + 1) * nd // 2))

    def step(i):
        if i < n:
            for h in range(2):
                y_copy(i, h).wait_recv()
                first_copy(i, h).start()
        if 0 <= i - lag[1] < n:
            for h in range(2):
                first_copy(i - lag[1], h).wait_recv()
                if i - lag[1] not in GATHER_PAIRS:
                    second_copy(i - lag[1], h).start()
            if i - lag[1] in GATHER_PAIRS:
                core_copy(i - lag[1]).start()
        if 0 <= i - lag[2] < n and i - lag[2] not in GATHER_PAIRS:
            for h in range(2):
                second_copy(i - lag[2], h).wait_recv()
            core_copy(i - lag[2]).start()
        if 0 <= i - lag[3] < n:
            core_copy(i - lag[3]).wait_recv()
        for todo in work.get(i, []):
            todo()

    def sent(a):
        for i in range(n):
            if chunks[i][0] == a:
                for h in range(2):
                    y_copy(i, h).wait_send()
                    first_copy(i, h).wait_send()
                    if i not in GATHER_PAIRS:
                        second_copy(i, h).wait_send()
                core_copy(i).wait_send()
        own_copy(a).wait_send()

    plan(ends[1] + 3, bind(sent, 0))

    def finish():
        ready(2)
        ready(3)
        for a in range(1, 4):
            sent(a)

    return begin, n + lag[3], ends[0], ends[1] + 3, step, finish


QBLK = 256


def attend_pair(q, k, v, ga, bias_ref, cos_ref, sa_ref, sb_ref, put_att, put_grad):
    f32, bf = jnp.float32, jnp.bfloat16
    nt = (((1,), (1,)), ((), ()))
    tn = (((0,), (0,)), ((), ()))
    lane = lax.broadcasted_iota(jnp.int32, (1, 128), 1)
    keep = [(lane < HEAD_DIM).astype(f32).astype(bf), (lane >= HEAD_DIM).astype(f32).astype(bf)]
    q = q * jnp.asarray(SCORE_SCALE, bf)
    attended, grad_q = [], []
    grad_k, grad_v = {}, {}
    n_blocks = TOK_DEV // QBLK

    def add(store, block, value):
        store[block] = value if block not in store else store[block] + value

    for r in range(n_blocks):
        rows = slice(r * QBLK, (r + 1) * QBLK)
        keys = (r + 1) * QBLK
        att = gq = None
        for h in range(2):
            qh = q[rows] * keep[h]
            gh = ga[rows] * keep[h]
            kh = k[:keys] * keep[h]
            vh = v[:keys] * keep[h]
            scores = lax.dot_general(qh, k[:keys], nt, preferred_element_type=f32) + bias_ref[rows, :keys]
            weight = jnp.exp(scores - jnp.max(scores, axis=-1, keepdims=True))
            soft = weight * (1.0 / jnp.sum(weight, axis=-1, keepdims=True))
            low = soft.astype(bf)
            grad_soft = lax.dot_general(gh, v[:keys], nt, preferred_element_type=f32)
            weighted = soft * grad_soft
            delta = jnp.sum(weighted, axis=-1, keepdims=True)
            grad_scores = (weighted - soft * delta).astype(bf)
            part = jnp.dot(low, vh, preferred_element_type=f32)
            att = part if att is None else att + part
            part = jnp.dot(grad_scores, kh, preferred_element_type=f32)
            gq = part if gq is None else gq + part
            gk = lax.dot_general(grad_scores, qh, tn, preferred_element_type=f32)
            gv = lax.dot_general(low, gh, tn, preferred_element_type=f32)
            for b in range(r + 1):
                span = slice(b * QBLK, (b + 1) * QBLK)
                add(grad_k, b, gk[span])
                add(grad_v, b, gv[span])
        attended.append(att)
        grad_q.append(gq)

    def unturn(x):
        x = x.astype(bf).astype(f32)
        return x * cos_ref[...] - pltpu.roll(x, 127, 1) * sa_ref[...] - pltpu.roll(x, 1, 1) * sb_ref[...]

    put_att(jnp.concatenate(attended, 0).astype(bf))
    put_grad(0, unturn(jnp.concatenate(grad_q, 0) * SCORE_SCALE).astype(bf))
    put_grad(1, unturn(jnp.concatenate([grad_k[b] for b in range(n_blocks)], 0)).astype(bf))
    put_grad(2, jnp.concatenate([grad_v[b] for b in range(n_blocks)], 0).astype(bf))


def reduce_steps(n_rep, n_chunks, lengths_ref, owner_ref, pos_ref, norm_ref, out_hbm_blocks, small_out, layer_hbm, grad_hbm,
                 layer_ref, grad_ref, left, right, turned, fc_full, qkv_full, out_full, gn_ref, base_ref, tok_ref, held_ref,
                 bias_ref, cos_ref, sa_ref, sb_ref, store_sem, c_send, c_keep, c_recv, acc, y_recv, recvs, s_buf, s_recv,
                 send_sem, recv_sem, s_send_sem, s_recv_sem):
    rep = lax.axis_index("rep")
    shard = lax.axis_index("shard")
    y, c = shard // 2, shard % 2
    nbits = int(math.log2(n_rep))
    bits = [(rep // (1 << b)) % 2 for b in range(nbits)]

    def rep_peer(b):
        return (rep + (1 << b) * (1 - 2 * bits[b]), shard)

    core_peer = (rep, shard + 1 - 2 * c)
    y_peer = (rep, shard + 2 - 4 * y)
    last = 3
    extra = list(range(last, nbits))
    half = BLK // 2

    def way(t):
        return (t % TURN) // (TURN - 1) if TURN else 0

    def pick(d, zero, one):
        return zero + d * (one - zero)

    def bit_of(k, d):
        return bits[2] if k == 2 else pick(d, bits[k], bits[1 - k])

    def bit_peer(k, d):
        return rep_peer(2) if k == 2 else (pick(d, rep_peer(k)[0], rep_peer(1 - k)[0]), shard)

    def base(k, d):
        off = 0
        for j in range(k):
            off = off + bit_of(j, d) * (half >> j)
        return off

    peers = [core_peer, y_peer] + [rep_peer(b) for b in range(nbits)]

    def copy(src, dst, stage, slot, peer):
        return pltpu.make_async_remote_copy(
            src_ref=src, dst_ref=dst, send_sem=send_sem.at[stage, slot],
            recv_sem=recv_sem.at[stage, slot], device_id=peer, device_id_type=MESH)

    def core_copy(t):
        s = t % SLOTS
        return copy(c_send.at[s], c_recv.at[s], 0, s, core_peer)

    def first_copy(t, d):
        s = t % SLOTS
        if d:
            return copy(acc.at[s, :, 1 - bits[1]], y_recv.at[s], 1, s, rep_peer(1))
        return copy(acc.at[s, 1 - y], y_recv.at[s], 1, s, y_peer)

    def second_copy(t):
        s, d = t % SLOTS, way(t)
        src = acc.at[s, pick(d, y, 1 - y), pick(d, 1 - bits[0], bits[1])]
        peer = (pick(d, rep_peer(0)[0], rep), pick(d, shard, y_peer[1]))
        return copy(src, recvs[0].at[s], 2, s, peer)

    def rows_copy(k, t):
        s, d = t % SLOTS, way(t)
        rows = half >> k
        start = pl.multiple_of(base(k + 1, d) - bit_of(0, d) * half + (1 - 2 * bit_of(k, d)) * rows, 16)
        return copy(acc.at[s, y, bit_of(0, d), pl.ds(start, rows)], recvs[k].at[s], 2 + k, s, bit_peer(k, d))

    def own(t):
        return pl.multiple_of(base(last, way(t)), 16)

    def own_acc(t, k=last):
        d = way(t)
        return t % SLOTS, y, bit_of(0, d), pl.ds(pl.multiple_of(base(k, d) - bit_of(0, d) * half, 16), half >> (k - 1))

    tail = BLK >> last

    def extra_copy(j, t):
        s = t % SLOTS
        return copy(acc.at[own_acc(t)], recvs[last + j].at[s], 2 + last + j, s, rep_peer(extra[j]))

    across = held_ref.shape[1] // COL

    def held(t, start, rows):
        at = pl.multiple_of(t // across * BLK + start, 16)
        return held_ref.at[pl.ds(at, rows), pl.ds(pl.multiple_of(t % across * COL, COL), COL)]

    def gather_copy(k, t):
        s, d = t % SLOTS, way(t)
        ref = held(t, base(k + 1, d), half >> k)
        return copy(ref, ref, 2 + last + len(extra) + k, s, bit_peer(k, d))

    f32, bf = jnp.float32, jnp.bfloat16
    nt = (((1,), (1,)), ((), ()))

    def block(start, j, size=256):
        return pl.ds(pl.multiple_of(start + j * size, size), size)

    def tables(u):
        first, used = spans_of(lengths_ref, owner_ref, rep * lax.axis_size("shard") + shard)
        lane = lax.broadcasted_iota(jnp.int32, (128, 128), 1)
        even = lane % 2 == 0
        lane = lane % HEAD_DIM
        inverse = jnp.exp((lane // 2).astype(f32) * (-2.0 * math.log(10000.0) / ROT_DIM))
        inverse = jnp.where(lane < ROT_DIM, inverse, 0.0)
        key = lax.broadcasted_iota(jnp.int32, (128, TOK_DEV), 1)
        for g in range(TOK_DEV // 128):
            rows = slice(g * 128, (g + 1) * 128)
            query = lax.broadcasted_iota(jnp.int32, (128, TOK_DEV), 0) + g * 128
            same = (query < used) & ((query < first) == (key < first))
            bias_ref[rows, :] = jnp.where((key == query) | ((key < query) & same), 0.0, NEG)
            place = jnp.broadcast_to(pos_ref[g:g + 1, :].astype(f32), (128, 128)).T
            angles = place * inverse
            sine = jnp.sin(angles)
            cos_ref[rows, :] = jnp.cos(angles)
            sa_ref[rows, :] = jnp.where(even, -sine, 0.0)
            sb_ref[rows, :] = jnp.where(even, 0.0, sine)

    def turn_rows(u):
        for b in range(2):
            rows = jnp.dot(left[:, 0:D], qkv_full[:, block(0, 2 * u + b)], preferred_element_type=f32)
            for g in range(2):
                part = rows[:, g * 128:(g + 1) * 128]
                part = part * cos_ref[...] + pltpu.roll(part, 127, 1) * sa_ref[...] + pltpu.roll(part, 1, 1) * sb_ref[...]
                right[:, block(0, 4 * u + 2 * b + g, 128)] = part.astype(bf)

    def value_rows(u):
        for b in range(2):
            at = block(2 * D, 2 * u + b)
            right[:, at] = jnp.dot(left[:, 0:D], qkv_full[:, at], preferred_element_type=f32).astype(bf)

    def grad_attended(u):
        for b in range(2):
            part = lax.dot_general(right[:, 3 * D:4 * D], out_full[block(0, 2 * u + b), :], nt, preferred_element_type=f32)
            left[:, block(D, 2 * u + b)] = part.astype(bf)

    def attend(u):
        @pl.when(u % 2 == 0)
        def _():
            pair = u // 2
            spans = [block(k * D, pair, 128) for k in range(3)]
            span = block(D, pair, 128)

            def put_att(value):
                left[:, span] = value

            def put_grad(part, value):
                right[:, spans[part]] = value
            attend_pair(right[:, spans[0]], right[:, spans[1]], right[:, spans[2]], left[:, span],
                        bias_ref, cos_ref, sa_ref, sb_ref, put_att, put_grad)

    def grad_normed(u):
        at = block(0, u)
        gn_ref[:, at] = gn_ref[:, at] + lax.dot_general(right[:, 0:3 * D], qkv_full[at, :], nt, preferred_element_type=f32)

    def feed_forward(u):
        at = block(0, u)
        base_ref[:, at] = base_ref[:, at] + jnp.dot(left[:, 2 * D:6 * D], fc_full[:, at], preferred_element_type=f32)

    def project(u):
        for b in range(2):
            at = block(0, 2 * u + b)
            layer_ref[:, at] = (base_ref[:, at] + jnp.dot(left[:, D:2 * D], out_full[:, at], preferred_element_type=f32)).astype(bf)

    def norm_back(u):
        @pl.when(u == 0)
        def _():
            s_buf[0, :, 4 * D:] = jnp.zeros((1, 3 * D), f32)
        at = block(0, u, 64)
        x = tok_ref[at, :].astype(f32)
        center = x - jnp.mean(x, axis=-1, keepdims=True)
        scale = lax.rsqrt(jnp.mean(center * center, axis=-1, keepdims=True) + EPS)
        unit = center * scale
        grad = gn_ref[at, :]
        upstream = right[at, 3 * D:4 * D].astype(f32)
        wide = grad * norm_ref[0:1, :]
        lean = wide - jnp.mean(wide, axis=-1, keepdims=True) - unit * jnp.mean(wide * unit, axis=-1, keepdims=True)
        grad_ref[at, :] = (lean * scale + upstream).astype(bf)
        for k, value in enumerate((upstream, grad * unit, grad)):
            span = slice((4 + k) * D, (5 + k) * D)
            s_buf[0, :, span] = s_buf[0, :, span] + jnp.sum(value, axis=0, keepdims=True)

    row_copies = [pltpu.make_async_copy(src, dst, store_sem.at[4 + j])
                  for j, (src, dst) in enumerate(((layer_ref, layer_hbm), (grad_ref, grad_hbm)))]

    def send_rows(u):
        for row_copy in row_copies:
            row_copy.start()

    tasks = [(0, 1, tables), (EARLY, 4, turn_rows), (EARLY, 2, value_rows), (EARLY + 2, 2, grad_attended),
             (EARLY + 4, 16, attend), (EARLY + 20, 4, grad_normed), (EARLY + 24, 4, feed_forward), (EARLY + 28, 2, project),
             (EARLY + 28, 8, norm_back), (EARLY + 36, 1, send_rows)]

    def store(t):
        return pltpu.make_async_copy(held(t, 0, BLK), out_hbm_blocks.at[t], store_sem.at[t % 4])

    def compute(t):
        s = t % SLOTS
        first, stride, column, new = chunk_plan(t)

        @pl.when(new)
        def _():
            for o in range(4):
                at = pl.multiple_of(first + o * stride, BLK)
                turned[o % 2, (o // 2) * BLK:(o // 2 + 1) * BLK, :] = left[:, pl.ds(at, BLK)].T
        operand = right[:, pl.ds(pl.multiple_of(column, COL), COL)]
        for side, dst in ((1 - c, c_send), (c, c_keep)):
            part = jnp.dot(turned[side], operand, preferred_element_type=jnp.float32)
            dst[s] = part.astype(jnp.bfloat16).reshape(2, 2, half, COL)
        core_copy(t).start()

    def each_way(t, body):
        for d in range(2 if TURN else 1):
            @pl.when(way(t) == d)
            def _(d=d):
                body(d)

    def after_core(t):
        s = t % SLOTS
        core_copy(t).wait()

        def total(d):
            for own_half in range(2):
                if d:
                    at = (s, slice(None), bits[1] if own_half else 1 - bits[1])
                else:
                    at = (s, y if own_half else 1 - y)
                acc[at] = c_keep[at] + c_recv[at]
                if not own_half:
                    first_copy(t, d).start()
        each_way(t, total)

    def after_first(t):
        s = t % SLOTS

        def total(d):
            first_copy(t, d).wait()
            at = (s, slice(None), bits[1]) if d else (s, y)
            acc[at] = acc[at] + y_recv[s]
        each_way(t, total)
        second_copy(t).start()

    def after_rows(k, t):
        s = t % SLOTS
        (second_copy(t) if k == 0 else rows_copy(k, t)).wait()
        at = own_acc(t, k + 1)
        total = acc[at] + recvs[k][s]
        if k + 1 < last:
            acc[at] = total
            rows_copy(k + 1, t).start()
        elif extra:
            acc[at] = total
            extra_copy(0, t).start()
        else:
            held(t, base(last, way(t)), tail)[...] = total
            gather_copy(last - 1, t).start()

    def after_extra(j, t):
        s = t % SLOTS
        extra_copy(j, t).wait()
        total = acc[own_acc(t)] + recvs[last + j][s]
        if j + 1 < len(extra):
            acc[own_acc(t)] = total
            extra_copy(j + 1, t).start()
        else:
            held(t, base(last, way(t)), tail)[...] = total
            gather_copy(last - 1, t).start()

    def after_gather(k, t):
        gather_copy(k, t).wait()
        if k > 0:
            gather_copy(k - 1, t).start()
        else:
            @pl.when(t >= 4)
            def _():
                store(t - 4).wait()
            store(t).start()

    stages = [(0, compute), (LAGS[0], after_core), (LAGS[0]+LAGS[1], after_first)]
    lag = LAGS[0]+LAGS[1]
    for k in range(last):
        lag += LAGS[2+k]
        stages.append((lag, functools.partial(after_rows, k)))
    for j in range(len(extra)):
        lag += 1
        stages.append((lag, functools.partial(after_extra, j)))
    for k in reversed(range(last)):
        lag += LAGS[5+last-1-k]
        stages.append((lag, functools.partial(after_gather, k)))

    s_peers = peers

    def small_copy(j):
        return pltpu.make_async_remote_copy(
            src_ref=s_buf.at[j], dst_ref=s_recv.at[j], send_sem=s_send_sem.at[j],
            recv_sem=s_recv_sem.at[j], device_id=s_peers[j], device_id_type=MESH)

    def small_step(j):
        if j > 0:
            small_copy(j - 1).wait()
            total = s_buf[j - 1] + s_recv[j - 1]
            if j < len(s_peers):
                s_buf[j] = total
            else:
                small_out[...] = total
        if j < len(s_peers):
            small_copy(j).start()

    def step(i, carry):
        for delay, stage in reversed(stages):
            @pl.when((i >= delay) & (i < n_chunks + delay))
            def _(stage=stage, delay=delay):
                stage(i - delay)
        for start, count, task in tasks:
            @pl.when((i >= start) & (i < start + count))
            def _(start=start, task=task):
                task(i - start)
        for j in range(len(s_peers) + 1):
            @pl.when(i == 47 + j)
            def _(j=j):
                small_step(j)
        return carry

    def finish():
        for t in range(n_chunks - 4, n_chunks):
            store(t).wait()
        for row_copy in row_copies:
            row_copy.wait()
    return n_chunks + lag, step, finish


def block_kernel(shards, n_rep, n_chunks, n_recvs, small_ref, lengths_ref, owner_ref, pos_ref, tok_hbm, cot_hbm,
                 in_own, fc_own, qkv_own, out_own, blocks_hbm, small_out, layer_hbm, grad_hbm,
                 in_full, fc_full, qkv_full, out_full, left, right, turned, gn_ref, base_ref, tok_ref,
                 small_full, ff_bias, norm_ref, bias_ref, cos_ref, sa_ref, sb_ref, s_buf, s_recv,
                 layer_ref, grad_ref, c_send, c_keep, c_recv, acc, y_recv, *rest):
    recvs, sems = rest[:n_recvs], rest[n_recvs:]
    rep = lax.axis_index("rep")
    shard = lax.axis_index("shard")
    barrier = pltpu.get_barrier_semaphore()
    peers = [(rep, 4 * (shard // 4) + (shard + k) % 4) for k in range(1, 4)]
    b = 1
    while b < n_rep:
        peers.append((rep + b * (1 - 2 * ((rep // b) % 2)), shard))
        b *= 2
    for p in peers:
        pl.semaphore_signal(barrier, inc=1, device_id=p, device_id_type=MESH)
    pl.semaphore_wait(barrier, len(peers))

    begin, gather_steps, free_from, in_done, gather_step, gather_finish = front_steps(
        shards, small_ref, lengths_ref, owner_ref, tok_hbm, cot_hbm,
        (in_own, fc_own, qkv_own, out_own), (in_full, fc_full, qkv_full, out_full),
        left.at[:, 0:D], left.at[:, 2 * D:6 * D], right.at[:, 4 * D:8 * D], right.at[:, 3 * D:4 * D],
        base_ref, gn_ref, tok_ref, s_buf.at[0], norm_ref, small_full, ff_bias, *sems[:9])
    total, step, finish = reduce_steps(
        n_rep, n_chunks, lengths_ref, owner_ref, pos_ref, norm_ref, blocks_hbm, small_out, layer_hbm, grad_hbm,
        layer_ref, grad_ref, left, right, turned, fc_full, qkv_full, out_full, gn_ref, base_ref, tok_ref, in_full,
        bias_ref, cos_ref, sa_ref, sb_ref, sems[9], c_send, c_keep, c_recv, acc, y_recv, recvs, s_buf, s_recv, *sems[10:])
    begin()
    early = 0
    for i in range(gather_steps):
        gather_step(i)
        due = (i - free_from + 1) * EARLY // (gather_steps - free_from)
        while early < (due if i >= in_done else min(due, WRITES)):
            step(early, 0)
            early += 1
    gather_finish()
    lax.fori_loop(early, total, step, 0)
    finish()


def block(small, lengths, owner, positions, tokens, cotangent, in_own, fc_own, qkv_own, out_own, n_rep, shards, n_chunks):
    nbits = int(math.log2(n_rep))
    last = 3
    n_extra = nbits - last
    n_stage = 2 + last + n_extra + last
    bf, f32 = jnp.bfloat16, jnp.float32
    rows = tokens.shape[0]
    ff = in_own.shape[1]
    n = sum(GATHER_CHUNKS)
    recv_rows = [BLK >> (k + 1) for k in range(last)] + [BLK >> last] * n_extra
    chunk = (SLOTS, 2, BLK // 2, COL)
    pair = (SLOTS, 2, 2, BLK // 2, COL)
    n_small = 2 + nbits
    sums = (1, 3 * D + ff)
    hbm = pl.BlockSpec(memory_space=pl.ANY)
    vm = pl.BlockSpec(memory_space=pltpu.VMEM)
    dma = pltpu.SemaphoreType.DMA

    def full(own):
        return pltpu.VMEM((own.shape[0] * shards, own.shape[1]), bf)
    return pl.pallas_call(
        functools.partial(block_kernel, shards, n_rep, n_chunks, len(recv_rows)),
        out_shape=(jax.ShapeDtypeStruct((n_chunks, BLK, COL), bf), jax.ShapeDtypeStruct(sums, f32),
                   jax.ShapeDtypeStruct((rows, D), bf), jax.ShapeDtypeStruct((rows, D), bf)),
        in_specs=[vm] * 4 + [hbm] * 6,
        out_specs=(hbm, vm, hbm, hbm),
        scratch_shapes=[
            full(in_own), full(fc_own), full(qkv_own), full(out_own),
            pltpu.VMEM((rows, 2 * D + ff), bf), pltpu.VMEM((rows, 4 * D + ff), bf), pltpu.VMEM((2, 2 * BLK, rows), bf),
            pltpu.VMEM((rows, D), f32), pltpu.VMEM((rows, D), f32), pltpu.VMEM((rows, D), bf),
            pltpu.VMEM((shards,) + small.shape, f32), pltpu.VMEM((1, ff), f32), pltpu.VMEM((8, D), f32),
            pltpu.VMEM((rows, rows), f32), *[pltpu.VMEM((rows, 128), f32)] * 3,
            pltpu.VMEM((n_small,) + sums, f32), pltpu.VMEM((n_small,) + sums, f32),
            pltpu.VMEM((rows, D), bf), pltpu.VMEM((rows, D), bf),
            pltpu.VMEM(pair, bf), pltpu.VMEM(pair, bf), pltpu.VMEM(pair, bf), pltpu.VMEM(pair, bf), pltpu.VMEM(chunk, bf),
            *[pltpu.VMEM((SLOTS, r, COL), bf) for r in recv_rows],
            dma((3, n, 2)), dma((3, n, 2)), dma((n,)), dma((n,)), dma((4,)), dma((4,)), dma((6,)), dma((3,)), dma((3,)),
            dma((6,)), dma((n_stage, SLOTS)), dma((n_stage, SLOTS)), dma((n_small,)), dma((n_small,)),
        ],
        compiler_params=pltpu.CompilerParams(collective_id=1, has_side_effects=True, vmem_limit_bytes=67043328),
        name="block",
    )(small, lengths, owner, positions, tokens, cotangent, in_own, fc_own, qkv_own, out_own)


def chunk_plan(t):
    cases = [
        (2 * D + (t // 2) * BLK, D, 3 * D + (t % 2) * COL, t % 2),
        (((t - 16) // 8) * BLK, D // 4, 4 * D + (t % 8) * COL, t % 8),
        (((t - 32) // 6) * BLK, D // 4, ((t - 32) % 6) * COL, (t - 32) % 6),
        (D + ((t - 44) // 2) * BLK, D // 4, 3 * D + (t % 2) * COL, t % 2),
    ]
    first, stride, column, within = (
        jnp.where(t < 16, cases[0][i], jnp.where(t < 32, cases[1][i], jnp.where(t < 44, cases[2][i], cases[3][i])))
        for i in range(4))
    return first, stride, column, within == 0


def assemble(blocks, rows, places, scale):
    def kern(in_hbm, *rest):
        n = len(rows)
        row_hbm, row_out, row_ref, outs = rest[:n], rest[n:2 * n], rest[-4 - n:-4], rest[2 * n:-4 - n]
        in_ref, stage, load_sem, sem = rest[-4:]
        first_row = blocks.shape[0]
        copies = []
        row_loads = [pltpu.make_async_copy(row_hbm[j], row_ref[j], sem.at[first_row + j]) for j in range(n)]
        row_stores = [pltpu.make_async_copy(row_ref[j], row_out[j], sem.at[first_row + n + j]) for j in range(n)]
        for load_row in row_loads:
            load_row.start()
        part = 4

        def load(g):
            at = pl.ds(g * part, part)
            return pltpu.make_async_copy(in_hbm.at[at], in_ref.at[at], load_sem.at[g])
        for g in range(blocks.shape[0] // part):
            load(g).start()
        for load_row, store_row in zip(row_loads, row_stores):
            load_row.wait()
            store_row.start()
            copies.append(store_row)
        for (first, height, cols), out in zip(places, outs):
            across = cols // COL
            for i in range(height // BLK):
                for j in range(across):
                    t = first + i * across + j
                    if t % part == 0:
                        load(t // part).wait()
                    stage[t] = in_ref[t].astype(jnp.float32) * scale
                    copies.append(pltpu.make_async_copy(
                        stage.at[t], out.at[i * BLK:(i + 1) * BLK, j * COL:(j + 1) * COL], sem.at[t]))
                    copies[-1].start()
        for copy in copies:
            copy.wait()

    return pl.pallas_call(
        kern,
        out_shape=[jax.ShapeDtypeStruct(x.shape, x.dtype) for x in rows]
        + [jax.ShapeDtypeStruct((height, cols), jnp.float32) for _, height, cols in places],
        in_specs=[pl.BlockSpec(memory_space=pl.ANY)] * (1 + len(rows)),
        out_specs=[pl.BlockSpec(memory_space=pl.ANY)] * (len(rows) + len(places)),
        scratch_shapes=[*[pltpu.VMEM(x.shape, x.dtype) for x in rows], pltpu.VMEM(blocks.shape, blocks.dtype), pltpu.VMEM(blocks.shape, jnp.float32),
                        pltpu.SemaphoreType.DMA((blocks.shape[0] // 4,)), pltpu.SemaphoreType.DMA((blocks.shape[0] + 2 * len(rows),))],
        compiler_params=pltpu.CompilerParams(vmem_limit_bytes=63 * 2**20),
        name="assemble",
    )(blocks, *rows)


def body(
    tokens,
    positions,
    lengths,
    owner,
    qkv_weight,
    out_weight,
    in_weight,
    in_bias,
    fc_weight,
    fc_bias,
    norm_gain,
    norm_bias,
    cotangent,
):
    rep_count = lax.axis_size("rep")
    shard_count = lax.axis_size("shard")
    shard = lax.axis_index("shard")
    grad_scale = 1.0 / math.sqrt(TOK_DEV * rep_count * shard_count)
    lengths, owner = lengths.reshape(1, -1), owner.reshape(1, -1)
    small = sum(jnp.pad(part.astype(jnp.float32), (first, 2048 - first - part.shape[0])) for first, part in (
        (0, in_bias), (1024, fc_bias), (1280, norm_gain), (1536, norm_bias))).reshape(16, 128)
    blocks, small_sum, layer_out, input_grad = block(
        small, lengths, owner, positions.reshape(-1, 128), tokens, cotangent, in_weight, fc_weight, qkv_weight, out_weight,
        rep_count, shard_count, 48)
    small_sum = small_sum.reshape(-1) * grad_scale

    def own_part(first, size):
        return lax.dynamic_slice_in_dim(small_sum, first + shard * (size // 4), size // 4)

    layer_out, input_grad, grad_in, grad_fc, grad_qkv, grad_out = assemble(
        blocks, (layer_out, input_grad), ((16, 256, 4 * D), (0, 1024, D), (32, 256, 3 * D), (44, 256, D)), grad_scale)
    return (
        layer_out,
        input_grad,
        grad_qkv,
        grad_out,
        grad_in,
        own_part(0, 4096),
        grad_fc,
        own_part(4096, D),
        own_part(4096 + D, D),
        own_part(4096 + 2 * D, D),
    )


def solution(mesh):
    in_specs = (
        P(("rep", "shard"), None),
        P(("rep", "shard")),
        P(),
        P(),
        P("shard", None),
        P("shard", None),
        P("shard", None),
        P("shard"),
        P("shard", None),
        P("shard"),
        P("shard"),
        P("shard"),
        P(("rep", "shard"), None),
    )
    out_specs = (
        P(("rep", "shard"), None),
        P(("rep", "shard"), None),
        P("shard", None),
        P("shard", None),
        P("shard", None),
        P("shard"),
        P("shard", None),
        P("shard"),
        P("shard"),
        P("shard"),
    )
    return jax.shard_map(body, mesh=mesh, in_specs=in_specs, out_specs=out_specs, check_vma=False)
```
